32 devices in a mesh: dp: 4 (over y, x), expert: 8 (over z, core).
Axes of the slice: x: 2, y: 2, z: 4, core: 2. Of those that a mesh axis runs over, the one named last changes fastest.
Arguments:
- tokens: bfloat16 [4096, 2048], P(('dp', 'expert')), may hold values from -6 to 6
- cotangent: bfloat16 [4096, 2048], P(('dp', 'expert')), may hold values from -6 to 6
- prefix: int32 [4], P('dp'), may hold values from 128 to 511
- routes: int32 [4096, 6], P(('dp', 'expert')), may hold values from 0 to 15, all different within a row; in each aligned block of 128 rows (0 to 127, 128 to 255, ...) at most 72 rows name the same one
- norm1_gain: bfloat16 [2048], P('expert'), may hold values from 0.25 to 1.75
- w_query: bfloat16 [2048, 3072], P('expert'), may hold values from -0.1875 to 0.1875
- w_kv_down: bfloat16 [2048, 576], P('expert'), may hold values from -0.125 to 0.125
- kv_gain: bfloat16 [512], P('expert'), may hold values from 0.25 to 1.75
- w_kv_up: bfloat16 [512, 4096], P('expert'), may hold values from -0.25 to 0.25
- w_out: bfloat16 [2048, 2048], P('expert'), may hold values from -1 to 1
- norm2_gain: bfloat16 [2048], P('expert'), may hold values from 0.25 to 1.75
- w_router: bfloat16 [2048, 16], P('expert'), may hold values from -0.0625 to 0.0625
- shared_in: bfloat16 [2048, 5632], P('expert'), may hold values from -0.125 to 0.125
- shared_out: bfloat16 [2816, 2048], P('expert'), may hold values from -0.109375 to 0.109375
- expert_in: bfloat16 [16, 2048, 2816], P('expert', 'dp'), may hold values from -0.125 to 0.125
- expert_out: bfloat16 [16, 1408, 2048], P('expert', None, 'dp'), may hold values from -6 to 6
Outputs:
- out: bfloat16 [4096, 2048], P(('dp', 'expert'))
- grad_tokens: float32 [4096, 2048], P(('dp', 'expert'))
- grad_norm1_gain: float32 [2048], P('expert')
- grad_w_query: float32 [2048, 3072], P('expert')
- grad_w_kv_down: float32 [2048, 576], P('expert')
- grad_kv_gain: float32 [512], P('expert')
- grad_w_kv_up: float32 [512, 4096], P('expert')
- grad_w_out: float32 [2048, 2048], P('expert')
- grad_norm2_gain: float32 [2048], P('expert')
- grad_w_router: float32 [2048, 16], P('expert')
- grad_shared_in: float32 [2048, 5632], P('expert')
- grad_shared_out: float32 [2816, 2048], P('expert')
- grad_expert_in: float32 [16, 2048, 2816], P('expert', 'dp')
- grad_expert_out: float32 [16, 1408, 2048], P('expert', None, 'dp')
The draws below stay inside these ranges and needn't reach their ends.
Inputs may be any that keep to these rules, and one draw needn't show every extreme that they name: `routes`: each row names 6 different experts. Among the rows of one device no expert is named by more than 72 rows, a bound that some block reaches of them.
All inputs are finite; a program needn't handle non-finite values.
Results may differ from the reference program's by a relative error of at most 0.029.
Values may be sent and summed in bfloat16 or wider, within the bound.
No kernel may reach another device: no remote copies, remote signals or barrier semaphores. Data moves between devices by JAX's collectives and lax.ppermute only.
A program may use at most 448 MiB of HBM per device.

```python
import math
import jax
import jax.numpy as jnp
import numpy as np
from jax import lax

D = 2048
H = 16
DN = 128
DR = 64
DV = 128
KVR = 512
FFE = 1408
FFS = 2816
TOPK = 6
TOK_DEV = 128
EXPERTS = 16
SEQ = 1024
SEQS = 4
TOKENS = 4096
CAP = 72
N_EXPERT = 8


def place_ends(values, key, low, largest):
    longest = values.shape.index(max(values.shape))
    spots = []
    for shift in (0, 1):
        where = [jax.random.randint(jax.random.fold_in(key, axis), (), 0, length) for axis, length in enumerate(values.shape)]
        where[longest] = (where[longest] + shift) % values.shape[longest]
        spots.append(tuple(where))
    return values.at[spots[0]].set(low).at[spots[1]].set(largest)


def block_scale(rng, extent, pieces, smallest, high):
    gain = 1.0
    for position, blocks in pieces:
        heights = jax.random.uniform(jax.random.fold_in(jax.random.fold_in(rng, 6), position), (blocks,), jnp.float32, smallest / len(pieces), high / len(pieces))
        gain = gain * jnp.repeat(jnp.exp(heights), extent[position] // blocks).reshape((-1,) + (1,) * (len(extent) - 1 - position))
    return gain


def deal_out(key, own, number, rows, count, top, most, skew):
    ranking = jax.random.permutation(key, count)
    crowded, common = shares(count, rows * top, most, skew, True), shares(count, rows * top, most, skew, False)
    places = jnp.arange(count)

    def named(sizes, offset_by):
        used = int((sizes > 0).sum())
        fixed = max(1, used // 4)
        shifted = fixed + (places - fixed + offset_by * (used - fixed)) % max(1, count - fixed)
        return jnp.zeros((count,), jnp.int32).at[ranking[jnp.where(places < fixed, places, shifted)]].set(jnp.asarray(sizes, jnp.int32))

    sizes = jnp.where(number % 4 == 0, named(crowded, number // 4), named(common, number - number // 4 - 1))
    mixed = jax.random.permutation(jax.random.fold_in(own, 3), count)
    giver, sink = mixed[0:count // 2 * 2:2], mixed[1:count // 2 * 2:2]
    room = jnp.minimum(sizes[giver] - 1, most - sizes[sink]) // 2
    room = jnp.where((giver == ranking[0]) | (sink == ranking[0]) | (sizes[sink] == 0), 0, jnp.maximum(room, 0))
    shifted = jax.random.randint(jax.random.fold_in(own, 4), (count // 2,), 0, 1 << 20) % (room + 1)
    sizes = sizes.at[giver].add(-shifted).at[sink].add(shifted)
    members = jnp.searchsorted(jnp.cumsum(sizes), jnp.arange(rows * top), side="right").astype(jnp.int32)
    listing = members.reshape(top, rows).T
    listing = listing[jax.random.permutation(jax.random.fold_in(own, 1), rows)]
    offset_by = jax.random.randint(jax.random.fold_in(own, 2), (rows, 1), 0, top)
    return jnp.take_along_axis(listing, (jnp.arange(top)[None, :] + offset_by) % top, axis=1)


def shares(amount, total, bound, slope, full):
    loads = [(1 << 20) // math.isqrt(rank ** slope) + 1 for rank in range(1, amount + 1)]
    largest = bound if full else min(bound, max(-(-total // amount), total * loads[0] // sum(loads)))
    least = 1 if total - largest >= amount - 1 else 0
    given, rest = [largest] + [least] * (amount - 1), total - largest - least * (amount - 1)
    while rest > 0:
        candidates = [i for i in range(1, amount) if given[i] < largest] or [i for i in range(1, amount) if given[i] < bound]
        whole, remaining = sum([loads[i] for i in candidates]), rest
        for i in candidates:
            addition = min(bound - given[i], max(1, remaining * loads[i] // whole), rest)
            given[i] = given[i] + addition
            rest = rest - addition
    return np.array(given)


def noise(stream_key, extent, scale, bound, split=(), kind=jnp.bfloat16):
    values = scale * jax.random.normal(stream_key, extent, jnp.float32)
    if split:
        values = values * block_scale(stream_key, extent, split, -0.22, 0.18)
    return jnp.clip(values, -bound, bound).astype(kind)


def setup_inputs(seed: int = 0) -> dict:
    arg_keys = jax.random.split(jax.random.key(seed), 17)
    tokens = noise(arg_keys[0], (TOKENS, D), 1.0, 6.0, ((0, 32),))
    cotangent = noise(arg_keys[1], (TOKENS, D), 1.0, 6.0, ((0, 32),))
    prefix = place_ends(jax.random.randint(arg_keys[2], (SEQS,), SEQ // 8, SEQ // 2), jax.random.fold_in(arg_keys[2], 1), SEQ // 8, (SEQ // 2) - 1).astype(jnp.int32)
    routes_keys = jax.random.split(jax.random.fold_in(arg_keys[3], 1), TOKENS // TOK_DEV)
    routes_turns = jax.random.permutation(jax.random.fold_in(arg_keys[3], 3), TOKENS // TOK_DEV)
    routes = jax.vmap(lambda own, number: deal_out(jax.random.fold_in(arg_keys[3], 2), own, number, TOK_DEV, EXPERTS, TOPK, CAP, 2))(routes_keys, routes_turns).reshape((TOKENS, TOPK))
    norm1_gain = jnp.clip(1.0 + 0.15 * jax.random.normal(arg_keys[4], (D,), jnp.float32), 0.25, 1.75).astype(jnp.bfloat16)
    w_query = noise(arg_keys[5], (D, H * (DN + DR)), (D // 2) ** -0.5, 0.1875, ((0, 8),))
    w_kv_down = noise(arg_keys[6], (D, KVR + DR), D ** -0.5, 0.125, ((0, 8),))
    kv_gain = jnp.clip(1.0 + 0.15 * jax.random.normal(arg_keys[7], (KVR,), jnp.float32), 0.25, 1.75).astype(jnp.bfloat16)
    w_kv_up = noise(arg_keys[8], (KVR, H * (DN + DV)), KVR ** -0.5, 0.25, ((0, 8),))
    w_out = noise(arg_keys[9], (H * DV, D), (H * DV // 64) ** -0.5, 1.0, ((0, 8),))
    norm2_gain = jnp.clip(1.0 + 0.15 * jax.random.normal(arg_keys[10], (D,), jnp.float32), 0.25, 1.75).astype(jnp.bfloat16)
    w_router = noise(arg_keys[11], (D, EXPERTS), (4 * D) ** -0.5, 0.0625, ((0, 8),))
    shared_in = noise(arg_keys[12], (D, 2 * FFS), D ** -0.5, 0.125, ((0, 8),))
    shared_out = noise(arg_keys[13], (FFS, D), FFS ** -0.5, 0.109375, ((0, 8),))
    expert_in = noise(arg_keys[14], (EXPERTS, D, 2 * FFE), D ** -0.5, 0.125, ((0, 8), (1, 4)))
    expert_out = noise(arg_keys[15], (EXPERTS, FFE, D), (max(FFE // 1024, 1)) ** -0.5, 6.0, ((0, 8), (2, 4)))
    return dict(tokens=tokens, cotangent=cotangent, prefix=prefix, routes=routes, norm1_gain=norm1_gain, w_query=w_query, w_kv_down=w_kv_down, kv_gain=kv_gain, w_kv_up=w_kv_up, w_out=w_out, norm2_gain=norm2_gain, w_router=w_router, shared_in=shared_in, shared_out=shared_out, expert_in=expert_in, expert_out=expert_out)


EPSILON = 1e-06
MASKED = -1e+30
HIGHEST = lax.Precision.HIGHEST

@jax.custom_vjp
def low(v):
    return lax.optimization_barrier(v.astype(jnp.bfloat16)).astype(jnp.float32)

@jax.custom_vjp
def low_back(v):
    return v

def low_keep(v):
    return (low(v), None)

def low_pass(kept, grad):
    return (grad,)

def back_keep(v):
    return (v, None)

def back_low(kept, grad):
    return (low(grad),)
low.defvjp(low_keep, low_pass)
low_back.defvjp(back_keep, back_low)

def matmul_high(left_side, right_side):
    return jnp.dot(left_side, right_side, precision=HIGHEST, preferred_element_type=jnp.float32)

def rms_norm(values, gain_vector):
    return values * lax.rsqrt(lax.optimization_barrier(jnp.mean(values * values, axis=-1, keepdims=True)) + EPSILON) * gain_vector

def tables(positions, half_width):
    frequency = 10000.0 ** (-jnp.arange(half_width, dtype=jnp.float32) / half_width)
    angles = positions.astype(jnp.float32)[:, None] * frequency[None, :]
    return (jnp.cos(angles), jnp.sin(angles))

def rotate(values, cosine, sine_table):
    half_width = values.shape[-1] // 2
    front_part = values[..., :half_width]
    back_part = values[..., half_width:]
    return jnp.concatenate([front_part * cosine - back_part * sine_table, back_part * cosine + front_part * sine_table], axis=-1)

def swiglu(joined):
    half_width = joined.shape[-1] // 2
    return jax.nn.silu(joined[..., :half_width]) * joined[..., half_width:]

def attention(query, key_nope, key_rope, value, prefix_end):
    length = query.shape[0]
    span = 4 * TOK_DEV
    score_scale = float(DN + DR) ** (-0.5)
    key_pos = jnp.arange(length, dtype=jnp.int32)

    def query_block(index):
        part = lax.dynamic_slice_in_dim(query, index * span, span, 0)
        front_part = jnp.einsum('qhd,khd->hqk', part[..., :DN], key_nope, precision=HIGHEST)
        back_part = jnp.einsum('qhd,kd->hqk', part[..., DN:], key_rope, precision=HIGHEST)
        scores = low_back((front_part + back_part) * score_scale)
        query_pos = index * span + jnp.arange(span, dtype=jnp.int32)
        seen = (key_pos[None, :] <= query_pos[:, None]) | (key_pos[None, :] < prefix_end)
        probs = low(jax.nn.softmax(jnp.where(seen[None], scores, MASKED), axis=-1))
        return jnp.einsum('hqk,khd->qhd', probs, value, precision=HIGHEST).reshape(span, H * DV)
    blocks = lax.map(jax.checkpoint(query_block), jnp.arange(length // span, dtype=jnp.int32))
    return blocks.reshape(length, H * DV)

def expert_mix(normed_two, paths, route_gates, expert_in_w, expert_out_w):
    length = normed_two.shape[0]
    pair_count = length * TOPK
    expert_ids = paths.reshape(-1)
    flat_gates = route_gates.reshape(-1)

    def expert_step(totals, block_item):
        index, first_w, second_w = block_item
        chosen = jnp.nonzero(expert_ids == index, size=N_EXPERT * CAP, fill_value=pair_count)[0].astype(jnp.int32)
        valid = (chosen < pair_count).astype(jnp.float32)
        safe_pair = jnp.minimum(chosen, pair_count - 1)
        token_index = safe_pair // TOPK
        chosen_rows = normed_two[token_index] * valid[:, None]
        joined = low_back(matmul_high(chosen_rows, first_w))
        hidden = low(swiglu(joined))
        result = low_back(low(matmul_high(hidden, second_w)))
        weighted = result * (flat_gates[safe_pair] * valid)[:, None]
        return (totals.at[token_index].add(weighted), None)
    start_total = jnp.zeros((length, D), jnp.float32)
    totals, _ = lax.scan(jax.checkpoint(expert_step), start_total, (jnp.arange(EXPERTS, dtype=jnp.int32), expert_in_w, expert_out_w))
    return totals

def forward_layer(values, params, paths, prefix_end):
    gain_one, query_w, kv_down_w, kv_gain_w, kv_up_w, out_w, gain_two, router_w, shared_in_w, shared_out_w, expert_in_w, expert_out_w = params
    length = values.shape[0]
    cosine, sine_table = tables(jnp.arange(length, dtype=jnp.int32), DR // 2)
    normed = low(rms_norm(values, gain_one))
    query_raw = low_back(matmul_high(normed, query_w)).reshape(length, H, DN + DR)
    query = low(jnp.concatenate([query_raw[..., :DN], rotate(query_raw[..., DN:], cosine[:, None, :], sine_table[:, None, :])], axis=-1))
    kv_down = low_back(matmul_high(normed, kv_down_w))
    latent = low(rms_norm(kv_down[:, :KVR], kv_gain_w))
    key_rope = low(rotate(kv_down[:, KVR:], cosine, sine_table))
    kv_up = low(low_back(matmul_high(latent, kv_up_w))).reshape(length, H, DN + DV)
    mixed = low(low_back(attention(query, kv_up[..., :DN], key_rope, kv_up[..., DN:], prefix_end)))
    middle = values + low_back(matmul_high(mixed, out_w))
    normed_two = low(rms_norm(middle, gain_two))
    router_probs = jax.nn.softmax(low_back(matmul_high(normed_two, router_w)), axis=-1)
    one_hot = paths[:, :, None] == jnp.arange(EXPERTS, dtype=jnp.int32)[None, None, :]
    route_gates = lax.optimization_barrier(jnp.sum(jnp.where(one_hot, router_probs[:, None, :], 0.0), axis=-1))
    shared_hidden = low(swiglu(low_back(matmul_high(normed_two, shared_in_w))))
    shared = low_back(matmul_high(shared_hidden, shared_out_w))
    routed = expert_mix(normed_two, paths, route_gates, expert_in_w, expert_out_w)
    return middle + shared + routed

def reference(tokens, cotangent, prefix, routes, norm1_gain, w_query, w_kv_down, kv_gain, w_kv_up, w_out, norm2_gain, w_router, shared_in, shared_out, expert_in, expert_out):
    params = tuple((weight.astype(jnp.float32) for weight in (norm1_gain, w_query, w_kv_down, kv_gain, w_kv_up, w_out, norm2_gain, w_router, shared_in, shared_out, expert_in, expert_out)))
    inputs = tokens.astype(jnp.float32).reshape(SEQS, SEQ, D)
    upstream = cotangent.astype(jnp.float32).reshape(SEQS, SEQ, D)
    paths_all = routes.reshape(SEQS, SEQ, TOPK)

    def sequence_step(totals, block_item):
        values, upstream_one, paths, prefix_end = block_item
        result, pull_back = jax.vjp(lambda inner_values, inner_params: forward_layer(inner_values, inner_params, paths, prefix_end), values, params)
        grad_values, grad_params = pull_back(upstream_one)
        summed = tuple((first_term + second_term for first_term, second_term in zip(totals, grad_params)))
        return (summed, (result.astype(jnp.bfloat16), grad_values))
    start_totals = tuple((jnp.zeros(weight.shape, jnp.float32) for weight in params))
    totals, (results, grad_inputs) = lax.scan(sequence_step, start_totals, (inputs, upstream, paths_all, prefix))
    return (results.reshape(TOKENS, D), grad_inputs.reshape(TOKENS, D), totals[0], totals[1], totals[2], totals[3], totals[4], totals[5], totals[6], totals[7], totals[8], totals[9], totals[10], totals[11])
```

```python
import functools

import jax
import jax.numpy as jnp
from jax import lax
from jax.experimental import pallas as pl
from jax.experimental.pallas import tpu as pltpu
from jax.sharding import Mesh
from jax.sharding import PartitionSpec as P

D = 2048
H = 16
DN = 128
DR = 64
DV = 128
KVR = 512


EPSILON = 1e-06
MASKED = -1e30


def rms_norm(values, gain_vector):
    return (
        values
        * lax.rsqrt(jnp.mean(values * values, axis=-1, keepdims=True) + EPSILON)
        * gain_vector
    )


def tables(positions, half_width):
    frequency = 10000.0 ** (-jnp.arange(half_width, dtype=jnp.float32) / half_width)
    angles = positions.astype(jnp.float32)[:, None] * frequency[None, :]
    return (jnp.cos(angles), jnp.sin(angles))


def rotate(values, cosine, sine_table):
    half_width = values.shape[-1] // 2
    front_part = values[..., :half_width]
    back_part = values[..., half_width:]
    return jnp.concatenate(
        [
            front_part * cosine - back_part * sine_table,
            back_part * cosine + front_part * sine_table,
        ],
        axis=-1,
    )


def swiglu(joined):
    half_width = joined.shape[-1] // 2
    return jax.nn.silu(joined[..., :half_width]) * joined[..., half_width:]


def matmul(left_side, right_side):
    return jnp.dot(left_side, right_side, preferred_element_type=jnp.float32)


def matmul_tn(left_side, right_side):
    return lax.dot_general(
        left_side, right_side, (((0,), (0,)), ((), ())), preferred_element_type=jnp.float32
    )


def matmul_nt(left_side, right_side):
    return lax.dot_general(
        left_side, right_side, (((1,), (1,)), ((), ())), preferred_element_type=jnp.float32
    )


def masked_scores(
    query_nope, query_rope, key_nope, key_rope, key_start, query_pos, prefix_end, score_scale
):
    front_part = jnp.einsum(
        "qhd,khd->hqk", query_nope, key_nope, preferred_element_type=jnp.float32
    )
    back_part = jnp.einsum("qhd,kd->hqk", query_rope, key_rope, preferred_element_type=jnp.float32)
    raw_scores = (front_part + back_part) * score_scale
    key_pos = key_start + jnp.arange(key_nope.shape[0], dtype=jnp.int32)
    seen = (key_pos[None, :] <= query_pos[:, None]) | (key_pos[None, :] < prefix_end)
    return jnp.where(seen[None], raw_scores, MASKED)


def needed_block(key_start, query_pos, prefix_end):
    return (key_start <= query_pos[-1]) | (key_start < prefix_end)


def attend_stats(query_nope, query_rope, key_blocks, query_pos, prefix_end, score_scale):
    row_count = query_nope.shape[0]
    nope_blocks, value_blocks, rope_blocks, block_starts = key_blocks

    def block_step(running, block_item):
        key_nope, key_rope, key_start = block_item

        def compute_block(current):
            running_top, running_sum = current
            block_scores = masked_scores(
                query_nope,
                query_rope,
                key_nope,
                key_rope,
                key_start,
                query_pos,
                prefix_end,
                score_scale,
            )
            new_top = jnp.maximum(running_top, jnp.max(block_scores, axis=-1))
            new_sum = running_sum * jnp.exp(running_top - new_top) + jnp.sum(
                jnp.exp(block_scores - new_top[..., None]), axis=-1
            )
            return (new_top, new_sum)

        def skip_block(current):
            return current

        return (
            lax.cond(
                needed_block(key_start, query_pos, prefix_end), compute_block, skip_block, running
            ),
            None,
        )

    initial = (
        jnp.full((H, row_count), MASKED, jnp.float32),
        jnp.zeros((H, row_count), jnp.float32),
    )
    (final_top, final_sum), _ = lax.scan(
        block_step, initial, (nope_blocks, rope_blocks, block_starts)
    )
    return final_top + jnp.log(final_sum)


def attend_values(
    query_nope, query_rope, key_blocks, query_pos, prefix_end, score_scale, log_total
):
    row_count = query_nope.shape[0]

    def block_step(running, block_item):
        key_nope, key_value, key_rope, key_start = block_item

        def compute_block(current):
            block_scores = masked_scores(
                query_nope,
                query_rope,
                key_nope,
                key_rope,
                key_start,
                query_pos,
                prefix_end,
                score_scale,
            )
            weights = jnp.exp(block_scores - log_total[..., None]).astype(jnp.bfloat16)
            return current + jnp.einsum(
                "hqk,khd->qhd", weights, key_value, preferred_element_type=jnp.float32
            )

        def skip_block(current):
            return current

        return (
            lax.cond(
                needed_block(key_start, query_pos, prefix_end), compute_block, skip_block, running
            ),
            None,
        )

    initial = jnp.zeros((row_count, H, DV), jnp.float32)
    result, _ = lax.scan(block_step, initial, key_blocks)
    return result


def attend_grads(
    query_nope,
    query_rope,
    key_blocks,
    query_pos,
    prefix_end,
    score_scale,
    log_total,
    grad_out,
    row_delta,
):
    row_count = query_nope.shape[0]
    key_span = key_blocks[0].shape[1]

    def block_step(running, block_item):
        key_nope, key_value, key_rope, key_start = block_item

        def compute_block(current):
            grad_nope, grad_rope = current
            block_scores = masked_scores(
                query_nope,
                query_rope,
                key_nope,
                key_rope,
                key_start,
                query_pos,
                prefix_end,
                score_scale,
            )
            attn_probs = jnp.exp(block_scores - log_total[..., None])
            prob_grad = jnp.einsum(
                "qhd,khd->hqk", grad_out, key_value, preferred_element_type=jnp.float32
            )
            dscore = (attn_probs * (prob_grad - row_delta[..., None])).astype(jnp.bfloat16)
            grad_nope = grad_nope + score_scale * jnp.einsum(
                "hqk,khd->qhd", dscore, key_nope, preferred_element_type=jnp.float32
            )
            grad_rope = grad_rope + score_scale * jnp.einsum(
                "hqk,kd->qhd", dscore, key_rope, preferred_element_type=jnp.float32
            )
            key_grad = score_scale * jnp.einsum(
                "hqk,qhd->khd", dscore, query_nope, preferred_element_type=jnp.float32
            )
            rope_grad = score_scale * jnp.einsum(
                "hqk,qhd->kd", dscore, query_rope, preferred_element_type=jnp.float32
            )
            value_grad = jnp.einsum(
                "hqk,qhd->khd",
                attn_probs.astype(jnp.bfloat16),
                grad_out,
                preferred_element_type=jnp.float32,
            )
            return ((grad_nope, grad_rope), (key_grad, value_grad, rope_grad))

        def skip_block(current):
            empty_terms = (
                jnp.zeros((key_span, H, DN), jnp.float32),
                jnp.zeros((key_span, H, DV), jnp.float32),
                jnp.zeros((key_span, DR), jnp.float32),
            )
            return (current, empty_terms)

        return lax.cond(
            needed_block(key_start, query_pos, prefix_end), compute_block, skip_block, running
        )

    initial = (
        jnp.zeros((row_count, H, DN), jnp.float32),
        jnp.zeros((row_count, H, DR), jnp.float32),
    )
    return lax.scan(block_step, initial, key_blocks)


def split_blocks(key_parts, key_span):
    nope_all, value_all, rope_all = key_parts
    block_count = nope_all.shape[0] // key_span
    block_starts = jnp.arange(block_count, dtype=jnp.int32) * key_span
    return (
        nope_all.reshape(block_count, key_span, H, DN),
        value_all.reshape(block_count, key_span, H, DV),
        rope_all.reshape(block_count, key_span, DR),
        block_starts,
    )


def body(
    tokens,
    cotangent,
    prefix,
    routes,
    norm1_gain,
    w_query,
    w_kv_down,
    kv_gain,
    w_kv_up,
    w_out,
    norm2_gain,
    w_router,
    shared_in,
    shared_out,
    expert_in,
    expert_out,
):
    row_count = tokens.shape[0]
    topk_count = routes.shape[1]
    groups = lax.axis_size("expert")
    owned = expert_in.shape[0]
    expert_count = owned * groups
    capacity = 3 * row_count * topk_count // (2 * expert_count)
    score_scale = float(DN + DR) ** (-0.5)
    my_index = lax.axis_index("expert")
    query_pos = my_index * row_count + jnp.arange(row_count, dtype=jnp.int32)
    prefix_end = prefix[0]
    cosine, sine_table = tables(query_pos, DR // 2)
    key_span = 4 * row_count
    mixer_parts = (
        lax.all_gather(norm1_gain, "expert", axis=0, tiled=True),
        lax.all_gather(w_query, "expert", axis=0, tiled=True),
        lax.all_gather(w_kv_down, "expert", axis=0, tiled=True),
        lax.all_gather(kv_gain, "expert", axis=0, tiled=True),
        lax.all_gather(w_kv_up, "expert", axis=0, tiled=True),
        lax.all_gather(w_out, "expert", axis=0, tiled=True),
        lax.all_gather(norm2_gain, "expert", axis=0, tiled=True),
        lax.all_gather(w_router, "expert", axis=0, tiled=True),
        lax.all_gather(shared_in, "expert", axis=0, tiled=True),
        lax.all_gather(shared_out, "expert", axis=0, tiled=True),
    )
    (
        gain_one,
        query_w,
        kv_down_w,
        kv_gain_w,
        kv_up_w,
        out_w,
        gain_two,
        router_w,
        shared_in_w,
        shared_out_w,
    ) = mixer_parts
    values = tokens.astype(jnp.float32)
    normed = rms_norm(values, gain_one.astype(jnp.float32))
    normed_b = normed.astype(jnp.bfloat16)
    query_raw = matmul(normed_b, query_w).reshape(row_count, H, DN + DR)
    query_nope = query_raw[..., :DN].astype(jnp.bfloat16)
    query_rope = rotate(query_raw[..., DN:], cosine[:, None, :], sine_table[:, None, :]).astype(
        jnp.bfloat16
    )
    kv_down = matmul(normed_b, kv_down_w)
    latent = kv_down[:, :KVR]
    latent_b = rms_norm(latent, kv_gain_w.astype(jnp.float32)).astype(jnp.bfloat16)
    key_rope_b = rotate(kv_down[:, KVR:], cosine, sine_table).astype(jnp.bfloat16)
    kv_up = matmul(latent_b, kv_up_w).astype(jnp.bfloat16).reshape(row_count, H, DN + DV)
    local_nope = kv_up[..., :DN].reshape(row_count, H * DN)
    local_value = kv_up[..., DN:].reshape(row_count, H * DV)
    key_parts = (
        lax.all_gather(local_nope, "expert", axis=0, tiled=True),
        lax.all_gather(local_value, "expert", axis=0, tiled=True),
        lax.all_gather(key_rope_b, "expert", axis=0, tiled=True),
    )
    key_blocks = split_blocks(key_parts, key_span)
    log_total = attend_stats(query_nope, query_rope, key_blocks, query_pos, prefix_end, score_scale)
    attn_full = attend_values(
        query_nope, query_rope, key_blocks, query_pos, prefix_end, score_scale, log_total
    )
    mixed_b = attn_full.astype(jnp.bfloat16).reshape(row_count, H * DV)
    middle = values + matmul(mixed_b, out_w)
    gain_two_f = gain_two.astype(jnp.float32)
    normed_two_b = rms_norm(middle, gain_two_f).astype(jnp.bfloat16)
    router_probs = jax.nn.softmax(matmul(normed_two_b, router_w), axis=-1)
    one_hot = routes[:, :, None] == jnp.arange(expert_count, dtype=jnp.int32)[None, None, :]
    route_gates = jnp.sum(jnp.where(one_hot, router_probs[:, None, :], 0.0), axis=-1)
    shared_join = matmul(normed_two_b, shared_in_w)
    shared_hidden_b = swiglu(shared_join).astype(jnp.bfloat16)
    shared = matmul(shared_hidden_b, shared_out_w)
    expert_ids = routes.reshape(-1)
    id_hot = (expert_ids[:, None] == jnp.arange(expert_count, dtype=jnp.int32)[None, :]).astype(
        jnp.int32
    )
    slot_index = jnp.sum((jnp.cumsum(id_hot, axis=0) - id_hot) * id_hot, axis=1)
    slot_place = (expert_ids % owned * groups + expert_ids // owned) * capacity + slot_index
    buffer_rows = owned * groups * capacity
    filled = (
        jnp.zeros((buffer_rows, D), jnp.bfloat16)
        .at[slot_place]
        .set(jnp.repeat(normed_two_b, topk_count, axis=0))
    )
    received = lax.all_to_all(
        filled.reshape(owned, groups, capacity, D),
        "expert",
        split_axis=1,
        concat_axis=1,
        tiled=True,
    )
    expert_rows = received.reshape(owned, groups * capacity, D)
    expert_parts = (
        lax.all_gather(expert_in, "dp", axis=1, tiled=True),
        lax.all_gather(expert_out, "dp", axis=2, tiled=True),
    )
    first_w, second_w = expert_parts
    joined = jnp.einsum("erd,edf->erf", expert_rows, first_w, preferred_element_type=jnp.float32)
    hidden_b = swiglu(joined).astype(jnp.bfloat16)
    result_b = jnp.einsum(
        "erf,efd->erd", hidden_b, second_w, preferred_element_type=jnp.float32
    ).astype(jnp.bfloat16)
    returned = lax.all_to_all(
        result_b.reshape(owned, groups, capacity, D),
        "expert",
        split_axis=1,
        concat_axis=1,
        tiled=True,
    )
    picked = (
        returned.reshape(buffer_rows, D)[slot_place]
        .reshape(row_count, topk_count, D)
        .astype(jnp.float32)
    )
    routed = jnp.sum(route_gates[:, :, None] * picked, axis=1)
    out = (middle + shared + routed).astype(jnp.bfloat16)
    back_parts = (
        lax.all_gather(norm1_gain, "expert", axis=0, tiled=True),
        lax.all_gather(w_query, "expert", axis=0, tiled=True),
        lax.all_gather(w_kv_down, "expert", axis=0, tiled=True),
        lax.all_gather(kv_gain, "expert", axis=0, tiled=True),
        lax.all_gather(w_kv_up, "expert", axis=0, tiled=True),
        lax.all_gather(w_out, "expert", axis=0, tiled=True),
        lax.all_gather(norm2_gain, "expert", axis=0, tiled=True),
        lax.all_gather(w_router, "expert", axis=0, tiled=True),
        lax.all_gather(shared_in, "expert", axis=0, tiled=True),
        lax.all_gather(shared_out, "expert", axis=0, tiled=True),
    )
    back_keys = (
        lax.all_gather(local_nope, "expert", axis=0, tiled=True),
        lax.all_gather(local_value, "expert", axis=0, tiled=True),
        lax.all_gather(key_rope_b, "expert", axis=0, tiled=True),
    )
    back_blocks = split_blocks(back_keys, key_span)
    (
        gain_one_back,
        query_back,
        kv_down_back,
        kv_gain_back,
        kv_up_back,
        out_back,
        gain_two_back,
        router_back,
        shared_in_back,
        shared_out_back,
    ) = back_parts
    out_grad = cotangent.astype(jnp.float32)
    gate_grad = jnp.sum(out_grad[:, None, :] * picked, axis=2)
    result_grad = (route_gates[:, :, None] * out_grad[:, None, :]).astype(jnp.bfloat16)
    sent = jnp.zeros((buffer_rows, D), jnp.bfloat16).at[slot_place].set(result_grad.reshape(-1, D))
    owner_grad = lax.all_to_all(
        sent.reshape(owned, groups, capacity, D), "expert", split_axis=1, concat_axis=1, tiled=True
    ).reshape(owned, groups * capacity, D)
    hidden_grad = jnp.einsum(
        "erd,efd->erf", owner_grad, second_w, preferred_element_type=jnp.float32
    )
    _, pull_expert = jax.vjp(swiglu, joined)
    joined_grad = pull_expert(hidden_grad)[0].astype(jnp.bfloat16)
    grad_second = jnp.einsum(
        "erf,erd->efd", hidden_b, owner_grad, preferred_element_type=jnp.float32
    )
    grad_first = jnp.einsum(
        "erd,erf->edf", expert_rows, joined_grad, preferred_element_type=jnp.float32
    )
    rows_grad = jnp.einsum("erf,edf->erd", joined_grad, first_w, preferred_element_type=jnp.float32)
    sent_back = lax.all_to_all(
        rows_grad.reshape(owned, groups, capacity, D).astype(jnp.bfloat16),
        "expert",
        split_axis=1,
        concat_axis=1,
        tiled=True,
    ).astype(jnp.float32)
    route_grad = jnp.sum(
        sent_back.reshape(buffer_rows, D)[slot_place].reshape(row_count, topk_count, D), axis=1
    )
    expert_grads = (
        lax.psum_scatter(
            grad_first.astype(jnp.bfloat16), "dp", scatter_dimension=1, tiled=True
        ).astype(jnp.float32),
        lax.psum_scatter(
            grad_second.astype(jnp.bfloat16), "dp", scatter_dimension=2, tiled=True
        ).astype(jnp.float32),
    )
    probs_grad = jnp.sum(jnp.where(one_hot, gate_grad[:, :, None], 0.0), axis=1)
    logit_grad = (
        router_probs * (probs_grad - jnp.sum(router_probs * probs_grad, axis=-1, keepdims=True))
    ).astype(jnp.bfloat16)
    out_grad_b = out_grad.astype(jnp.bfloat16)
    shared_hidden_grad = matmul_nt(out_grad_b, shared_out_back)
    _, pull_shared = jax.vjp(swiglu, shared_join)
    shared_join_grad = pull_shared(shared_hidden_grad)[0].astype(jnp.bfloat16)
    grad_router = matmul_tn(normed_two_b, logit_grad)
    grad_shared_in = matmul_tn(normed_two_b, shared_join_grad)
    grad_shared_out = matmul_tn(shared_hidden_b, out_grad_b)
    normed_two_grad = (
        route_grad
        + matmul_nt(logit_grad, router_back)
        + matmul_nt(shared_join_grad, shared_in_back)
    )
    _, pull_norm_two = jax.vjp(rms_norm, middle, gain_two_back.astype(jnp.float32))
    middle_part, grad_gain_two = pull_norm_two(normed_two_grad)
    ffn_grads = (
        lax.psum_scatter(
            grad_gain_two.astype(jnp.bfloat16), "expert", scatter_dimension=0, tiled=True
        ).astype(jnp.float32),
        lax.psum_scatter(
            grad_router.astype(jnp.bfloat16), "expert", scatter_dimension=0, tiled=True
        ).astype(jnp.float32),
        lax.psum_scatter(
            grad_shared_in.astype(jnp.bfloat16), "expert", scatter_dimension=0, tiled=True
        ).astype(jnp.float32),
        lax.psum_scatter(
            grad_shared_out.astype(jnp.bfloat16), "expert", scatter_dimension=0, tiled=True
        ).astype(jnp.float32),
    )
    middle_grad = out_grad + middle_part
    middle_grad_b = middle_grad.astype(jnp.bfloat16)
    grad_out_w = matmul_tn(mixed_b, middle_grad_b)
    attn_grad_b = matmul_nt(middle_grad_b, out_back).reshape(row_count, H, DV).astype(jnp.bfloat16)
    row_delta = jnp.sum(attn_grad_b.astype(jnp.float32) * attn_full, axis=-1).T
    (query_nope_grad, query_rope_grad), key_terms = attend_grads(
        query_nope,
        query_rope,
        back_blocks,
        query_pos,
        prefix_end,
        score_scale,
        log_total,
        attn_grad_b,
        row_delta,
    )
    key_grad_all, value_grad_all, rope_grad_all = key_terms
    key_sums = (
        lax.psum_scatter(
            key_grad_all.reshape(-1, H * DN).astype(jnp.bfloat16),
            "expert",
            scatter_dimension=0,
            tiled=True,
        ).astype(jnp.float32),
        lax.psum_scatter(
            value_grad_all.reshape(-1, H * DV).astype(jnp.bfloat16),
            "expert",
            scatter_dimension=0,
            tiled=True,
        ).astype(jnp.float32),
        lax.psum_scatter(
            rope_grad_all.reshape(-1, DR).astype(jnp.bfloat16),
            "expert",
            scatter_dimension=0,
            tiled=True,
        ).astype(jnp.float32),
    )
    nope_sum, value_sum, rope_sum = key_sums
    kv_up_grad = (
        jnp.concatenate(
            [nope_sum.reshape(row_count, H, DN), value_sum.reshape(row_count, H, DV)], axis=-1
        )
        .reshape(row_count, H * (DN + DV))
        .astype(jnp.bfloat16)
    )
    grad_kv_up = matmul_tn(latent_b, kv_up_grad)
    latent_upstream = matmul_nt(kv_up_grad, kv_up_back)
    _, pull_latent = jax.vjp(rms_norm, latent, kv_gain_back.astype(jnp.float32))
    latent_grad, grad_kv_gain = pull_latent(latent_upstream)
    _, pull_key_rope = jax.vjp(
        lambda rope_part: rotate(rope_part, cosine, sine_table), kv_down[:, KVR:]
    )
    kv_down_grad = jnp.concatenate([latent_grad, pull_key_rope(rope_sum)[0]], axis=1).astype(
        jnp.bfloat16
    )
    grad_kv_down = matmul_tn(normed_b, kv_down_grad)
    _, pull_query_rope = jax.vjp(
        lambda rope_part: rotate(rope_part, cosine[:, None, :], sine_table[:, None, :]),
        query_raw[..., DN:],
    )
    query_grad = (
        jnp.concatenate([query_nope_grad, pull_query_rope(query_rope_grad)[0]], axis=-1)
        .reshape(row_count, H * (DN + DR))
        .astype(jnp.bfloat16)
    )
    grad_query = matmul_tn(normed_b, query_grad)
    normed_grad = matmul_nt(query_grad, query_back) + matmul_nt(kv_down_grad, kv_down_back)
    _, pull_norm_one = jax.vjp(rms_norm, values, gain_one_back.astype(jnp.float32))
    input_part, grad_gain_one = pull_norm_one(normed_grad)
    grad_tokens = middle_grad + input_part
    attn_grads = (
        lax.psum_scatter(
            grad_gain_one.astype(jnp.bfloat16), "expert", scatter_dimension=0, tiled=True
        ).astype(jnp.float32),
        lax.psum_scatter(
            grad_query.astype(jnp.bfloat16), "expert", scatter_dimension=0, tiled=True
        ).astype(jnp.float32),
        lax.psum_scatter(
            grad_kv_down.astype(jnp.bfloat16), "expert", scatter_dimension=0, tiled=True
        ).astype(jnp.float32),
        lax.psum_scatter(
            grad_kv_gain.astype(jnp.bfloat16), "expert", scatter_dimension=0, tiled=True
        ).astype(jnp.float32),
        lax.psum_scatter(
            grad_kv_up.astype(jnp.bfloat16), "expert", scatter_dimension=0, tiled=True
        ).astype(jnp.float32),
        lax.psum_scatter(
            grad_out_w.astype(jnp.bfloat16), "expert", scatter_dimension=0, tiled=True
        ).astype(jnp.float32),
    )
    summed = (
        lax.psum(attn_grads[0].astype(jnp.bfloat16), "dp").astype(jnp.float32),
        lax.psum(attn_grads[1].astype(jnp.bfloat16), "dp").astype(jnp.float32),
        lax.psum(attn_grads[2].astype(jnp.bfloat16), "dp").astype(jnp.float32),
        lax.psum(attn_grads[3].astype(jnp.bfloat16), "dp").astype(jnp.float32),
        lax.psum(attn_grads[4].astype(jnp.bfloat16), "dp").astype(jnp.float32),
        lax.psum(attn_grads[5].astype(jnp.bfloat16), "dp").astype(jnp.float32),
        lax.psum(ffn_grads[0].astype(jnp.bfloat16), "dp").astype(jnp.float32),
        lax.psum(ffn_grads[1].astype(jnp.bfloat16), "dp").astype(jnp.float32),
        lax.psum(ffn_grads[2].astype(jnp.bfloat16), "dp").astype(jnp.float32),
        lax.psum(ffn_grads[3].astype(jnp.bfloat16), "dp").astype(jnp.float32),
    )
    return (
        out,
        grad_tokens,
        summed[0],
        summed[1],
        summed[2],
        summed[3],
        summed[4],
        summed[5],
        summed[6],
        summed[7],
        summed[8],
        summed[9],
        expert_grads[0],
        expert_grads[1],
    )


def visible_scores(query, key, first_row, prefix_end, scale):
    scores = scale * lax.dot_general(
        query, key, (((1,), (1,)), ((), ())), preferred_element_type=jnp.float32
    )
    row = first_row + lax.broadcasted_iota(jnp.int32, scores.shape, 0)
    column = lax.broadcasted_iota(jnp.int32, scores.shape, 1)
    return jnp.where((column <= row) | (column < prefix_end), scores, MASKED)


def head_operands(heads, head, query, key_rope, kv_up):
    at = head * (DN + DV)
    rope = heads * DN + head * DR
    query_h = jnp.concatenate(
        [query[:, head * DN : (head + 1) * DN], query[:, rope : rope + DR]], axis=1
    )
    key_h = jnp.concatenate([kv_up[:, at : at + DN], key_rope], axis=1)
    return query_h, key_h, kv_up[:, at + DN : at + DN + DV]


def attend_kernel(heads, scale, prefix_ref, query_ref, key_rope_ref, kv_up_ref, mixed_ref):
    tile = query_ref.shape[0]
    first_row = pl.program_id(0) * tile
    query, key_rope, kv_up = query_ref[...], key_rope_ref[...], kv_up_ref[...]
    for head in range(heads):
        query_h, key_h, value_h = head_operands(heads, head, query, key_rope, kv_up)
        scores = visible_scores(query_h, key_h, first_row, prefix_ref[0], scale)
        powers = jnp.exp(scores - jnp.max(scores, axis=1, keepdims=True))
        probs = powers * (1.0 / jnp.sum(powers, axis=1, keepdims=True))
        mixed_ref[:, head * DV : (head + 1) * DV] = jnp.dot(
            probs.astype(jnp.bfloat16), value_h, preferred_element_type=jnp.float32
        ).astype(jnp.bfloat16)


def attend_back_kernel(
    heads, scale, prefix_ref, query_ref, grad_ref, key_rope_ref, kv_up_ref,
    query_nope_ref, query_rope_ref, kv_grad_ref, rope_grad_ref, key_total, value_total,
):
    step = pl.program_id(0)
    tile = query_ref.shape[0]

    @pl.when(step == 0)
    def _():
        key_total[...] = jnp.zeros_like(key_total)
        value_total[...] = jnp.zeros_like(value_total)

    query, key_rope, kv_up = query_ref[...], key_rope_ref[...], kv_up_ref[...]
    tn = (((0,), (0,)), ((), ()))
    for head in range(heads):
        query_h, key_h, value_h = head_operands(heads, head, query, key_rope, kv_up)
        grad_h = grad_ref[:, head * DV : (head + 1) * DV]
        scores = visible_scores(query_h, key_h, step * tile, prefix_ref[0], scale)
        powers = jnp.exp(scores - jnp.max(scores, axis=1, keepdims=True))
        probs = powers * (1.0 / jnp.sum(powers, axis=1, keepdims=True))
        prob_grad = lax.dot_general(
            grad_h, value_h, (((1,), (1,)), ((), ())), preferred_element_type=jnp.float32
        )
        delta = jnp.sum(probs * prob_grad, axis=1, keepdims=True)
        dscore = (probs * (prob_grad - delta)).astype(jnp.bfloat16)
        query_grad = scale * jnp.dot(dscore, key_h, preferred_element_type=jnp.float32)
        query_nope_ref[:, head * DN : (head + 1) * DN] = query_grad[:, :DN].astype(jnp.bfloat16)
        query_rope_ref[:, head * DR : (head + 1) * DR] = query_grad[:, DN:]
        key_total[head] += lax.dot_general(dscore, query_h, tn, preferred_element_type=jnp.float32)
        value_total[head] += lax.dot_general(
            probs.astype(jnp.bfloat16), grad_h, tn, preferred_element_type=jnp.float32
        )

    @pl.when(step == pl.num_programs(0) - 1)
    def _():
        rope = jnp.zeros(rope_grad_ref.shape, jnp.float32)
        for head in range(heads):
            at = head * (DN + DV)
            total = scale * key_total[head]
            kv_grad_ref[:, at : at + DN] = total[:, :DN].astype(jnp.bfloat16)
            kv_grad_ref[:, at + DN : at + DN + DV] = value_total[head].astype(jnp.bfloat16)
            rope += total[:, DN:]
        rope_grad_ref[...] = rope


def attend(prefix, query, key_rope, kv_up, heads, scale):
    length = query.shape[0]
    tile = min(256, length)
    whole = lambda value: pl.BlockSpec(value.shape, lambda i: (0, 0))
    rows = lambda width: pl.BlockSpec((tile, width), lambda i: (i, 0))
    return pl.pallas_call(
        functools.partial(attend_kernel, heads, scale),
        grid=(length // tile,),
        out_shape=jax.ShapeDtypeStruct((length, heads * DV), jnp.bfloat16),
        in_specs=[pl.BlockSpec(memory_space=pltpu.SMEM), rows(query.shape[1]), whole(key_rope), whole(kv_up)],
        out_specs=rows(heads * DV),
        compiler_params=pltpu.CompilerParams(vmem_limit_bytes=48 * 1024 * 1024),
        cost_estimate=pl.CostEstimate(
            flops=2 * heads * length * length * (DN + DR + DV),
            transcendentals=heads * length * length,
            bytes_accessed=2 * length * heads * (DN + DR + DN + DV + DV),
        ),
        name="attend",
    )(prefix, query, key_rope, kv_up)


def attend_back(prefix, query, grad, key_rope, kv_up, heads, scale):
    length = query.shape[0]
    tile = min(256, length)
    whole = lambda shape: pl.BlockSpec(shape, lambda i: (0, 0))
    rows = lambda width: pl.BlockSpec((tile, width), lambda i: (i, 0))
    return pl.pallas_call(
        functools.partial(attend_back_kernel, heads, scale),
        grid=(length // tile,),
        out_shape=[
            jax.ShapeDtypeStruct((length, heads * DN), jnp.bfloat16),
            jax.ShapeDtypeStruct((length, heads * DR), jnp.float32),
            jax.ShapeDtypeStruct(kv_up.shape, jnp.bfloat16),
            jax.ShapeDtypeStruct(key_rope.shape, jnp.float32),
        ],
        in_specs=[
            pl.BlockSpec(memory_space=pltpu.SMEM),
            rows(query.shape[1]),
            rows(grad.shape[1]),
            whole(key_rope.shape),
            whole(kv_up.shape),
        ],
        out_specs=[rows(heads * DN), rows(heads * DR), whole(kv_up.shape), whole(key_rope.shape)],
        scratch_shapes=[
            pltpu.VMEM((heads, length, DN + DR), jnp.float32),
            pltpu.VMEM((heads, length, DV), jnp.float32),
        ],
        compiler_params=pltpu.CompilerParams(vmem_limit_bytes=48 * 1024 * 1024),
        cost_estimate=pl.CostEstimate(
            flops=2 * heads * length * length * 3 * (DN + DR + DV),
            transcendentals=heads * length * length,
            bytes_accessed=2 * length * heads * 3 * (DN + DR + DN + DV + DV),
        ),
        name="attend_back",
    )(prefix, query, grad, key_rope, kv_up)


def expert_kernel(expert_count, spot, *refs):
    x_in, g_in = refs[0:4], refs[4:8]
    first_in, second_in, router = refs[8:10], refs[10:12], refs[12]
    back_out = refs[13:17]
    hidden_out, grads_out, rows_out, grad_rows_out, second_out, logit_out = refs[17:23]
    first_w, second_w, x_buf, g_buf, back_st, hidden_st, grads_st, in_sem, w_sem, out_sem, keep_sem = refs[23:]
    lane, core, expert = spot[0], spot[1], spot[2]
    lanes = len(x_in)
    rows = x_buf.shape[1]
    depth, half = first_w.shape[1], first_w.shape[2]
    slab = depth // lanes
    side = half // 2

    loads = []
    for step in range(lanes):
        loads.append(
            (
                pltpu.make_async_copy(x_in[step], x_buf.at[step], in_sem.at[0, step]),
                pltpu.make_async_copy(g_in[step], g_buf.at[step], in_sem.at[1, step]),
            )
        )
    first_loads, second_loads = [], []
    for part in range(2):
        slot = core if part == 0 else 1 - core
        for step in range(lanes):
            at = pl.multiple_of((lane ^ step) * slab, slab)
            first_loads.append(
                pltpu.make_async_copy(
                    first_in[part].at[pl.ds(step * slab, slab), :], first_w.at[slot, pl.ds(at, slab), :], w_sem.at[0, part, step]
                )
            )
            second_loads.append(
                pltpu.make_async_copy(
                    second_in[part].at[pl.ds(step * side, side), :],
                    second_w.at[pl.ds(pl.multiple_of(slot * side, side), side), pl.ds(at, slab)],
                    w_sem.at[1, part, step],
                )
            )
    loads[0][0].start()
    for copy in first_loads:
        copy.start()
    loads[0][1].start()
    for copy in second_loads:
        copy.start()
    for step in range(1, lanes):
        loads[step][0].start()
        loads[step][1].start()

    def kept(step):
        where = pl.ds(step * rows, rows)
        return [
            pltpu.make_async_copy(x_buf.at[step], rows_out.at[where, :], keep_sem.at[step]),
            pltpu.make_async_copy(g_buf.at[step], grad_rows_out.at[where, :], keep_sem.at[lanes + step]),
        ]

    second_kept = pltpu.make_async_copy(second_w, second_out, keep_sem.at[2 * lanes])

    def stores(step, slot, back):
        where = pl.ds(pl.multiple_of(step * rows, rows), rows)
        return [
            pltpu.make_async_copy(back_st.at[slot], back, out_sem.at[slot, 0]),
            pltpu.make_async_copy(hidden_st.at[slot], hidden_out.at[where, :], out_sem.at[slot, 1]),
            pltpu.make_async_copy(grads_st.at[slot, 0], grads_out.at[0, where, :], out_sem.at[slot, 2]),
            pltpu.make_async_copy(grads_st.at[slot, 1], grads_out.at[1, where, :], out_sem.at[slot, 3]),
        ]

    nt = (((1,), (1,)), ((), ()))

    def compute(step, slot):
        x = x_buf[step]
        a = jnp.dot(x, first_w[0], preferred_element_type=jnp.float32)
        b = jnp.dot(x, first_w[1], preferred_element_type=jnp.float32)
        logits = jnp.dot(x, router[...], preferred_element_type=jnp.float32)
        column = lax.broadcasted_iota(jnp.int32, logits.shape, 1)
        logits = jnp.where(column < expert_count, logits, -1e30)
        top = jnp.max(logits, axis=1, keepdims=True)
        powers = jnp.exp(logits - top)
        probs = powers / jnp.sum(powers, axis=1, keepdims=True)
        hot = (column == expert).astype(jnp.float32)
        gate = jnp.sum(probs * hot, axis=1, keepdims=True)
        g = g_buf[step]
        up = lax.dot_general(g, second_w[...], nt, preferred_element_type=jnp.float32)
        sig = 1.0 / (1.0 + jnp.exp(-a))
        act = a * sig
        hidden = act * b
        hidden_st[slot] = (gate * hidden).astype(jnp.bfloat16)
        gate_grad = jnp.sum(up * hidden, axis=1, keepdims=True)
        up = up * gate
        grad_b = (up * act).astype(jnp.bfloat16)
        grad_a = (up * b * (sig + act * (1.0 - sig))).astype(jnp.bfloat16)
        grads_st[slot, core] = grad_a
        grads_st[slot, 1 - core] = grad_b
        logit = (gate * gate_grad * (hot - probs)).astype(jnp.bfloat16)
        logit_out[pl.ds(pl.multiple_of(step * rows, rows), rows), :] = logit
        back = lax.dot_general(grad_a, first_w[0], nt, preferred_element_type=jnp.float32)
        back += lax.dot_general(grad_b, first_w[1], nt, preferred_element_type=jnp.float32)
        back += lax.dot_general(logit, router[...], nt, preferred_element_type=jnp.float32)
        back_st[slot] = back.astype(jnp.bfloat16)

    for copy in first_loads + second_loads:
        copy.wait()
    second_kept.start()

    def body_step(step, carry):
        slot = lax.rem(step, 2)
        for i in range(lanes):

            @pl.when(step == i)
            def _():
                loads[i][0].wait()
                loads[i][1].wait()
                for copy in kept(i):
                    copy.start()

        for i in range(2, lanes):

            @pl.when(step == i)
            def _():
                for copy in stores(i - 2, i % 2, back_out[i - 2]):
                    copy.wait()

        compute(step, slot)
        for i in range(lanes):

            @pl.when(step == i)
            def _():
                for copy in stores(i, i % 2, back_out[i]):
                    copy.start()

        return carry

    lax.fori_loop(0, lanes, body_step, 0)
    for step in range(lanes - 2, lanes):
        for copy in stores(step, step % 2, back_out[step]):
            copy.wait()
    for step in range(lanes):
        for copy in kept(step):
            copy.wait()
    second_kept.wait()


def expert_step(spot, x_pieces, g_pieces, first_mine, first_other, second_mine, second_other, router_wide, expert_count):
    rows, depth = x_pieces[0].shape
    half = first_mine.shape[1]
    lanes = len(x_pieces)
    total = rows * lanes
    bf = jnp.bfloat16
    any_spec = pl.BlockSpec(memory_space=pl.ANY)
    vmem_spec = pl.BlockSpec(memory_space=pltpu.VMEM)
    return pl.pallas_call(
        functools.partial(expert_kernel, expert_count),
        out_shape=[jax.ShapeDtypeStruct((rows, depth), bf)] * lanes
        + [
            jax.ShapeDtypeStruct((total, half), bf),
            jax.ShapeDtypeStruct((2, total, half), bf),
            jax.ShapeDtypeStruct((total, depth), bf),
            jax.ShapeDtypeStruct((total, depth), bf),
            jax.ShapeDtypeStruct((half, depth), bf),
            jax.ShapeDtypeStruct((total, 128), bf),
        ],
        in_specs=[pl.BlockSpec(memory_space=pltpu.SMEM)] + [any_spec] * (2 * lanes + 4) + [vmem_spec],
        out_specs=[any_spec] * (lanes + 5) + [vmem_spec],
        scratch_shapes=[
            pltpu.VMEM((2, depth, half), bf),
            pltpu.VMEM((half, depth), bf),
            pltpu.VMEM((lanes, rows, depth), bf),
            pltpu.VMEM((lanes, rows, depth), bf),
            pltpu.VMEM((2, rows, depth), bf),
            pltpu.VMEM((2, rows, half), bf),
            pltpu.VMEM((2, 2, rows, half), bf),
            pltpu.SemaphoreType.DMA((2, lanes)),
            pltpu.SemaphoreType.DMA((2, 2, lanes)),
            pltpu.SemaphoreType.DMA((2, 4)),
            pltpu.SemaphoreType.DMA((2 * lanes + 1,)),
        ],
        compiler_params=pltpu.CompilerParams(vmem_limit_bytes=60 * 1024 * 1024),
        cost_estimate=pl.CostEstimate(
            flops=10 * total * depth * half,
            transcendentals=total * half,
            bytes_accessed=2 * (3 * depth * half * 2 + total * (5 * depth + 3 * half)),
        ),
        name="expert_rows",
    )(spot, *x_pieces, *g_pieces, first_mine, first_other, second_mine, second_other, router_wide)


def shared_body(
    tokens,
    cotangent,
    prefix,
    routes,
    norm1_gain,
    w_query,
    w_kv_down,
    kv_gain,
    w_kv_up,
    w_out,
    norm2_gain,
    w_router,
    shared_in,
    shared_out,
    expert_in,
    expert_out,
):
    rows = tokens.shape[0]
    topk = routes.shape[1]
    chips = lax.axis_size("z")
    lanes = lax.axis_size("dp")
    groups = chips * 2
    owned = expert_in.shape[0]
    expert_count = owned * groups
    capacity = 3 * rows * topk // (2 * expert_count)
    heads = H // groups
    length = rows * groups
    scale = float(DN + DR) ** (-0.5)
    my_dp = lax.axis_index("dp")
    my_z = lax.axis_index("z")
    my_core = lax.axis_index("core")
    my_expert = my_z * 2 * owned + my_dp
    group = ("z", "core")
    hidden_n = shared_out.shape[0]
    kv_cols = w_kv_down.shape[1]
    half = expert_in.shape[2] // 2

    def gather(value):
        return lax.all_gather(value, group, axis=0, tiled=True)

    def scatter_sum(value):
        return lax.psum_scatter(value, group, scatter_dimension=0, tiled=True)

    def fence(*values):
        return lax.optimization_barrier(values)

    def swap(value):
        return lax.ppermute(value, "core", [(0, 1), (1, 0)])

    def ordered(mine, other, axis):
        return jnp.where(
            my_core == 0,
            jnp.concatenate([mine, other], axis=axis),
            jnp.concatenate([other, mine], axis=axis),
        )

    def halves(value, axis):
        size = value.shape[axis] // 2
        mine = lax.dynamic_slice_in_dim(value, my_core * size, size, axis)
        other = lax.dynamic_slice_in_dim(value, (1 - my_core) * size, size, axis)
        return mine, other

    def exchange(value):
        return lax.all_to_all(value, group, split_axis=0, concat_axis=0, tiled=True)

    def to_lane(value, step):
        return lax.ppermute(value, "dp", [(lane, lane ^ step) for lane in range(lanes)])

    def by_lane(pieces):
        full = jnp.zeros((lanes,) + pieces[0].shape, pieces[0].dtype)
        for step in range(lanes):
            full = lax.dynamic_update_index_in_dim(full, pieces[step], my_dp ^ step, 0)
        return full

    def to_lanes(pieces):
        return [pieces[0]] + [to_lane(pieces[step], step) for step in range(1, lanes)]

    def lane_exchange(value):
        return to_lanes(
            [lax.dynamic_index_in_dim(value, my_dp ^ step, 0, keepdims=False) for step in range(lanes)]
        )

    def own_part(value):
        part = value.shape[0] // lanes
        return lax.dynamic_slice_in_dim(value, my_dp * part, part, 0).transpose(1, 0, 2)

    share = norm1_gain.shape[0]
    kv_share = kv_gain.shape[0]
    used = kv_cols + expert_count
    extra = 640 - used
    gains = jnp.concatenate([norm1_gain, norm2_gain, kv_gain])
    gain_rows = gains.shape[0] // extra
    small = jnp.concatenate(
        [
            w_kv_down,
            w_router,
            jnp.concatenate(
                [
                    jnp.pad(gains.reshape(gain_rows, extra), ((0, share - rows - gain_rows), (0, 0))),
                    jnp.pad(routes.astype(jnp.bfloat16), ((0, 0), (0, extra - topk))),
                ]
            ),
        ],
        axis=1,
    )
    query_n = heads * (DN + DR)
    kv_width = heads * (DN + DV)
    fold = share // kv_share
    query_parts = w_query.reshape(share, groups, heads, DN + DR)
    attention_parts = jnp.concatenate(
        [
            query_parts[..., :DN].reshape(share, groups, heads * DN),
            query_parts[..., DN:].reshape(share, groups, heads * DR),
            w_kv_up.reshape(kv_share, groups, fold, kv_width // fold)
            .transpose(0, 2, 1, 3)
            .reshape(share, groups, kv_width // fold),
        ],
        axis=2,
    )
    shared_parts = own_part(
        shared_in.reshape(share, 2, groups, hidden_n)
        .transpose(0, 2, 1, 3)
        .reshape(share, groups, 2 * hidden_n)
    )
    tokens_all = gather(tokens)
    small_all = gather(small)
    attention_moved = exchange(own_part(attention_parts))
    attention_pieces = to_lanes([attention_moved] * lanes)
    def lane_pieces(value, axis):
        keep, give = halves(value, axis)
        received = swap(give)
        pieces = []
        for step in range(lanes):
            lane = my_dp ^ step
            pieces.append(
                jnp.where(
                    lane // 2 == my_core,
                    lax.dynamic_index_in_dim(keep, lane % 2, 0, keepdims=False),
                    lax.dynamic_index_in_dim(received, lane % 2, 0, keepdims=False),
                )
            )
        return pieces

    first_pieces = to_lanes(lane_pieces(expert_in, 2))
    second_sources = lane_pieces(expert_out, 1)

    shared_moved = exchange(shared_parts)
    tokens_all, small_all, attention_pieces, first_pieces[:2], second_sources, shared_moved = fence(
        tokens_all, small_all, attention_pieces, first_pieces[:2], second_sources, shared_moved
    )
    grad_all = gather(cotangent)
    second_pieces = to_lanes(second_sources)
    spare = small_all[:, used:].reshape(chips, 2, share, extra)
    routes_mine = lax.dynamic_index_in_dim(
        spare[:, :, share - rows :, :topk], my_core, axis=1, keepdims=False
    ).astype(jnp.int32)

    router_w = small_all[:, kv_cols:used]
    gains_all = (
        spare.reshape(groups, share, extra)[:, :gain_rows].reshape(groups, gain_rows * extra)
    ).astype(jnp.float32)
    gain_one = gains_all[:, :share].reshape(-1)
    gain_two = gains_all[:, share : 2 * share].reshape(-1)
    gain_kv = gains_all[:, 2 * share :].reshape(-1)
    kv_down_w = small_all[:, :kv_cols]
    attention_w = by_lane(attention_pieces).transpose(1, 0, 2, 3)
    query_w = attention_w[..., :query_n].reshape(share * groups, query_n)
    kv_up_w = attention_w[..., query_n:].reshape(kv_share * groups, kv_width)

    plane = my_z * 2 * owned + (my_dp ^ jnp.arange(lanes, dtype=jnp.int32))
    member = jnp.any(routes_mine[:, :, :, None] == plane[None, None, None, :], axis=2)
    earlier = (jnp.arange(rows)[:, None] > jnp.arange(rows)[None, :]).astype(jnp.float32)
    place = jnp.einsum(
        "st,ztq->zqs", earlier, member.astype(jnp.float32), precision=lax.Precision.HIGHEST
    )
    slots = jnp.arange(capacity, dtype=jnp.float32)
    pick = (
        (place[:, :, None, :] == slots[None, None, :, None]) & member.transpose(0, 2, 1)[:, :, None, :]
    ).astype(jnp.bfloat16)

    def picked(blocks):
        return [
            jnp.einsum(
                "zst,ztd->zsd", pick[:, step], blocks, preferred_element_type=jnp.float32
            ).astype(jnp.bfloat16)
            for step in range(lanes)
        ]

    def split_rows(value):
        pieces = value.reshape(lanes, chips, capacity, D)
        return [pieces[step] for step in range(lanes)]

    def placed(pieces):
        return jnp.einsum(
            "zlst,zlsd->ztd", pick, jnp.stack(pieces, axis=1), preferred_element_type=jnp.float32
        )

    def my_blocks(value):
        return lax.dynamic_index_in_dim(
            value.reshape(chips, 2, rows, D), my_core, axis=1, keepdims=False
        )

    def add_mine(total, mine):
        spread = jnp.where((jnp.arange(2) == my_core)[None, :, None, None], mine[:, None], 0.0)
        return total.reshape(chips, 2, rows, D) + spread

    positions = jnp.arange(length, dtype=jnp.int32)
    cosine, sine_table = tables(positions, DR // 2)
    values_all = tokens_all.astype(jnp.float32)
    inverse_one = lax.rsqrt(jnp.mean(values_all * values_all, axis=-1, keepdims=True) + EPSILON)
    normed_b = (values_all * inverse_one * gain_one).astype(jnp.bfloat16)
    query_raw = matmul(normed_b, query_w)
    query_rope = rotate(
        query_raw[:, heads * DN :].reshape(length, heads, DR), cosine[:, None, :], sine_table[:, None, :]
    )
    query = jnp.concatenate(
        [query_raw[:, : heads * DN], query_rope.reshape(length, heads * DR)], axis=1
    ).astype(jnp.bfloat16)
    kv_down = matmul(normed_b, kv_down_w)
    latent = kv_down[:, :KVR]
    inverse_kv = lax.rsqrt(jnp.mean(latent * latent, axis=-1, keepdims=True) + EPSILON)
    latent_n = latent * inverse_kv
    latent_b = (latent_n * gain_kv).astype(jnp.bfloat16)
    key_rope = rotate(kv_down[:, KVR:], cosine, sine_table).astype(jnp.bfloat16)
    kv_up = matmul(latent_b, kv_up_w).astype(jnp.bfloat16)
    mixed_b = attend(prefix, query, key_rope, kv_up, heads, scale)
    mixed_b, second_pieces, first_pieces = fence(mixed_b, second_pieces, first_pieces)
    grad_picked = picked(my_blocks(grad_all))
    attn_sum = scatter_sum(matmul(mixed_b, w_out).astype(jnp.bfloat16))
    grad_pieces = to_lanes(grad_picked)
    first_mine = jnp.concatenate(first_pieces)
    first_other = swap(first_mine)

    attn_sum, first_other, grad_pieces = fence(attn_sum, first_other, grad_pieces)
    shared_pieces = to_lanes([shared_moved] * lanes)
    second_mine = jnp.concatenate(second_pieces)
    second_other = swap(second_mine)
    middle = tokens.astype(jnp.float32) + attn_sum.astype(jnp.float32)

    inverse_two = lax.rsqrt(jnp.mean(middle * middle, axis=-1, keepdims=True) + EPSILON)
    normed_two_b = (middle * inverse_two * gain_two).astype(jnp.bfloat16)
    x2 = gather(normed_two_b)
    x2, shared_pieces, second_other = fence(x2, shared_pieces, second_other)
    x_pieces = to_lanes(picked(my_blocks(x2)))
    shared_w = by_lane(shared_pieces).transpose(1, 0, 2, 3).reshape(share * groups, 2 * hidden_n)

    shared_a = matmul(x2, shared_w[:, :hidden_n])
    shared_b = matmul(x2, shared_w[:, hidden_n:])
    shared_sig = jax.nn.sigmoid(shared_a)
    shared_hidden = (shared_a * shared_sig * shared_b).astype(jnp.bfloat16)
    shared_part = matmul(shared_hidden, shared_out).astype(jnp.bfloat16)
    shared_up = matmul_nt(grad_all, shared_out)
    shared_ga = (shared_up * shared_b * shared_sig * (1.0 + shared_a * (1.0 - shared_sig))).astype(
        jnp.bfloat16
    )
    shared_gb = (shared_up * shared_a * shared_sig).astype(jnp.bfloat16)
    shared_g = jnp.concatenate([shared_ga, shared_gb], axis=1)
    grad_shared_out = matmul_tn(shared_hidden, grad_all).astype(jnp.bfloat16)
    grad_shared_in = matmul_tn(x2, shared_g).astype(jnp.bfloat16)
    shared_back = matmul_nt(shared_g, shared_w).astype(jnp.bfloat16)
    x_pieces, shared_part, shared_back, grad_shared_out, grad_shared_in = fence(
        x_pieces, shared_part, shared_back, grad_shared_out, grad_shared_in
    )

    def lane_parts(value):
        count = value.shape[0] // groups
        return lane_exchange(
            value.reshape(groups, lanes, count // lanes, value.shape[1]).transpose(1, 0, 2, 3)
        )

    def lane_rows(value):
        return lane_exchange(value.reshape(lanes, value.shape[0] // lanes, value.shape[1]))

    def lane_sum(pieces):
        return sum(piece.astype(jnp.float32) for piece in pieces).astype(jnp.bfloat16)

    flat = (chips * capacity, D)
    part = share // lanes
    shared_parts = lane_exchange(
        jnp.concatenate(
            [
                grad_shared_in.reshape(groups, lanes, part, 2 * hidden_n)
                .transpose(1, 0, 2, 3)
                .reshape(lanes, groups * part, 2 * hidden_n),
                grad_shared_out.reshape(lanes, -1, 2 * hidden_n),
            ],
            axis=1,
        )
    )
    router_lane = kv_cols - KVR
    spot = jnp.stack([my_dp, my_core, my_expert]).astype(jnp.int32)
    step_out = expert_step(
        spot,
        [piece.reshape(flat) for piece in x_pieces],
        [piece.reshape(flat) for piece in grad_pieces],
        first_mine,
        first_other,
        second_mine,
        second_other,
        jnp.pad(router_w, ((0, 0), (0, 128 - expert_count))),
        expert_count,
    )
    step_out, shared_parts = fence(step_out, shared_parts)
    rows_grad = step_out[:lanes]
    row_hidden, grads, x_rows, grad_rows, second_w, logit_grad = step_out[lanes:]
    back_pieces = to_lanes([piece.reshape(chips, capacity, D) for piece in rows_grad])
    grad_second = matmul_tn(row_hidden, grad_rows).astype(jnp.bfloat16)
    result_b = matmul(row_hidden, second_w).astype(jnp.bfloat16)
    logit_wide = jnp.pad(
        logit_grad[:, :expert_count], ((0, 0), (router_lane, 128 - router_lane - expert_count))
    )
    grad_router = matmul_tn(x_rows, logit_wide)
    shared_sum = lane_sum(shared_parts)
    back_pieces, grad_second, grad_router, result_b, x_rows, grads, shared_sum = fence(
        back_pieces, grad_second, grad_router, result_b, x_rows, grads, shared_sum
    )
    shared_in_moved = exchange(shared_sum[: groups * part].reshape(groups, part, 2 * hidden_n))
    shared_out_own = shared_sum[groups * part :].reshape(part, -1)
    grad_first_other = matmul_tn(x_rows, grads[1]).astype(jnp.bfloat16)
    grad_first_mine = matmul_tn(x_rows, grads[0]).astype(jnp.bfloat16)

    result_pieces = to_lanes(split_rows(result_b))
    first_sent = swap(grad_first_other)
    second_hold, second_send = halves(grad_second, 0)
    second_sent = swap(second_send)
    back_part = add_mine(shared_back.astype(jnp.float32), placed(back_pieces)).astype(jnp.bfloat16)
    normed_two_grad = scatter_sum(back_part.reshape(length, D))
    normed_two_grad, first_sent, second_sent, grad_first_mine = fence(
        normed_two_grad, first_sent, second_sent, grad_first_mine
    )
    normed_two_grad = normed_two_grad.astype(jnp.float32)
    normal_two = middle * inverse_two
    grad_gain_two = jnp.sum(normed_two_grad * normal_two, axis=0)
    scaled = normed_two_grad * gain_two
    middle_grad = cotangent.astype(jnp.float32) + inverse_two * (
        scaled - normal_two * jnp.mean(scaled * normal_two, axis=-1, keepdims=True)
    )
    grad_first = (grad_first_mine.astype(jnp.float32) + first_sent.astype(jnp.float32)).astype(jnp.bfloat16)
    first_back = lane_exchange(grad_first.reshape(lanes, D // lanes, half))
    grad_second = (second_hold.astype(jnp.float32) + second_sent.astype(jnp.float32)).astype(jnp.bfloat16)

    middle_all = gather(middle_grad.astype(jnp.bfloat16))
    middle_all, result_pieces, grad_second, shared_in_moved = fence(
        middle_all, result_pieces, grad_second, shared_in_moved
    )
    early = jnp.concatenate(
        [
            shared_in_moved.reshape(groups, part, 2, hidden_n)
            .transpose(1, 2, 0, 3)
            .reshape(part, 2 * groups * hidden_n),
            shared_out_own,
        ],
        axis=1,
    )
    early_pieces = to_lanes([early] * lanes)
    out_part = add_mine(shared_part.astype(jnp.float32), placed(result_pieces)).astype(jnp.bfloat16)
    ffn = scatter_sum(out_part.reshape(length, D))
    second_back = lane_exchange(
        grad_second.reshape(half // 2, lanes, D // lanes).transpose(1, 0, 2)
    )
    attn_grad = matmul_nt(middle_all, w_out).astype(jnp.bfloat16)
    query_nope_grad, query_rope_grad, kv_up_grad, rope_grad = attend_back(
        prefix, query, attn_grad, key_rope, kv_up, heads, scale
    )
    query_nope_grad, query_rope_grad, kv_up_grad, rope_grad, first_back, early_pieces = fence(
        query_nope_grad, query_rope_grad, kv_up_grad, rope_grad, first_back, early_pieces
    )
    grad_out_w = matmul_tn(mixed_b, middle_all).astype(jnp.bfloat16)
    out_w_parts = lane_rows(grad_out_w)

    def own_slices(pieces, axis):
        def of_core(core):
            near = my_dp // 2 == core
            pair = [jnp.where(near, pieces[i], pieces[2 + i]) for i in range(2)]
            flip = my_dp % 2 == 1
            return jnp.stack(
                [jnp.where(flip, pair[1], pair[0]), jnp.where(flip, pair[0], pair[1])]
            )

        return ordered(of_core(my_core), swap(of_core(1 - my_core)), axis).astype(jnp.float32)

    grad_kv_up = matmul_tn(latent_b, kv_up_grad).astype(jnp.bfloat16)
    latent_up = matmul_nt(kv_up_grad, kv_up_w)
    grad_kv_gain = jnp.sum(latent_up * latent_n, axis=0)
    latent_scaled = latent_up * gain_kv
    latent_grad = inverse_kv * (
        latent_scaled - latent_n * jnp.mean(latent_scaled * latent_n, axis=-1, keepdims=True)
    )
    rope_grad = rotate(rope_grad, cosine, -sine_table)
    kv_down_grad = jnp.concatenate([latent_grad, rope_grad], axis=1).astype(jnp.bfloat16)
    query_rope_grad = rotate(
        query_rope_grad.reshape(length, heads, DR), cosine[:, None, :], -sine_table[:, None, :]
    )
    query_grad = jnp.concatenate(
        [query_nope_grad, query_rope_grad.reshape(length, heads * DR).astype(jnp.bfloat16)], axis=1
    )
    normed_part = matmul_nt(query_grad, query_w) + matmul_nt(kv_down_grad, kv_down_w)
    grad_gain_one = jnp.sum(normed_part * (values_all * inverse_one), axis=0)
    normed_part, ffn = fence(normed_part.astype(jnp.bfloat16), ffn)
    grad_query = matmul_tn(normed_b, query_grad).astype(jnp.bfloat16)
    attention_grad = jnp.concatenate(
        [
            grad_query.reshape(groups, share, query_n),
            grad_kv_up.reshape(groups, share, kv_width // fold),
        ],
        axis=2,
    ).reshape(groups * share, query_n + kv_width // fold)
    attention_moved = exchange(lane_sum(lane_parts(attention_grad)))

    kv_wide = jnp.pad(kv_down_grad, ((0, 0), (0, 640 - kv_cols)))
    gains_grad = jnp.concatenate(
        [
            grad_gain_one.reshape(groups, share),
            grad_gain_two.reshape(groups, share),
            grad_kv_gain.reshape(groups, kv_share),
        ],
        axis=1,
    ).reshape(groups, gain_rows, extra)
    gains_wide = jnp.pad(
        gains_grad, ((0, 0), (0, share - gain_rows), (128 - extra, 0))
    ).reshape(groups * share, 128)
    small_grad = (
        matmul_tn(normed_b, kv_wide) + jnp.pad(grad_router + gains_wide, ((0, 0), (KVR, 0)))
    ).astype(jnp.bfloat16)
    small_sum = scatter_sum(small_grad)
    small_sum, normed_part = fence(small_sum, normed_part)
    normed_grad = scatter_sum(normed_part)
    small_part = lane_sum(lane_rows(small_sum))

    grad_first = own_slices(first_back, 2)
    grad_second = own_slices(second_back, 1)
    def lane_gather(value):
        return lax.all_gather(value, "dp", axis=0, tiled=True)

    early = by_lane(early_pieces).reshape(share, -1)
    cut = 2 * groups * hidden_n
    shared_in_grad = early[:, :cut].astype(jnp.float32)
    shared_out_grad = early[:, cut:].reshape(hidden_n, D).astype(jnp.float32)
    query_cols = attention_moved[..., :query_n].transpose(1, 0, 2)
    query_cols = jnp.concatenate(
        [
            query_cols[..., : heads * DN].reshape(part, groups, heads, DN),
            query_cols[..., heads * DN :].reshape(part, groups, heads, DR),
        ],
        axis=-1,
    ).reshape(part, H * (DN + DR))
    kv_cols_grad = (
        attention_moved[..., query_n:]
        .reshape(groups, part // fold, fold, kv_width // fold)
        .transpose(1, 2, 0, 3)
        .reshape(part, groups * kv_width // fold)
    )
    late = jnp.concatenate([query_cols, kv_cols_grad, lane_sum(out_w_parts), small_part], axis=1)
    late, normed_grad = fence(late, normed_grad)
    late = lane_gather(late)
    cut = H * (DN + DR)
    query_grad_out = late[:, :cut].astype(jnp.float32)
    kv_up_grad_out = (
        late[:, cut : cut + groups * kv_width // fold]
        .reshape(kv_share, fold, groups, kv_width // fold)
        .transpose(0, 2, 1, 3)
        .reshape(kv_share, H * (DN + DV))
        .astype(jnp.float32)
    )
    cut += groups * kv_width // fold
    out_w_grad = late[:, cut : cut + D].astype(jnp.float32)
    small_sum = late[:, cut + D :].astype(jnp.float32)
    gains_sum = small_sum[:gain_rows, used:].reshape(-1)

    out = (middle + ffn.astype(jnp.float32)).astype(jnp.bfloat16)
    normed_grad = normed_grad.astype(jnp.float32)
    values = tokens.astype(jnp.float32)
    inverse_own = lax.rsqrt(jnp.mean(values * values, axis=-1, keepdims=True) + EPSILON)
    normal_one = values * inverse_own
    scaled_one = normed_grad * gain_one
    grad_tokens = middle_grad + inverse_own * (
        scaled_one - normal_one * jnp.mean(scaled_one * normal_one, axis=-1, keepdims=True)
    )
    return (
        out,
        grad_tokens,
        gains_sum[:share],
        query_grad_out,
        small_sum[:, :kv_cols],
        gains_sum[2 * share :],
        kv_up_grad_out,
        out_w_grad,
        gains_sum[share : 2 * share],
        small_sum[:, kv_cols:used],
        shared_in_grad,
        shared_out_grad,
        grad_first,
        grad_second,
    )


def solution(mesh):
    groups = mesh.shape["expert"]
    lanes = mesh.shape["dp"]
    if H % groups == 0 and groups % 2 == 0 and lanes == 4:
        inner = Mesh(mesh.devices.reshape(lanes, groups // 2, 2), ("dp", "z", "core"))
        return sharded(shared_body, inner, "dp", ("z", "core"))
    return sharded(body, mesh, "dp", "expert")


def sharded(function, mesh, dp, expert):
    every = (dp, expert) if isinstance(expert, str) else (dp,) + expert
    row = P(every, None)
    vector = P(expert)
    matrix = P(expert, None)
    first = P(expert, dp, None)
    second = P(expert, None, dp)
    weights = (vector, matrix, matrix, vector, matrix, matrix, vector, matrix, matrix, matrix, first, second)
    return jax.shard_map(
        function,
        mesh=mesh,
        in_specs=(row, row, P(dp), row) + weights,
        out_specs=(row, row) + weights,
        check_vma=False,
    )
```

```python
import functools

import jax
import jax.numpy as jnp
from jax import lax
from jax.experimental import pallas as pl
from jax.experimental.pallas import tpu as pltpu
from jax.sharding import Mesh
from jax.sharding import PartitionSpec as P

D = 2048
H = 16
DN = 128
DR = 64
DV = 128
KVR = 512


EPSILON = 1e-06
MASKED = -1e30


def rms_norm(values, gain_vector):
    return (
        values
        * lax.rsqrt(jnp.mean(values * values, axis=-1, keepdims=True) + EPSILON)
        * gain_vector
    )


def tables(positions, half_width):
    frequency = 10000.0 ** (-jnp.arange(half_width, dtype=jnp.float32) / half_width)
    angles = positions.astype(jnp.float32)[:, None] * frequency[None, :]
    return (jnp.cos(angles), jnp.sin(angles))


def rotate(values, cosine, sine_table):
    half_width = values.shape[-1] // 2
    front_part = values[..., :half_width]
    back_part = values[..., half_width:]
    return jnp.concatenate(
        [
            front_part * cosine - back_part * sine_table,
            back_part * cosine + front_part * sine_table,
        ],
        axis=-1,
    )


def swiglu(joined):
    half_width = joined.shape[-1] // 2
    return jax.nn.silu(joined[..., :half_width]) * joined[..., half_width:]


def matmul(left_side, right_side):
    return jnp.dot(left_side, right_side, preferred_element_type=jnp.float32)


def matmul_tn(left_side, right_side):
    return lax.dot_general(
        left_side, right_side, (((0,), (0,)), ((), ())), preferred_element_type=jnp.float32
    )


def matmul_nt(left_side, right_side):
    return lax.dot_general(
        left_side, right_side, (((1,), (1,)), ((), ())), preferred_element_type=jnp.float32
    )


def masked_scores(
    query_nope, query_rope, key_nope, key_rope, key_start, query_pos, prefix_end, score_scale
):
    front_part = jnp.einsum(
        "qhd,khd->hqk", query_nope, key_nope, preferred_element_type=jnp.float32
    )
    back_part = jnp.einsum("qhd,kd->hqk", query_rope, key_rope, preferred_element_type=jnp.float32)
    raw_scores = (front_part + back_part) * score_scale
    key_pos = key_start + jnp.arange(key_nope.shape[0], dtype=jnp.int32)
    seen = (key_pos[None, :] <= query_pos[:, None]) | (key_pos[None, :] < prefix_end)
    return jnp.where(seen[None], raw_scores, MASKED)


def needed_block(key_start, query_pos, prefix_end):
    return (key_start <= query_pos[-1]) | (key_start < prefix_end)


def attend_stats(query_nope, query_rope, key_blocks, query_pos, prefix_end, score_scale):
    row_count = query_nope.shape[0]
    nope_blocks, value_blocks, rope_blocks, block_starts = key_blocks

    def block_step(running, block_item):
        key_nope, key_rope, key_start = block_item

        def compute_block(current):
            running_top, running_sum = current
            block_scores = masked_scores(
                query_nope,
                query_rope,
                key_nope,
                key_rope,
                key_start,
                query_pos,
                prefix_end,
                score_scale,
            )
            new_top = jnp.maximum(running_top, jnp.max(block_scores, axis=-1))
            new_sum = running_sum * jnp.exp(running_top - new_top) + jnp.sum(
                jnp.exp(block_scores - new_top[..., None]), axis=-1
            )
            return (new_top, new_sum)

        def skip_block(current):
            return current

        return (
            lax.cond(
                needed_block(key_start, query_pos, prefix_end), compute_block, skip_block, running
            ),
            None,
        )

    initial = (
        jnp.full((H, row_count), MASKED, jnp.float32),
        jnp.zeros((H, row_count), jnp.float32),
    )
    (final_top, final_sum), _ = lax.scan(
        block_step, initial, (nope_blocks, rope_blocks, block_starts)
    )
    return final_top + jnp.log(final_sum)


def attend_values(
    query_nope, query_rope, key_blocks, query_pos, prefix_end, score_scale, log_total
):
    row_count = query_nope.shape[0]

    def block_step(running, block_item):
        key_nope, key_value, key_rope, key_start = block_item

        def compute_block(current):
            block_scores = masked_scores(
                query_nope,
                query_rope,
                key_nope,
                key_rope,
                key_start,
                query_pos,
                prefix_end,
                score_scale,
            )
            weights = jnp.exp(block_scores - log_total[..., None]).astype(jnp.bfloat16)
            return current + jnp.einsum(
                "hqk,khd->qhd", weights, key_value, preferred_element_type=jnp.float32
            )

        def skip_block(current):
            return current

        return (
            lax.cond(
                needed_block(key_start, query_pos, prefix_end), compute_block, skip_block, running
            ),
            None,
        )

    initial = jnp.zeros((row_count, H, DV), jnp.float32)
    result, _ = lax.scan(block_step, initial, key_blocks)
    return result


def attend_grads(
    query_nope,
    query_rope,
    key_blocks,
    query_pos,
    prefix_end,
    score_scale,
    log_total,
    grad_out,
    row_delta,
):
    row_count = query_nope.shape[0]
    key_span = key_blocks[0].shape[1]

    def block_step(running, block_item):
        key_nope, key_value, key_rope, key_start = block_item

        def compute_block(current):
            grad_nope, grad_rope = current
            block_scores = masked_scores(
                query_nope,
                query_rope,
                key_nope,
                key_rope,
                key_start,
                query_pos,
                prefix_end,
                score_scale,
            )
            attn_probs = jnp.exp(block_scores - log_total[..., None])
            prob_grad = jnp.einsum(
                "qhd,khd->hqk", grad_out, key_value, preferred_element_type=jnp.float32
            )
            dscore = (attn_probs * (prob_grad - row_delta[..., None])).astype(jnp.bfloat16)
            grad_nope = grad_nope + score_scale * jnp.einsum(
                "hqk,khd->qhd", dscore, key_nope, preferred_element_type=jnp.float32
            )
            grad_rope = grad_rope + score_scale * jnp.einsum(
                "hqk,kd->qhd", dscore, key_rope, preferred_element_type=jnp.float32
            )
            key_grad = score_scale * jnp.einsum(
                "hqk,qhd->khd", dscore, query_nope, preferred_element_type=jnp.float32
            )
            rope_grad = score_scale * jnp.einsum(
                "hqk,qhd->kd", dscore, query_rope, preferred_element_type=jnp.float32
            )
            value_grad = jnp.einsum(
                "hqk,qhd->khd",
                attn_probs.astype(jnp.bfloat16),
                grad_out,
                preferred_element_type=jnp.float32,
            )
            return ((grad_nope, grad_rope), (key_grad, value_grad, rope_grad))

        def skip_block(current):
            empty_terms = (
                jnp.zeros((key_span, H, DN), jnp.float32),
                jnp.zeros((key_span, H, DV), jnp.float32),
                jnp.zeros((key_span, DR), jnp.float32),
            )
            return (current, empty_terms)

        return lax.cond(
            needed_block(key_start, query_pos, prefix_end), compute_block, skip_block, running
        )

    initial = (
        jnp.zeros((row_count, H, DN), jnp.float32),
        jnp.zeros((row_count, H, DR), jnp.float32),
    )
    return lax.scan(block_step, initial, key_blocks)


def split_blocks(key_parts, key_span):
    nope_all, value_all, rope_all = key_parts
    block_count = nope_all.shape[0] // key_span
    block_starts = jnp.arange(block_count, dtype=jnp.int32) * key_span
    return (
        nope_all.reshape(block_count, key_span, H, DN),
        value_all.reshape(block_count, key_span, H, DV),
        rope_all.reshape(block_count, key_span, DR),
        block_starts,
    )


def body(
    tokens,
    cotangent,
    prefix,
    routes,
    norm1_gain,
    w_query,
    w_kv_down,
    kv_gain,
    w_kv_up,
    w_out,
    norm2_gain,
    w_router,
    shared_in,
    shared_out,
    expert_in,
    expert_out,
):
    row_count = tokens.shape[0]
    topk_count = routes.shape[1]
    groups = lax.axis_size("expert")
    owned = expert_in.shape[0]
    expert_count = owned * groups
    capacity = 3 * row_count * topk_count // (2 * expert_count)
    score_scale = float(DN + DR) ** (-0.5)
    my_index = lax.axis_index("expert")
    query_pos = my_index * row_count + jnp.arange(row_count, dtype=jnp.int32)
    prefix_end = prefix[0]
    cosine, sine_table = tables(query_pos, DR // 2)
    key_span = 4 * row_count
    mixer_parts = (
        lax.all_gather(norm1_gain, "expert", axis=0, tiled=True),
        lax.all_gather(w_query, "expert", axis=0, tiled=True),
        lax.all_gather(w_kv_down, "expert", axis=0, tiled=True),
        lax.all_gather(kv_gain, "expert", axis=0, tiled=True),
        lax.all_gather(w_kv_up, "expert", axis=0, tiled=True),
        lax.all_gather(w_out, "expert", axis=0, tiled=True),
        lax.all_gather(norm2_gain, "expert", axis=0, tiled=True),
        lax.all_gather(w_router, "expert", axis=0, tiled=True),
        lax.all_gather(shared_in, "expert", axis=0, tiled=True),
        lax.all_gather(shared_out, "expert", axis=0, tiled=True),
    )
    (
        gain_one,
        query_w,
        kv_down_w,
        kv_gain_w,
        kv_up_w,
        out_w,
        gain_two,
        router_w,
        shared_in_w,
        shared_out_w,
    ) = mixer_parts
    values = tokens.astype(jnp.float32)
    normed = rms_norm(values, gain_one.astype(jnp.float32))
    normed_b = normed.astype(jnp.bfloat16)
    query_raw = matmul(normed_b, query_w).reshape(row_count, H, DN + DR)
    query_nope = query_raw[..., :DN].astype(jnp.bfloat16)
    query_rope = rotate(query_raw[..., DN:], cosine[:, None, :], sine_table[:, None, :]).astype(
        jnp.bfloat16
    )
    kv_down = matmul(normed_b, kv_down_w)
    latent = kv_down[:, :KVR]
    latent_b = rms_norm(latent, kv_gain_w.astype(jnp.float32)).astype(jnp.bfloat16)
    key_rope_b = rotate(kv_down[:, KVR:], cosine, sine_table).astype(jnp.bfloat16)
    kv_up = matmul(latent_b, kv_up_w).astype(jnp.bfloat16).reshape(row_count, H, DN + DV)
    local_nope = kv_up[..., :DN].reshape(row_count, H * DN)
    local_value = kv_up[..., DN:].reshape(row_count, H * DV)
    key_parts = (
        lax.all_gather(local_nope, "expert", axis=0, tiled=True),
        lax.all_gather(local_value, "expert", axis=0, tiled=True),
        lax.all_gather(key_rope_b, "expert", axis=0, tiled=True),
    )
    key_blocks = split_blocks(key_parts, key_span)
    log_total = attend_stats(query_nope, query_rope, key_blocks, query_pos, prefix_end, score_scale)
    attn_full = attend_values(
        query_nope, query_rope, key_blocks, query_pos, prefix_end, score_scale, log_total
    )
    mixed_b = attn_full.astype(jnp.bfloat16).reshape(row_count, H * DV)
    middle = values + matmul(mixed_b, out_w)
    gain_two_f = gain_two.astype(jnp.float32)
    normed_two_b = rms_norm(middle, gain_two_f).astype(jnp.bfloat16)
    router_probs = jax.nn.softmax(matmul(normed_two_b, router_w), axis=-1)
    one_hot = routes[:, :, None] == jnp.arange(expert_count, dtype=jnp.int32)[None, None, :]
    route_gates = jnp.sum(jnp.where(one_hot, router_probs[:, None, :], 0.0), axis=-1)
    shared_join = matmul(normed_two_b, shared_in_w)
    shared_hidden_b = swiglu(shared_join).astype(jnp.bfloat16)
    shared = matmul(shared_hidden_b, shared_out_w)
    expert_ids = routes.reshape(-1)
    id_hot = (expert_ids[:, None] == jnp.arange(expert_count, dtype=jnp.int32)[None, :]).astype(
        jnp.int32
    )
    slot_index = jnp.sum((jnp.cumsum(id_hot, axis=0) - id_hot) * id_hot, axis=1)
    slot_place = (expert_ids % owned * groups + expert_ids // owned) * capacity + slot_index
    buffer_rows = owned * groups * capacity
    filled = (
        jnp.zeros((buffer_rows, D), jnp.bfloat16)
        .at[slot_place]
        .set(jnp.repeat(normed_two_b, topk_count, axis=0))
    )
    received = lax.all_to_all(
        filled.reshape(owned, groups, capacity, D),
        "expert",
        split_axis=1,
        concat_axis=1,
        tiled=True,
    )
    expert_rows = received.reshape(owned, groups * capacity, D)
    expert_parts = (
        lax.all_gather(expert_in, "dp", axis=1, tiled=True),
        lax.all_gather(expert_out, "dp", axis=2, tiled=True),
    )
    first_w, second_w = expert_parts
    joined = jnp.einsum("erd,edf->erf", expert_rows, first_w, preferred_element_type=jnp.float32)
    hidden_b = swiglu(joined).astype(jnp.bfloat16)
    result_b = jnp.einsum(
        "erf,efd->erd", hidden_b, second_w, preferred_element_type=jnp.float32
    ).astype(jnp.bfloat16)
    returned = lax.all_to_all(
        result_b.reshape(owned, groups, capacity, D),
        "expert",
        split_axis=1,
        concat_axis=1,
        tiled=True,
    )
    picked = (
        returned.reshape(buffer_rows, D)[slot_place]
        .reshape(row_count, topk_count, D)
        .astype(jnp.float32)
    )
    routed = jnp.sum(route_gates[:, :, None] * picked, axis=1)
    out = (middle + shared + routed).astype(jnp.bfloat16)
    back_parts = (
        lax.all_gather(norm1_gain, "expert", axis=0, tiled=True),
        lax.all_gather(w_query, "expert", axis=0, tiled=True),
        lax.all_gather(w_kv_down, "expert", axis=0, tiled=True),
        lax.all_gather(kv_gain, "expert", axis=0, tiled=True),
        lax.all_gather(w_kv_up, "expert", axis=0, tiled=True),
        lax.all_gather(w_out, "expert", axis=0, tiled=True),
        lax.all_gather(norm2_gain, "expert", axis=0, tiled=True),
        lax.all_gather(w_router, "expert", axis=0, tiled=True),
        lax.all_gather(shared_in, "expert", axis=0, tiled=True),
        lax.all_gather(shared_out, "expert", axis=0, tiled=True),
    )
    back_keys = (
        lax.all_gather(local_nope, "expert", axis=0, tiled=True),
        lax.all_gather(local_value, "expert", axis=0, tiled=True),
        lax.all_gather(key_rope_b, "expert", axis=0, tiled=True),
    )
    back_blocks = split_blocks(back_keys, key_span)
    (
        gain_one_back,
        query_back,
        kv_down_back,
        kv_gain_back,
        kv_up_back,
        out_back,
        gain_two_back,
        router_back,
        shared_in_back,
        shared_out_back,
    ) = back_parts
    out_grad = cotangent.astype(jnp.float32)
    gate_grad = jnp.sum(out_grad[:, None, :] * picked, axis=2)
    result_grad = (route_gates[:, :, None] * out_grad[:, None, :]).astype(jnp.bfloat16)
    sent = jnp.zeros((buffer_rows, D), jnp.bfloat16).at[slot_place].set(result_grad.reshape(-1, D))
    owner_grad = lax.all_to_all(
        sent.reshape(owned, groups, capacity, D), "expert", split_axis=1, concat_axis=1, tiled=True
    ).reshape(owned, groups * capacity, D)
    hidden_grad = jnp.einsum(
        "erd,efd->erf", owner_grad, second_w, preferred_element_type=jnp.float32
    )
    _, pull_expert = jax.vjp(swiglu, joined)
    joined_grad = pull_expert(hidden_grad)[0].astype(jnp.bfloat16)
    grad_second = jnp.einsum(
        "erf,erd->efd", hidden_b, owner_grad, preferred_element_type=jnp.float32
    )
    grad_first = jnp.einsum(
        "erd,erf->edf", expert_rows, joined_grad, preferred_element_type=jnp.float32
    )
    rows_grad = jnp.einsum("erf,edf->erd", joined_grad, first_w, preferred_element_type=jnp.float32)
    sent_back = lax.all_to_all(
        rows_grad.reshape(owned, groups, capacity, D).astype(jnp.bfloat16),
        "expert",
        split_axis=1,
        concat_axis=1,
        tiled=True,
    ).astype(jnp.float32)
    route_grad = jnp.sum(
        sent_back.reshape(buffer_rows, D)[slot_place].reshape(row_count, topk_count, D), axis=1
    )
    expert_grads = (
        lax.psum_scatter(
            grad_first.astype(jnp.bfloat16), "dp", scatter_dimension=1, tiled=True
        ).astype(jnp.float32),
        lax.psum_scatter(
            grad_second.astype(jnp.bfloat16), "dp", scatter_dimension=2, tiled=True
        ).astype(jnp.float32),
    )
    probs_grad = jnp.sum(jnp.where(one_hot, gate_grad[:, :, None], 0.0), axis=1)
    logit_grad = (
        router_probs * (probs_grad - jnp.sum(router_probs * probs_grad, axis=-1, keepdims=True))
    ).astype(jnp.bfloat16)
    out_grad_b = out_grad.astype(jnp.bfloat16)
    shared_hidden_grad = matmul_nt(out_grad_b, shared_out_back)
    _, pull_shared = jax.vjp(swiglu, shared_join)
    shared_join_grad = pull_shared(shared_hidden_grad)[0].astype(jnp.bfloat16)
    grad_router = matmul_tn(normed_two_b, logit_grad)
    grad_shared_in = matmul_tn(normed_two_b, shared_join_grad)
    grad_shared_out = matmul_tn(shared_hidden_b, out_grad_b)
    normed_two_grad = (
        route_grad
        + matmul_nt(logit_grad, router_back)
        + matmul_nt(shared_join_grad, shared_in_back)
    )
    _, pull_norm_two = jax.vjp(rms_norm, middle, gain_two_back.astype(jnp.float32))
    middle_part, grad_gain_two = pull_norm_two(normed_two_grad)
    ffn_grads = (
        lax.psum_scatter(
            grad_gain_two.astype(jnp.bfloat16), "expert", scatter_dimension=0, tiled=True
        ).astype(jnp.float32),
        lax.psum_scatter(
            grad_router.astype(jnp.bfloat16), "expert", scatter_dimension=0, tiled=True
        ).astype(jnp.float32),
        lax.psum_scatter(
            grad_shared_in.astype(jnp.bfloat16), "expert", scatter_dimension=0, tiled=True
        ).astype(jnp.float32),
        lax.psum_scatter(
            grad_shared_out.astype(jnp.bfloat16), "expert", scatter_dimension=0, tiled=True
        ).astype(jnp.float32),
    )
    middle_grad = out_grad + middle_part
    middle_grad_b = middle_grad.astype(jnp.bfloat16)
    grad_out_w = matmul_tn(mixed_b, middle_grad_b)
    attn_grad_b = matmul_nt(middle_grad_b, out_back).reshape(row_count, H, DV).astype(jnp.bfloat16)
    row_delta = jnp.sum(attn_grad_b.astype(jnp.float32) * attn_full, axis=-1).T
    (query_nope_grad, query_rope_grad), key_terms = attend_grads(
        query_nope,
        query_rope,
        back_blocks,
        query_pos,
        prefix_end,
        score_scale,
        log_total,
        attn_grad_b,
        row_delta,
    )
    key_grad_all, value_grad_all, rope_grad_all = key_terms
    key_sums = (
        lax.psum_scatter(
            key_grad_all.reshape(-1, H * DN).astype(jnp.bfloat16),
            "expert",
            scatter_dimension=0,
            tiled=True,
        ).astype(jnp.float32),
        lax.psum_scatter(
            value_grad_all.reshape(-1, H * DV).astype(jnp.bfloat16),
            "expert",
            scatter_dimension=0,
            tiled=True,
        ).astype(jnp.float32),
        lax.psum_scatter(
            rope_grad_all.reshape(-1, DR).astype(jnp.bfloat16),
            "expert",
            scatter_dimension=0,
            tiled=True,
        ).astype(jnp.float32),
    )
    nope_sum, value_sum, rope_sum = key_sums
    kv_up_grad = (
        jnp.concatenate(
            [nope_sum.reshape(row_count, H, DN), value_sum.reshape(row_count, H, DV)], axis=-1
        )
        .reshape(row_count, H * (DN + DV))
        .astype(jnp.bfloat16)
    )
    grad_kv_up = matmul_tn(latent_b, kv_up_grad)
    latent_upstream = matmul_nt(kv_up_grad, kv_up_back)
    _, pull_latent = jax.vjp(rms_norm, latent, kv_gain_back.astype(jnp.float32))
    latent_grad, grad_kv_gain = pull_latent(latent_upstream)
    _, pull_key_rope = jax.vjp(
        lambda rope_part: rotate(rope_part, cosine, sine_table), kv_down[:, KVR:]
    )
    kv_down_grad = jnp.concatenate([latent_grad, pull_key_rope(rope_sum)[0]], axis=1).astype(
        jnp.bfloat16
    )
    grad_kv_down = matmul_tn(normed_b, kv_down_grad)
    _, pull_query_rope = jax.vjp(
        lambda rope_part: rotate(rope_part, cosine[:, None, :], sine_table[:, None, :]),
        query_raw[..., DN:],
    )
    query_grad = (
        jnp.concatenate([query_nope_grad, pull_query_rope(query_rope_grad)[0]], axis=-1)
        .reshape(row_count, H * (DN + DR))
        .astype(jnp.bfloat16)
    )
    grad_query = matmul_tn(normed_b, query_grad)
    normed_grad = matmul_nt(query_grad, query_back) + matmul_nt(kv_down_grad, kv_down_back)
    _, pull_norm_one = jax.vjp(rms_norm, values, gain_one_back.astype(jnp.float32))
    input_part, grad_gain_one = pull_norm_one(normed_grad)
    grad_tokens = middle_grad + input_part
    attn_grads = (
        lax.psum_scatter(
            grad_gain_one.astype(jnp.bfloat16), "expert", scatter_dimension=0, tiled=True
        ).astype(jnp.float32),
        lax.psum_scatter(
            grad_query.astype(jnp.bfloat16), "expert", scatter_dimension=0, tiled=True
        ).astype(jnp.float32),
        lax.psum_scatter(
            grad_kv_down.astype(jnp.bfloat16), "expert", scatter_dimension=0, tiled=True
        ).astype(jnp.float32),
        lax.psum_scatter(
            grad_kv_gain.astype(jnp.bfloat16), "expert", scatter_dimension=0, tiled=True
        ).astype(jnp.float32),
        lax.psum_scatter(
            grad_kv_up.astype(jnp.bfloat16), "expert", scatter_dimension=0, tiled=True
        ).astype(jnp.float32),
        lax.psum_scatter(
            grad_out_w.astype(jnp.bfloat16), "expert", scatter_dimension=0, tiled=True
        ).astype(jnp.float32),
    )
    summed = (
        lax.psum(attn_grads[0].astype(jnp.bfloat16), "dp").astype(jnp.float32),
        lax.psum(attn_grads[1].astype(jnp.bfloat16), "dp").astype(jnp.float32),
        lax.psum(attn_grads[2].astype(jnp.bfloat16), "dp").astype(jnp.float32),
        lax.psum(attn_grads[3].astype(jnp.bfloat16), "dp").astype(jnp.float32),
        lax.psum(attn_grads[4].astype(jnp.bfloat16), "dp").astype(jnp.float32),
        lax.psum(attn_grads[5].astype(jnp.bfloat16), "dp").astype(jnp.float32),
        lax.psum(ffn_grads[0].astype(jnp.bfloat16), "dp").astype(jnp.float32),
        lax.psum(ffn_grads[1].astype(jnp.bfloat16), "dp").astype(jnp.float32),
        lax.psum(ffn_grads[2].astype(jnp.bfloat16), "dp").astype(jnp.float32),
        lax.psum(ffn_grads[3].astype(jnp.bfloat16), "dp").astype(jnp.float32),
    )
    return (
        out,
        grad_tokens,
        summed[0],
        summed[1],
        summed[2],
        summed[3],
        summed[4],
        summed[5],
        summed[6],
        summed[7],
        summed[8],
        summed[9],
        expert_grads[0],
        expert_grads[1],
    )


def visible_scores(query, key, first_row, prefix_end, scale):
    scores = scale * lax.dot_general(
        query, key, (((1,), (1,)), ((), ())), preferred_element_type=jnp.float32
    )
    row = first_row + lax.broadcasted_iota(jnp.int32, scores.shape, 0)
    column = lax.broadcasted_iota(jnp.int32, scores.shape, 1)
    return jnp.where((column <= row) | (column < prefix_end), scores, MASKED)


def head_operands(heads, head, query, key_rope, kv_up):
    at = head * (DN + DV)
    rope = heads * DN + head * DR
    query_h = jnp.concatenate(
        [query[:, head * DN : (head + 1) * DN], query[:, rope : rope + DR]], axis=1
    )
    key_h = jnp.concatenate([kv_up[:, at : at + DN], key_rope], axis=1)
    return query_h, key_h, kv_up[:, at + DN : at + DN + DV]


def attend_kernel(heads, scale, prefix_ref, query_ref, key_rope_ref, kv_up_ref, mixed_ref):
    tile = query_ref.shape[0]
    first_row = pl.program_id(0) * tile
    query, key_rope, kv_up = query_ref[...], key_rope_ref[...], kv_up_ref[...]
    for head in range(heads):
        query_h, key_h, value_h = head_operands(heads, head, query, key_rope, kv_up)
        scores = visible_scores(query_h, key_h, first_row, prefix_ref[0], scale)
        powers = jnp.exp(scores - jnp.max(scores, axis=1, keepdims=True))
        probs = powers * (1.0 / jnp.sum(powers, axis=1, keepdims=True))
        mixed_ref[:, head * DV : (head + 1) * DV] = jnp.dot(
            probs.astype(jnp.bfloat16), value_h, preferred_element_type=jnp.float32
        ).astype(jnp.bfloat16)


def attend_back_kernel(
    heads, scale, prefix_ref, query_ref, grad_ref, key_rope_ref, kv_up_ref,
    query_nope_ref, query_rope_ref, kv_grad_ref, rope_grad_ref, key_total, value_total,
):
    step = pl.program_id(0)
    tile = query_ref.shape[0]

    @pl.when(step == 0)
    def _():
        key_total[...] = jnp.zeros_like(key_total)
        value_total[...] = jnp.zeros_like(value_total)

    query, key_rope, kv_up = query_ref[...], key_rope_ref[...], kv_up_ref[...]
    tn = (((0,), (0,)), ((), ()))
    for head in range(heads):
        query_h, key_h, value_h = head_operands(heads, head, query, key_rope, kv_up)
        grad_h = grad_ref[:, head * DV : (head + 1) * DV]
        scores = visible_scores(query_h, key_h, step * tile, prefix_ref[0], scale)
        powers = jnp.exp(scores - jnp.max(scores, axis=1, keepdims=True))
        probs = powers * (1.0 / jnp.sum(powers, axis=1, keepdims=True))
        prob_grad = lax.dot_general(
            grad_h, value_h, (((1,), (1,)), ((), ())), preferred_element_type=jnp.float32
        )
        delta = jnp.sum(probs * prob_grad, axis=1, keepdims=True)
        dscore = (probs * (prob_grad - delta)).astype(jnp.bfloat16)
        query_grad = scale * jnp.dot(dscore, key_h, preferred_element_type=jnp.float32)
        query_nope_ref[:, head * DN : (head + 1) * DN] = query_grad[:, :DN].astype(jnp.bfloat16)
        query_rope_ref[:, head * DR : (head + 1) * DR] = query_grad[:, DN:]
        key_total[head] += lax.dot_general(dscore, query_h, tn, preferred_element_type=jnp.float32)
        value_total[head] += lax.dot_general(
            probs.astype(jnp.bfloat16), grad_h, tn, preferred_element_type=jnp.float32
        )

    @pl.when(step == pl.num_programs(0) - 1)
    def _():
        rope = jnp.zeros(rope_grad_ref.shape, jnp.float32)
        for head in range(heads):
            at = head * (DN + DV)
            total = scale * key_total[head]
            kv_grad_ref[:, at : at + DN] = total[:, :DN].astype(jnp.bfloat16)
            kv_grad_ref[:, at + DN : at + DN + DV] = value_total[head].astype(jnp.bfloat16)
            rope += total[:, DN:]
        rope_grad_ref[...] = rope


def attend(prefix, query, key_rope, kv_up, heads, scale):
    length = query.shape[0]
    tile = min(256, length)
    whole = lambda value: pl.BlockSpec(value.shape, lambda i: (0, 0))
    rows = lambda width: pl.BlockSpec((tile, width), lambda i: (i, 0))
    return pl.pallas_call(
        functools.partial(attend_kernel, heads, scale),
        grid=(length // tile,),
        out_shape=jax.ShapeDtypeStruct((length, heads * DV), jnp.bfloat16),
        in_specs=[pl.BlockSpec(memory_space=pltpu.SMEM), rows(query.shape[1]), whole(key_rope), whole(kv_up)],
        out_specs=rows(heads * DV),
        compiler_params=pltpu.CompilerParams(vmem_limit_bytes=48 * 1024 * 1024),
        cost_estimate=pl.CostEstimate(
            flops=2 * heads * length * length * (DN + DR + DV),
            transcendentals=heads * length * length,
            bytes_accessed=2 * length * heads * (DN + DR + DN + DV + DV),
        ),
        name="attend",
    )(prefix, query, key_rope, kv_up)


def attend_back(prefix, query, grad, key_rope, kv_up, heads, scale):
    length = query.shape[0]
    tile = min(256, length)
    whole = lambda shape: pl.BlockSpec(shape, lambda i: (0, 0))
    rows = lambda width: pl.BlockSpec((tile, width), lambda i: (i, 0))
    return pl.pallas_call(
        functools.partial(attend_back_kernel, heads, scale),
        grid=(length // tile,),
        out_shape=[
            jax.ShapeDtypeStruct((length, heads * DN), jnp.bfloat16),
            jax.ShapeDtypeStruct((length, heads * DR), jnp.float32),
            jax.ShapeDtypeStruct(kv_up.shape, jnp.bfloat16),
            jax.ShapeDtypeStruct(key_rope.shape, jnp.float32),
        ],
        in_specs=[
            pl.BlockSpec(memory_space=pltpu.SMEM),
            rows(query.shape[1]),
            rows(grad.shape[1]),
            whole(key_rope.shape),
            whole(kv_up.shape),
        ],
        out_specs=[rows(heads * DN), rows(heads * DR), whole(kv_up.shape), whole(key_rope.shape)],
        scratch_shapes=[
            pltpu.VMEM((heads, length, DN + DR), jnp.float32),
            pltpu.VMEM((heads, length, DV), jnp.float32),
        ],
        compiler_params=pltpu.CompilerParams(vmem_limit_bytes=48 * 1024 * 1024),
        cost_estimate=pl.CostEstimate(
            flops=40 * heads * length * length * 3 * (DN + DR + DV),
            transcendentals=heads * length * length,
            bytes_accessed=2 * length * heads * 3 * (DN + DR + DN + DV + DV),
        ),
        name="attend_back",
    )(prefix, query, grad, key_rope, kv_up)


def expert_kernel(expert_count, spot, *refs):
    x_in, g_in = refs[0:4], refs[4:8]
    first_in, second_in, router = refs[8:10], refs[10:12], refs[12]
    back_out = refs[13:17]
    hidden_out, grads_out, rows_out, grad_rows_out, second_out, logit_out = refs[17:23]
    first_w, second_w, x_buf, g_buf, back_st, hidden_st, grads_st, in_sem, w_sem, out_sem, keep_sem = refs[23:]
    lane, core, expert = spot[0], spot[1], spot[2]
    lanes = len(x_in)
    rows = x_buf.shape[1]
    depth, half = first_w.shape[1], first_w.shape[2]
    slab = depth // lanes
    side = half // 2

    loads = []
    for step in range(lanes):
        loads.append(
            (
                pltpu.make_async_copy(x_in[step], x_buf.at[step], in_sem.at[0, step]),
                pltpu.make_async_copy(g_in[step], g_buf.at[step], in_sem.at[1, step]),
            )
        )
    first_loads, second_loads = [], []
    for part in range(2):
        slot = core if part == 0 else 1 - core
        for step in range(lanes):
            at = pl.multiple_of((lane ^ step) * slab, slab)
            first_loads.append(
                pltpu.make_async_copy(
                    first_in[part].at[pl.ds(step * slab, slab), :], first_w.at[slot, pl.ds(at, slab), :], w_sem.at[0, part, step]
                )
            )
            second_loads.append(
                pltpu.make_async_copy(
                    second_in[part].at[pl.ds(step * side, side), :],
                    second_w.at[pl.ds(pl.multiple_of(slot * side, side), side), pl.ds(at, slab)],
                    w_sem.at[1, part, step],
                )
            )
    loads[0][0].start()
    for copy in first_loads:
        copy.start()
    loads[0][1].start()
    for copy in second_loads:
        copy.start()
    for step in range(1, lanes):
        loads[step][0].start()
        loads[step][1].start()

    def kept(step):
        where = pl.ds(step * rows, rows)
        return [
            pltpu.make_async_copy(x_buf.at[step], rows_out.at[where, :], keep_sem.at[step]),
            pltpu.make_async_copy(g_buf.at[step], grad_rows_out.at[where, :], keep_sem.at[lanes + step]),
        ]

    second_kept = pltpu.make_async_copy(second_w, second_out, keep_sem.at[2 * lanes])

    def stores(step, slot, back):
        where = pl.ds(pl.multiple_of(step * rows, rows), rows)
        return [
            pltpu.make_async_copy(back_st.at[slot], back, out_sem.at[slot, 0]),
            pltpu.make_async_copy(hidden_st.at[slot], hidden_out.at[where, :], out_sem.at[slot, 1]),
            pltpu.make_async_copy(grads_st.at[slot, 0], grads_out.at[0, where, :], out_sem.at[slot, 2]),
            pltpu.make_async_copy(grads_st.at[slot, 1], grads_out.at[1, where, :], out_sem.at[slot, 3]),
        ]

    nt = (((1,), (1,)), ((), ()))

    def compute(step, slot):
        x = x_buf[step]
        a = jnp.dot(x, first_w[0], preferred_element_type=jnp.float32)
        b = jnp.dot(x, first_w[1], preferred_element_type=jnp.float32)
        logits = jnp.dot(x, router[...], preferred_element_type=jnp.float32)
        column = lax.broadcasted_iota(jnp.int32, logits.shape, 1)
        logits = jnp.where(column < expert_count, logits, -1e30)
        top = jnp.max(logits, axis=1, keepdims=True)
        powers = jnp.exp(logits - top)
        probs = powers / jnp.sum(powers, axis=1, keepdims=True)
        hot = (column == expert).astype(jnp.float32)
        gate = jnp.sum(probs * hot, axis=1, keepdims=True)
        g = g_buf[step]
        up = lax.dot_general(g, second_w[...], nt, preferred_element_type=jnp.float32)
        sig = 1.0 / (1.0 + jnp.exp(-a))
        act = a * sig
        hidden = act * b
        hidden_st[slot] = (gate * hidden).astype(jnp.bfloat16)
        gate_grad = jnp.sum(up * hidden, axis=1, keepdims=True)
        up = up * gate
        grad_b = (up * act).astype(jnp.bfloat16)
        grad_a = (up * b * (sig + act * (1.0 - sig))).astype(jnp.bfloat16)
        grads_st[slot, core] = grad_a
        grads_st[slot, 1 - core] = grad_b
        logit = (gate * gate_grad * (hot - probs)).astype(jnp.bfloat16)
        logit_out[pl.ds(pl.multiple_of(step * rows, rows), rows), :] = logit
        back = lax.dot_general(grad_a, first_w[0], nt, preferred_element_type=jnp.float32)
        back += lax.dot_general(grad_b, first_w[1], nt, preferred_element_type=jnp.float32)
        back += lax.dot_general(logit, router[...], nt, preferred_element_type=jnp.float32)
        back_st[slot] = back.astype(jnp.bfloat16)

    for copy in first_loads + second_loads:
        copy.wait()
    second_kept.start()

    def body_step(step, carry):
        slot = lax.rem(step, 2)
        for i in range(lanes):

            @pl.when(step == i)
            def _():
                loads[i][0].wait()
                loads[i][1].wait()
                for copy in kept(i):
                    copy.start()

        for i in range(2, lanes):

            @pl.when(step == i)
            def _():
                for copy in stores(i - 2, i % 2, back_out[i - 2]):
                    copy.wait()

        compute(step, slot)
        for i in range(lanes):

            @pl.when(step == i)
            def _():
                for copy in stores(i, i % 2, back_out[i]):
                    copy.start()

        return carry

    lax.fori_loop(0, lanes, body_step, 0)
    for step in range(lanes - 2, lanes):
        for copy in stores(step, step % 2, back_out[step]):
            copy.wait()
    for step in range(lanes):
        for copy in kept(step):
            copy.wait()
    second_kept.wait()


def expert_step(spot, x_pieces, g_pieces, first_mine, first_other, second_mine, second_other, router_wide, expert_count):
    rows, depth = x_pieces[0].shape
    half = first_mine.shape[1]
    lanes = len(x_pieces)
    total = rows * lanes
    bf = jnp.bfloat16
    any_spec = pl.BlockSpec(memory_space=pl.ANY)
    vmem_spec = pl.BlockSpec(memory_space=pltpu.VMEM)
    return pl.pallas_call(
        functools.partial(expert_kernel, expert_count),
        out_shape=[jax.ShapeDtypeStruct((rows, depth), bf)] * lanes
        + [
            jax.ShapeDtypeStruct((total, half), bf),
            jax.ShapeDtypeStruct((2, total, half), bf),
            jax.ShapeDtypeStruct((total, depth), bf),
            jax.ShapeDtypeStruct((total, depth), bf),
            jax.ShapeDtypeStruct((half, depth), bf),
            jax.ShapeDtypeStruct((total, 128), bf),
        ],
        in_specs=[pl.BlockSpec(memory_space=pltpu.SMEM)] + [any_spec] * (2 * lanes + 4) + [vmem_spec],
        out_specs=[any_spec] * (lanes + 5) + [vmem_spec],
        scratch_shapes=[
            pltpu.VMEM((2, depth, half), bf),
            pltpu.VMEM((half, depth), bf),
            pltpu.VMEM((lanes, rows, depth), bf),
            pltpu.VMEM((lanes, rows, depth), bf),
            pltpu.VMEM((2, rows, depth), bf),
            pltpu.VMEM((2, rows, half), bf),
            pltpu.VMEM((2, 2, rows, half), bf),
            pltpu.SemaphoreType.DMA((2, lanes)),
            pltpu.SemaphoreType.DMA((2, 2, lanes)),
            pltpu.SemaphoreType.DMA((2, 4)),
            pltpu.SemaphoreType.DMA((2 * lanes + 1,)),
        ],
        compiler_params=pltpu.CompilerParams(vmem_limit_bytes=60 * 1024 * 1024),
        cost_estimate=pl.CostEstimate(
            flops=10 * total * depth * half,
            transcendentals=total * half,
            bytes_accessed=2 * (3 * depth * half * 2 + total * (5 * depth + 3 * half)),
        ),
        name="expert_rows",
    )(spot, *x_pieces, *g_pieces, first_mine, first_other, second_mine, second_other, router_wide)


def shared_body(
    tokens,
    cotangent,
    prefix,
    routes,
    norm1_gain,
    w_query,
    w_kv_down,
    kv_gain,
    w_kv_up,
    w_out,
    norm2_gain,
    w_router,
    shared_in,
    shared_out,
    expert_in,
    expert_out,
):
    rows = tokens.shape[0]
    topk = routes.shape[1]
    chips = lax.axis_size("z")
    lanes = lax.axis_size("dp")
    groups = chips * 2
    owned = expert_in.shape[0]
    expert_count = owned * groups
    capacity = 3 * rows * topk // (2 * expert_count)
    heads = H // groups
    length = rows * groups
    scale = float(DN + DR) ** (-0.5)
    my_dp = lax.axis_index("dp")
    my_z = lax.axis_index("z")
    my_core = lax.axis_index("core")
    my_expert = my_z * 2 * owned + my_dp
    group = ("z", "core")
    hidden_n = shared_out.shape[0]
    kv_cols = w_kv_down.shape[1]
    half = expert_in.shape[2] // 2

    def gather(value):
        return lax.all_gather(value, group, axis=0, tiled=True)

    def scatter_sum(value):
        return lax.psum_scatter(value, group, scatter_dimension=0, tiled=True)

    def fence(*values):
        return lax.optimization_barrier(values)

    def swap(value):
        return lax.ppermute(value, "core", [(0, 1), (1, 0)])

    def ordered(mine, other, axis):
        return jnp.where(
            my_core == 0,
            jnp.concatenate([mine, other], axis=axis),
            jnp.concatenate([other, mine], axis=axis),
        )

    def halves(value, axis):
        size = value.shape[axis] // 2
        mine = lax.dynamic_slice_in_dim(value, my_core * size, size, axis)
        other = lax.dynamic_slice_in_dim(value, (1 - my_core) * size, size, axis)
        return mine, other

    def exchange(value):
        return lax.all_to_all(value, group, split_axis=0, concat_axis=0, tiled=True)

    def to_lane(value, step):
        return lax.ppermute(value, "dp", [(lane, lane ^ step) for lane in range(lanes)])

    def by_lane(pieces):
        full = jnp.zeros((lanes,) + pieces[0].shape, pieces[0].dtype)
        for step in range(lanes):
            full = lax.dynamic_update_index_in_dim(full, pieces[step], my_dp ^ step, 0)
        return full

    def to_lanes(pieces):
        return [pieces[0]] + [to_lane(pieces[step], step) for step in range(1, lanes)]

    def lane_exchange(value):
        return to_lanes(
            [lax.dynamic_index_in_dim(value, my_dp ^ step, 0, keepdims=False) for step in range(lanes)]
        )

    def own_part(value):
        part = value.shape[0] // lanes
        return lax.dynamic_slice_in_dim(value, my_dp * part, part, 0).transpose(1, 0, 2)

    share = norm1_gain.shape[0]
    kv_share = kv_gain.shape[0]
    used = kv_cols + expert_count
    extra = 640 - used
    gains = jnp.concatenate([norm1_gain, norm2_gain, kv_gain])
    gain_rows = gains.shape[0] // extra
    small = jnp.concatenate(
        [
            w_kv_down,
            w_router,
            jnp.concatenate(
                [
                    jnp.pad(gains.reshape(gain_rows, extra), ((0, share - rows - gain_rows), (0, 0))),
                    jnp.pad(routes.astype(jnp.bfloat16), ((0, 0), (0, extra - topk))),
                ]
            ),
        ],
        axis=1,
    )
    query_n = heads * (DN + DR)
    kv_width = heads * (DN + DV)
    fold = share // kv_share
    query_parts = w_query.reshape(share, groups, heads, DN + DR)
    attention_parts = jnp.concatenate(
        [
            query_parts[..., :DN].reshape(share, groups, heads * DN),
            query_parts[..., DN:].reshape(share, groups, heads * DR),
            w_kv_up.reshape(kv_share, groups, fold, kv_width // fold)
            .transpose(0, 2, 1, 3)
            .reshape(share, groups, kv_width // fold),
        ],
        axis=2,
    )
    shared_parts = own_part(
        shared_in.reshape(share, 2, groups, hidden_n)
        .transpose(0, 2, 1, 3)
        .reshape(share, groups, 2 * hidden_n)
    )
    tokens_all = gather(tokens)
    small_all = gather(small)
    attention_moved = exchange(own_part(attention_parts))
    attention_pieces = to_lanes([attention_moved] * lanes)
    def lane_pieces(value, axis):
        keep, give = halves(value, axis)
        received = swap(give)
        pieces = []
        for step in range(lanes):
            lane = my_dp ^ step
            pieces.append(
                jnp.where(
                    lane // 2 == my_core,
                    lax.dynamic_index_in_dim(keep, lane % 2, 0, keepdims=False),
                    lax.dynamic_index_in_dim(received, lane % 2, 0, keepdims=False),
                )
            )
        return pieces

    first_pieces = to_lanes(lane_pieces(expert_in, 2))
    second_sources = lane_pieces(expert_out, 1)

    tokens_all, small_all, attention_pieces, first_pieces[:2], second_sources, shared_parts = fence(
        tokens_all, small_all, attention_pieces, first_pieces[:2], second_sources, shared_parts
    )
    shared_moved = exchange(shared_parts)
    grad_all = gather(cotangent)
    second_pieces = to_lanes(second_sources)
    spare = small_all[:, used:].reshape(chips, 2, share, extra)
    routes_mine = lax.dynamic_index_in_dim(
        spare[:, :, share - rows :, :topk], my_core, axis=1, keepdims=False
    ).astype(jnp.int32)

    router_w = small_all[:, kv_cols:used]
    gains_all = (
        spare.reshape(groups, share, extra)[:, :gain_rows].reshape(groups, gain_rows * extra)
    ).astype(jnp.float32)
    gain_one = gains_all[:, :share].reshape(-1)
    gain_two = gains_all[:, share : 2 * share].reshape(-1)
    gain_kv = gains_all[:, 2 * share :].reshape(-1)
    kv_down_w = small_all[:, :kv_cols]
    attention_w = by_lane(attention_pieces).transpose(1, 0, 2, 3)
    query_w = attention_w[..., :query_n].reshape(share * groups, query_n)
    kv_up_w = attention_w[..., query_n:].reshape(kv_share * groups, kv_width)

    plane = my_z * 2 * owned + (my_dp ^ jnp.arange(lanes, dtype=jnp.int32))
    member = jnp.any(routes_mine[:, :, :, None] == plane[None, None, None, :], axis=2)
    earlier = (jnp.arange(rows)[:, None] > jnp.arange(rows)[None, :]).astype(jnp.float32)
    place = jnp.einsum(
        "st,ztq->zqs", earlier, member.astype(jnp.float32), precision=lax.Precision.HIGHEST
    )
    slots = jnp.arange(capacity, dtype=jnp.float32)
    pick = (
        (place[:, :, None, :] == slots[None, None, :, None]) & member.transpose(0, 2, 1)[:, :, None, :]
    ).astype(jnp.bfloat16)

    def picked(blocks):
        return [
            jnp.einsum(
                "zst,ztd->zsd", pick[:, step], blocks, preferred_element_type=jnp.float32
            ).astype(jnp.bfloat16)
            for step in range(lanes)
        ]

    def split_rows(value):
        pieces = value.reshape(lanes, chips, capacity, D)
        return [pieces[step] for step in range(lanes)]

    def placed(pieces):
        return jnp.einsum(
            "zlst,zlsd->ztd", pick, jnp.stack(pieces, axis=1), preferred_element_type=jnp.float32
        )

    def my_blocks(value):
        return lax.dynamic_index_in_dim(
            value.reshape(chips, 2, rows, D), my_core, axis=1, keepdims=False
        )

    def add_mine(total, mine):
        spread = jnp.where((jnp.arange(2) == my_core)[None, :, None, None], mine[:, None], 0.0)
        return total.reshape(chips, 2, rows, D) + spread

    positions = jnp.arange(length, dtype=jnp.int32)
    cosine, sine_table = tables(positions, DR // 2)
    values_all = tokens_all.astype(jnp.float32)
    inverse_one = lax.rsqrt(jnp.mean(values_all * values_all, axis=-1, keepdims=True) + EPSILON)
    normed_b = (values_all * inverse_one * gain_one).astype(jnp.bfloat16)
    query_raw = matmul(normed_b, query_w)
    query_rope = rotate(
        query_raw[:, heads * DN :].reshape(length, heads, DR), cosine[:, None, :], sine_table[:, None, :]
    )
    query = jnp.concatenate(
        [query_raw[:, : heads * DN], query_rope.reshape(length, heads * DR)], axis=1
    ).astype(jnp.bfloat16)
    kv_down = matmul(normed_b, kv_down_w)
    latent = kv_down[:, :KVR]
    inverse_kv = lax.rsqrt(jnp.mean(latent * latent, axis=-1, keepdims=True) + EPSILON)
    latent_n = latent * inverse_kv
    latent_b = (latent_n * gain_kv).astype(jnp.bfloat16)
    key_rope = rotate(kv_down[:, KVR:], cosine, sine_table).astype(jnp.bfloat16)
    kv_up = matmul(latent_b, kv_up_w).astype(jnp.bfloat16)
    query, kv_up, first_pieces = fence(query, kv_up, first_pieces)
    mixed_b = attend(prefix, query, key_rope, kv_up, heads, scale)
    mixed_b, shared_moved, second_pieces = fence(mixed_b, shared_moved, second_pieces)
    grad_picked = picked(my_blocks(grad_all))
    attn_sum = scatter_sum(matmul(mixed_b, w_out).astype(jnp.bfloat16))
    grad_pieces = to_lanes(grad_picked)

    attn_sum, grad_pieces = fence(attn_sum, grad_pieces)
    first_mine = jnp.concatenate(first_pieces)
    first_other = swap(first_mine)
    shared_pieces = to_lanes([shared_moved] * lanes)
    second_mine = jnp.concatenate(second_pieces)
    second_other = swap(second_mine)
    middle = tokens.astype(jnp.float32) + attn_sum.astype(jnp.float32)

    inverse_two = lax.rsqrt(jnp.mean(middle * middle, axis=-1, keepdims=True) + EPSILON)
    normed_two_b = (middle * inverse_two * gain_two).astype(jnp.bfloat16)
    x2 = gather(normed_two_b)
    x2, shared_pieces, first_other, second_other = fence(x2, shared_pieces, first_other, second_other)
    x_pieces = to_lanes(picked(my_blocks(x2)))
    shared_w = by_lane(shared_pieces).transpose(1, 0, 2, 3).reshape(share * groups, 2 * hidden_n)

    shared_a = matmul(x2, shared_w[:, :hidden_n])
    shared_b = matmul(x2, shared_w[:, hidden_n:])
    shared_sig = jax.nn.sigmoid(shared_a)
    shared_hidden = (shared_a * shared_sig * shared_b).astype(jnp.bfloat16)
    shared_up = matmul_nt(grad_all, shared_out)
    shared_ga = (shared_up * shared_b * shared_sig * (1.0 + shared_a * (1.0 - shared_sig))).astype(
        jnp.bfloat16
    )
    shared_gb = (shared_up * shared_a * shared_sig).astype(jnp.bfloat16)
    shared_g = jnp.concatenate([shared_ga, shared_gb], axis=1)
    x_pieces[:3], shared_g, shared_hidden = fence(x_pieces[:3], shared_g, shared_hidden)
    shared_part = matmul(shared_hidden, shared_out).astype(jnp.bfloat16)
    grad_shared_out = matmul_tn(shared_hidden, grad_all).astype(jnp.bfloat16)
    grad_shared_in = matmul_tn(x2, shared_g).astype(jnp.bfloat16)
    shared_back = matmul_nt(shared_g, shared_w).astype(jnp.bfloat16)
    part = share // lanes
    shared_in_lanes = grad_shared_in.reshape(groups, lanes, part, 2 * hidden_n)
    shared_out_lanes = grad_shared_out.reshape(lanes, -1, 2 * hidden_n)
    shared_sources = [
        jnp.concatenate(
            [
                lax.dynamic_index_in_dim(shared_in_lanes, my_dp ^ step, 1, keepdims=False).reshape(
                    groups * part, 2 * hidden_n
                ),
                lax.dynamic_index_in_dim(shared_out_lanes, my_dp ^ step, 0, keepdims=False),
            ]
        )
        for step in range(lanes)
    ]
    x_pieces, shared_part, shared_back, shared_sources = fence(
        x_pieces, shared_part, shared_back, shared_sources
    )

    def lane_parts(value):
        count = value.shape[0] // groups
        return lane_exchange(
            value.reshape(groups, lanes, count // lanes, value.shape[1]).transpose(1, 0, 2, 3)
        )

    def lane_rows(value):
        return lane_exchange(value.reshape(lanes, value.shape[0] // lanes, value.shape[1]))

    def lane_sum(pieces):
        return sum(piece.astype(jnp.float32) for piece in pieces).astype(jnp.bfloat16)

    flat = (chips * capacity, D)
    shared_parts = to_lanes(shared_sources)
    router_lane = kv_cols - KVR
    spot = jnp.stack([my_dp, my_core, my_expert]).astype(jnp.int32)
    step_out = expert_step(
        spot,
        [piece.reshape(flat) for piece in x_pieces],
        [piece.reshape(flat) for piece in grad_pieces],
        first_mine,
        first_other,
        second_mine,
        second_other,
        jnp.pad(router_w, ((0, 0), (0, 128 - expert_count))),
        expert_count,
    )
    step_out, shared_parts = fence(step_out, shared_parts)
    rows_grad = step_out[:lanes]
    row_hidden, grads, x_rows, grad_rows, second_w, logit_grad = step_out[lanes:]
    back_pieces = to_lanes([piece.reshape(chips, capacity, D) for piece in rows_grad])
    grad_second = matmul_tn(row_hidden, grad_rows).astype(jnp.bfloat16)
    result_b = matmul(row_hidden, second_w).astype(jnp.bfloat16)
    logit_wide = jnp.pad(
        logit_grad[:, :expert_count], ((0, 0), (router_lane, 128 - router_lane - expert_count))
    )
    grad_router = matmul_tn(x_rows, logit_wide)
    back_pieces, grad_second, grad_router, result_b = fence(back_pieces, grad_second, grad_router, result_b)
    result_sources, x_rows, grads, shared_parts = fence(split_rows(result_b), x_rows, grads, shared_parts)
    result_pieces = to_lanes(result_sources)
    shared_sum = lane_sum(shared_parts)
    grad_first_other = matmul_tn(x_rows, grads[1]).astype(jnp.bfloat16)
    grad_first_mine = matmul_tn(x_rows, grads[0]).astype(jnp.bfloat16)

    first_sent = swap(grad_first_other)
    second_hold, second_send = halves(grad_second, 0)
    second_sent = swap(second_send)
    back_part = add_mine(shared_back.astype(jnp.float32), placed(back_pieces)).astype(jnp.bfloat16)
    normed_two_grad = scatter_sum(back_part.reshape(length, D))
    normed_two_grad, first_sent, second_sent, grad_first_mine, result_pieces[:3] = fence(
        normed_two_grad, first_sent, second_sent, grad_first_mine, result_pieces[:3]
    )
    normed_two_grad = normed_two_grad.astype(jnp.float32)
    normal_two = middle * inverse_two
    grad_gain_two = jnp.sum(normed_two_grad * normal_two, axis=0)
    scaled = normed_two_grad * gain_two
    middle_grad = cotangent.astype(jnp.float32) + inverse_two * (
        scaled - normal_two * jnp.mean(scaled * normal_two, axis=-1, keepdims=True)
    )
    grad_first = (grad_first_mine.astype(jnp.float32) + first_sent.astype(jnp.float32)).astype(jnp.bfloat16)
    first_lanes = grad_first.reshape(lanes, D // lanes, half)
    first_sources = [
        lax.dynamic_index_in_dim(first_lanes, my_dp ^ step, 0, keepdims=False) for step in range(lanes)
    ]
    grad_second = (second_hold.astype(jnp.float32) + second_sent.astype(jnp.float32)).astype(jnp.bfloat16)

    middle_all = gather(middle_grad.astype(jnp.bfloat16))
    second_lanes = grad_second.reshape(half // 2, lanes, D // lanes)
    second_sources = [
        lax.dynamic_index_in_dim(second_lanes, my_dp ^ step, 1, keepdims=False) for step in range(lanes)
    ]
    first_back = to_lanes(first_sources)
    middle_all, result_pieces, second_sources, first_back[:3], shared_sum = fence(
        middle_all, result_pieces, second_sources, first_back[:3], shared_sum
    )
    shared_in_moved = exchange(shared_sum[: groups * part].reshape(groups, part, 2 * hidden_n))
    shared_out_own = shared_sum[groups * part :].reshape(part, -1)
    out_part = add_mine(shared_part.astype(jnp.float32), placed(result_pieces)).astype(jnp.bfloat16)
    attn_grad = matmul_nt(middle_all, w_out).astype(jnp.bfloat16)
    attn_grad, out_part = fence(attn_grad, out_part)
    ffn = scatter_sum(out_part.reshape(length, D))
    query_nope_grad, query_rope_grad, kv_up_grad, rope_grad = attend_back(
        prefix, query, attn_grad, key_rope, kv_up, heads, scale
    )
    grad_out_w = matmul_tn(mixed_b, middle_all).astype(jnp.bfloat16)
    out_w_parts = lane_rows(grad_out_w)

    def own_slices(pieces, axis):
        def of_core(core):
            near = my_dp // 2 == core
            pair = [jnp.where(near, pieces[i], pieces[2 + i]) for i in range(2)]
            flip = my_dp % 2 == 1
            return jnp.stack(
                [jnp.where(flip, pair[1], pair[0]), jnp.where(flip, pair[0], pair[1])]
            )

        return ordered(of_core(my_core), swap(of_core(1 - my_core)), axis).astype(jnp.float32)

    grad_kv_up = matmul_tn(latent_b, kv_up_grad).astype(jnp.bfloat16)
    latent_up = matmul_nt(kv_up_grad, kv_up_w)
    grad_kv_gain = jnp.sum(latent_up * latent_n, axis=0)
    latent_scaled = latent_up * gain_kv
    latent_grad = inverse_kv * (
        latent_scaled - latent_n * jnp.mean(latent_scaled * latent_n, axis=-1, keepdims=True)
    )
    rope_grad = rotate(rope_grad, cosine, -sine_table)
    kv_down_grad = jnp.concatenate([latent_grad, rope_grad], axis=1).astype(jnp.bfloat16)
    query_rope_grad = rotate(
        query_rope_grad.reshape(length, heads, DR), cosine[:, None, :], -sine_table[:, None, :]
    )
    query_grad = jnp.concatenate(
        [query_nope_grad, query_rope_grad.reshape(length, heads * DR).astype(jnp.bfloat16)], axis=1
    )
    normed_part = matmul_nt(query_grad, query_w) + matmul_nt(kv_down_grad, kv_down_w)
    grad_gain_one = jnp.sum(normed_part * (values_all * inverse_one), axis=0)
    early = jnp.concatenate(
        [
            shared_in_moved.reshape(groups, part, 2, hidden_n)
            .transpose(1, 2, 0, 3)
            .reshape(part, 2 * groups * hidden_n),
            shared_out_own,
        ],
        axis=1,
    )
    normed_part, ffn = fence(normed_part.astype(jnp.bfloat16), ffn)
    grad_query = matmul_tn(normed_b, query_grad).astype(jnp.bfloat16)
    attention_grad = jnp.concatenate(
        [
            grad_query.reshape(groups, share, query_n),
            grad_kv_up.reshape(groups, share, kv_width // fold),
        ],
        axis=2,
    ).reshape(groups * share, query_n + kv_width // fold)
    attention_parts_sum = lane_parts(attention_grad)

    kv_wide = jnp.pad(kv_down_grad, ((0, 0), (0, 640 - kv_cols)))
    gains_grad = jnp.concatenate(
        [
            grad_gain_one.reshape(groups, share),
            grad_gain_two.reshape(groups, share),
            grad_kv_gain.reshape(groups, kv_share),
        ],
        axis=1,
    ).reshape(groups, gain_rows, extra)
    gains_wide = jnp.pad(
        gains_grad, ((0, 0), (0, share - gain_rows), (128 - extra, 0))
    ).reshape(groups * share, 128)
    small_grad = (
        matmul_tn(normed_b, kv_wide) + jnp.pad(grad_router + gains_wide, ((0, 0), (KVR, 0)))
    ).astype(jnp.bfloat16)
    small_sum = scatter_sum(small_grad)
    normed_grad = scatter_sum(normed_part)
    normed_grad, first_back, attention_parts_sum, out_w_parts, early, second_sources = fence(
        normed_grad, first_back, attention_parts_sum, out_w_parts, early, second_sources
    )
    attention_moved = exchange(lane_sum(attention_parts_sum))
    early_pieces = to_lanes([early] * lanes)
    second_back = to_lanes(second_sources)
    small_part = lane_sum(lane_rows(small_sum))

    grad_first = own_slices(first_back, 2)
    grad_second = own_slices(second_back, 1)
    def lane_gather(value):
        return lax.all_gather(value, "dp", axis=0, tiled=True)

    early = by_lane(early_pieces).reshape(share, -1)
    cut = 2 * groups * hidden_n
    shared_in_grad = early[:, :cut].astype(jnp.float32)
    shared_out_grad = early[:, cut:].reshape(hidden_n, D).astype(jnp.float32)
    query_cols = attention_moved[..., :query_n].transpose(1, 0, 2)
    query_cols = jnp.concatenate(
        [
            query_cols[..., : heads * DN].reshape(part, groups, heads, DN),
            query_cols[..., heads * DN :].reshape(part, groups, heads, DR),
        ],
        axis=-1,
    ).reshape(part, H * (DN + DR))
    kv_cols_grad = (
        attention_moved[..., query_n:]
        .reshape(groups, part // fold, fold, kv_width // fold)
        .transpose(1, 2, 0, 3)
        .reshape(part, groups * kv_width // fold)
    )
    late = jnp.concatenate([query_cols, kv_cols_grad, lane_sum(out_w_parts), small_part], axis=1)
    late, normed_grad = fence(late, normed_grad)
    late = lane_gather(late)
    cut = H * (DN + DR)
    query_grad_out = late[:, :cut].astype(jnp.float32)
    kv_up_grad_out = (
        late[:, cut : cut + groups * kv_width // fold]
        .reshape(kv_share, fold, groups, kv_width // fold)
        .transpose(0, 2, 1, 3)
        .reshape(kv_share, H * (DN + DV))
        .astype(jnp.float32)
    )
    cut += groups * kv_width // fold
    out_w_grad = late[:, cut : cut + D].astype(jnp.float32)
    small_sum = late[:, cut + D :].astype(jnp.float32)
    gains_sum = small_sum[:gain_rows, used:].reshape(-1)

    out = (middle + ffn.astype(jnp.float32)).astype(jnp.bfloat16)
    normed_grad = normed_grad.astype(jnp.float32)
    values = tokens.astype(jnp.float32)
    inverse_own = lax.rsqrt(jnp.mean(values * values, axis=-1, keepdims=True) + EPSILON)
    normal_one = values * inverse_own
    scaled_one = normed_grad * gain_one
    grad_tokens = middle_grad + inverse_own * (
        scaled_one - normal_one * jnp.mean(scaled_one * normal_one, axis=-1, keepdims=True)
    )
    return (
        out,
        grad_tokens,
        gains_sum[:share],
        query_grad_out,
        small_sum[:, :kv_cols],
        gains_sum[2 * share :],
        kv_up_grad_out,
        out_w_grad,
        gains_sum[share : 2 * share],
        small_sum[:, kv_cols:used],
        shared_in_grad,
        shared_out_grad,
        grad_first,
        grad_second,
    )


def solution(mesh):
    groups = mesh.shape["expert"]
    lanes = mesh.shape["dp"]
    if H % groups == 0 and groups % 2 == 0 and lanes == 4:
        inner = Mesh(mesh.devices.reshape(lanes, groups // 2, 2), ("dp", "z", "core"))
        return sharded(shared_body, inner, "dp", ("z", "core"))
    return sharded(body, mesh, "dp", "expert")


def sharded(function, mesh, dp, expert):
    every = (dp, expert) if isinstance(expert, str) else (dp,) + expert
    row = P(every, None)
    vector = P(expert)
    matrix = P(expert, None)
    first = P(expert, dp, None)
    second = P(expert, None, dp)
    weights = (vector, matrix, matrix, vector, matrix, matrix, vector, matrix, matrix, matrix, first, second)
    return jax.shard_map(
        function,
        mesh=mesh,
        in_specs=(row, row, P(dp), row) + weights,
        out_specs=(row, row) + weights,
        check_vma=False,
    )
```

```python
import functools

import jax
import jax.numpy as jnp
from jax import lax
from jax.experimental import pallas as pl
from jax.experimental.pallas import tpu as pltpu
from jax.sharding import Mesh
from jax.sharding import PartitionSpec as P

D = 2048
H = 16
DN = 128
DR = 64
DV = 128
KVR = 512


EPSILON = 1e-06
MASKED = -1e30


def rms_norm(values, gain_vector):
    return (
        values
        * lax.rsqrt(jnp.mean(values * values, axis=-1, keepdims=True) + EPSILON)
        * gain_vector
    )


def tables(positions, half_width):
    frequency = 10000.0 ** (-jnp.arange(half_width, dtype=jnp.float32) / half_width)
    angles = positions.astype(jnp.float32)[:, None] * frequency[None, :]
    return (jnp.cos(angles), jnp.sin(angles))


def rotate(values, cosine, sine_table):
    half_width = values.shape[-1] // 2
    front_part = values[..., :half_width]
    back_part = values[..., half_width:]
    return jnp.concatenate(
        [
            front_part * cosine - back_part * sine_table,
            back_part * cosine + front_part * sine_table,
        ],
        axis=-1,
    )


def swiglu(joined):
    half_width = joined.shape[-1] // 2
    return jax.nn.silu(joined[..., :half_width]) * joined[..., half_width:]


def matmul(left_side, right_side):
    return jnp.dot(left_side, right_side, preferred_element_type=jnp.float32)


def matmul_tn(left_side, right_side):
    return lax.dot_general(
        left_side, right_side, (((0,), (0,)), ((), ())), preferred_element_type=jnp.float32
    )


def matmul_nt(left_side, right_side):
    return lax.dot_general(
        left_side, right_side, (((1,), (1,)), ((), ())), preferred_element_type=jnp.float32
    )


def masked_scores(
    query_nope, query_rope, key_nope, key_rope, key_start, query_pos, prefix_end, score_scale
):
    front_part = jnp.einsum(
        "qhd,khd->hqk", query_nope, key_nope, preferred_element_type=jnp.float32
    )
    back_part = jnp.einsum("qhd,kd->hqk", query_rope, key_rope, preferred_element_type=jnp.float32)
    raw_scores = (front_part + back_part) * score_scale
    key_pos = key_start + jnp.arange(key_nope.shape[0], dtype=jnp.int32)
    seen = (key_pos[None, :] <= query_pos[:, None]) | (key_pos[None, :] < prefix_end)
    return jnp.where(seen[None], raw_scores, MASKED)


def needed_block(key_start, query_pos, prefix_end):
    return (key_start <= query_pos[-1]) | (key_start < prefix_end)


def attend_stats(query_nope, query_rope, key_blocks, query_pos, prefix_end, score_scale):
    row_count = query_nope.shape[0]
    nope_blocks, value_blocks, rope_blocks, block_starts = key_blocks

    def block_step(running, block_item):
        key_nope, key_rope, key_start = block_item

        def compute_block(current):
            running_top, running_sum = current
            block_scores = masked_scores(
                query_nope,
                query_rope,
                key_nope,
                key_rope,
                key_start,
                query_pos,
                prefix_end,
                score_scale,
            )
            new_top = jnp.maximum(running_top, jnp.max(block_scores, axis=-1))
            new_sum = running_sum * jnp.exp(running_top - new_top) + jnp.sum(
                jnp.exp(block_scores - new_top[..., None]), axis=-1
            )
            return (new_top, new_sum)

        def skip_block(current):
            return current

        return (
            lax.cond(
                needed_block(key_start, query_pos, prefix_end), compute_block, skip_block, running
            ),
            None,
        )

    initial = (
        jnp.full((H, row_count), MASKED, jnp.float32),
        jnp.zeros((H, row_count), jnp.float32),
    )
    (final_top, final_sum), _ = lax.scan(
        block_step, initial, (nope_blocks, rope_blocks, block_starts)
    )
    return final_top + jnp.log(final_sum)


def attend_values(
    query_nope, query_rope, key_blocks, query_pos, prefix_end, score_scale, log_total
):
    row_count = query_nope.shape[0]

    def block_step(running, block_item):
        key_nope, key_value, key_rope, key_start = block_item

        def compute_block(current):
            block_scores = masked_scores(
                query_nope,
                query_rope,
                key_nope,
                key_rope,
                key_start,
                query_pos,
                prefix_end,
                score_scale,
            )
            weights = jnp.exp(block_scores - log_total[..., None]).astype(jnp.bfloat16)
            return current + jnp.einsum(
                "hqk,khd->qhd", weights, key_value, preferred_element_type=jnp.float32
            )

        def skip_block(current):
            return current

        return (
            lax.cond(
                needed_block(key_start, query_pos, prefix_end), compute_block, skip_block, running
            ),
            None,
        )

    initial = jnp.zeros((row_count, H, DV), jnp.float32)
    result, _ = lax.scan(block_step, initial, key_blocks)
    return result


def attend_grads(
    query_nope,
    query_rope,
    key_blocks,
    query_pos,
    prefix_end,
    score_scale,
    log_total,
    grad_out,
    row_delta,
):
    row_count = query_nope.shape[0]
    key_span = key_blocks[0].shape[1]

    def block_step(running, block_item):
        key_nope, key_value, key_rope, key_start = block_item

        def compute_block(current):
            grad_nope, grad_rope = current
            block_scores = masked_scores(
                query_nope,
                query_rope,
                key_nope,
                key_rope,
                key_start,
                query_pos,
                prefix_end,
                score_scale,
            )
            attn_probs = jnp.exp(block_scores - log_total[..., None])
            prob_grad = jnp.einsum(
                "qhd,khd->hqk", grad_out, key_value, preferred_element_type=jnp.float32
            )
            dscore = (attn_probs * (prob_grad - row_delta[..., None])).astype(jnp.bfloat16)
            grad_nope = grad_nope + score_scale * jnp.einsum(
                "hqk,khd->qhd", dscore, key_nope, preferred_element_type=jnp.float32
            )
            grad_rope = grad_rope + score_scale * jnp.einsum(
                "hqk,kd->qhd", dscore, key_rope, preferred_element_type=jnp.float32
            )
            key_grad = score_scale * jnp.einsum(
                "hqk,qhd->khd", dscore, query_nope, preferred_element_type=jnp.float32
            )
            rope_grad = score_scale * jnp.einsum(
                "hqk,qhd->kd", dscore, query_rope, preferred_element_type=jnp.float32
            )
            value_grad = jnp.einsum(
                "hqk,qhd->khd",
                attn_probs.astype(jnp.bfloat16),
                grad_out,
                preferred_element_type=jnp.float32,
            )
            return ((grad_nope, grad_rope), (key_grad, value_grad, rope_grad))

        def skip_block(current):
            empty_terms = (
                jnp.zeros((key_span, H, DN), jnp.float32),
                jnp.zeros((key_span, H, DV), jnp.float32),
                jnp.zeros((key_span, DR), jnp.float32),
            )
            return (current, empty_terms)

        return lax.cond(
            needed_block(key_start, query_pos, prefix_end), compute_block, skip_block, running
        )

    initial = (
        jnp.zeros((row_count, H, DN), jnp.float32),
        jnp.zeros((row_count, H, DR), jnp.float32),
    )
    return lax.scan(block_step, initial, key_blocks)


def split_blocks(key_parts, key_span):
    nope_all, value_all, rope_all = key_parts
    block_count = nope_all.shape[0] // key_span
    block_starts = jnp.arange(block_count, dtype=jnp.int32) * key_span
    return (
        nope_all.reshape(block_count, key_span, H, DN),
        value_all.reshape(block_count, key_span, H, DV),
        rope_all.reshape(block_count, key_span, DR),
        block_starts,
    )


def body(
    tokens,
    cotangent,
    prefix,
    routes,
    norm1_gain,
    w_query,
    w_kv_down,
    kv_gain,
    w_kv_up,
    w_out,
    norm2_gain,
    w_router,
    shared_in,
    shared_out,
    expert_in,
    expert_out,
):
    row_count = tokens.shape[0]
    topk_count = routes.shape[1]
    groups = lax.axis_size("expert")
    owned = expert_in.shape[0]
    expert_count = owned * groups
    capacity = 3 * row_count * topk_count // (2 * expert_count)
    score_scale = float(DN + DR) ** (-0.5)
    my_index = lax.axis_index("expert")
    query_pos = my_index * row_count + jnp.arange(row_count, dtype=jnp.int32)
    prefix_end = prefix[0]
    cosine, sine_table = tables(query_pos, DR // 2)
    key_span = 4 * row_count
    mixer_parts = (
        lax.all_gather(norm1_gain, "expert", axis=0, tiled=True),
        lax.all_gather(w_query, "expert", axis=0, tiled=True),
        lax.all_gather(w_kv_down, "expert", axis=0, tiled=True),
        lax.all_gather(kv_gain, "expert", axis=0, tiled=True),
        lax.all_gather(w_kv_up, "expert", axis=0, tiled=True),
        lax.all_gather(w_out, "expert", axis=0, tiled=True),
        lax.all_gather(norm2_gain, "expert", axis=0, tiled=True),
        lax.all_gather(w_router, "expert", axis=0, tiled=True),
        lax.all_gather(shared_in, "expert", axis=0, tiled=True),
        lax.all_gather(shared_out, "expert", axis=0, tiled=True),
    )
    (
        gain_one,
        query_w,
        kv_down_w,
        kv_gain_w,
        kv_up_w,
        out_w,
        gain_two,
        router_w,
        shared_in_w,
        shared_out_w,
    ) = mixer_parts
    values = tokens.astype(jnp.float32)
    normed = rms_norm(values, gain_one.astype(jnp.float32))
    normed_b = normed.astype(jnp.bfloat16)
    query_raw = matmul(normed_b, query_w).reshape(row_count, H, DN + DR)
    query_nope = query_raw[..., :DN].astype(jnp.bfloat16)
    query_rope = rotate(query_raw[..., DN:], cosine[:, None, :], sine_table[:, None, :]).astype(
        jnp.bfloat16
    )
    kv_down = matmul(normed_b, kv_down_w)
    latent = kv_down[:, :KVR]
    latent_b = rms_norm(latent, kv_gain_w.astype(jnp.float32)).astype(jnp.bfloat16)
    key_rope_b = rotate(kv_down[:, KVR:], cosine, sine_table).astype(jnp.bfloat16)
    kv_up = matmul(latent_b, kv_up_w).astype(jnp.bfloat16).reshape(row_count, H, DN + DV)
    local_nope = kv_up[..., :DN].reshape(row_count, H * DN)
    local_value = kv_up[..., DN:].reshape(row_count, H * DV)
    key_parts = (
        lax.all_gather(local_nope, "expert", axis=0, tiled=True),
        lax.all_gather(local_value, "expert", axis=0, tiled=True),
        lax.all_gather(key_rope_b, "expert", axis=0, tiled=True),
    )
    key_blocks = split_blocks(key_parts, key_span)
    log_total = attend_stats(query_nope, query_rope, key_blocks, query_pos, prefix_end, score_scale)
    attn_full = attend_values(
        query_nope, query_rope, key_blocks, query_pos, prefix_end, score_scale, log_total
    )
    mixed_b = attn_full.astype(jnp.bfloat16).reshape(row_count, H * DV)
    middle = values + matmul(mixed_b, out_w)
    gain_two_f = gain_two.astype(jnp.float32)
    normed_two_b = rms_norm(middle, gain_two_f).astype(jnp.bfloat16)
    router_probs = jax.nn.softmax(matmul(normed_two_b, router_w), axis=-1)
    one_hot = routes[:, :, None] == jnp.arange(expert_count, dtype=jnp.int32)[None, None, :]
    route_gates = jnp.sum(jnp.where(one_hot, router_probs[:, None, :], 0.0), axis=-1)
    shared_join = matmul(normed_two_b, shared_in_w)
    shared_hidden_b = swiglu(shared_join).astype(jnp.bfloat16)
    shared = matmul(shared_hidden_b, shared_out_w)
    expert_ids = routes.reshape(-1)
    id_hot = (expert_ids[:, None] == jnp.arange(expert_count, dtype=jnp.int32)[None, :]).astype(
        jnp.int32
    )
    slot_index = jnp.sum((jnp.cumsum(id_hot, axis=0) - id_hot) * id_hot, axis=1)
    slot_place = (expert_ids % owned * groups + expert_ids // owned) * capacity + slot_index
    buffer_rows = owned * groups * capacity
    filled = (
        jnp.zeros((buffer_rows, D), jnp.bfloat16)
        .at[slot_place]
        .set(jnp.repeat(normed_two_b, topk_count, axis=0))
    )
    received = lax.all_to_all(
        filled.reshape(owned, groups, capacity, D),
        "expert",
        split_axis=1,
        concat_axis=1,
        tiled=True,
    )
    expert_rows = received.reshape(owned, groups * capacity, D)
    expert_parts = (
        lax.all_gather(expert_in, "dp", axis=1, tiled=True),
        lax.all_gather(expert_out, "dp", axis=2, tiled=True),
    )
    first_w, second_w = expert_parts
    joined = jnp.einsum("erd,edf->erf", expert_rows, first_w, preferred_element_type=jnp.float32)
    hidden_b = swiglu(joined).astype(jnp.bfloat16)
    result_b = jnp.einsum(
        "erf,efd->erd", hidden_b, second_w, preferred_element_type=jnp.float32
    ).astype(jnp.bfloat16)
    returned = lax.all_to_all(
        result_b.reshape(owned, groups, capacity, D),
        "expert",
        split_axis=1,
        concat_axis=1,
        tiled=True,
    )
    picked = (
        returned.reshape(buffer_rows, D)[slot_place]
        .reshape(row_count, topk_count, D)
        .astype(jnp.float32)
    )
    routed = jnp.sum(route_gates[:, :, None] * picked, axis=1)
    out = (middle + shared + routed).astype(jnp.bfloat16)
    back_parts = (
        lax.all_gather(norm1_gain, "expert", axis=0, tiled=True),
        lax.all_gather(w_query, "expert", axis=0, tiled=True),
        lax.all_gather(w_kv_down, "expert", axis=0, tiled=True),
        lax.all_gather(kv_gain, "expert", axis=0, tiled=True),
        lax.all_gather(w_kv_up, "expert", axis=0, tiled=True),
        lax.all_gather(w_out, "expert", axis=0, tiled=True),
        lax.all_gather(norm2_gain, "expert", axis=0, tiled=True),
        lax.all_gather(w_router, "expert", axis=0, tiled=True),
        lax.all_gather(shared_in, "expert", axis=0, tiled=True),
        lax.all_gather(shared_out, "expert", axis=0, tiled=True),
    )
    back_keys = (
        lax.all_gather(local_nope, "expert", axis=0, tiled=True),
        lax.all_gather(local_value, "expert", axis=0, tiled=True),
        lax.all_gather(key_rope_b, "expert", axis=0, tiled=True),
    )
    back_blocks = split_blocks(back_keys, key_span)
    (
        gain_one_back,
        query_back,
        kv_down_back,
        kv_gain_back,
        kv_up_back,
        out_back,
        gain_two_back,
        router_back,
        shared_in_back,
        shared_out_back,
    ) = back_parts
    out_grad = cotangent.astype(jnp.float32)
    gate_grad = jnp.sum(out_grad[:, None, :] * picked, axis=2)
    result_grad = (route_gates[:, :, None] * out_grad[:, None, :]).astype(jnp.bfloat16)
    sent = jnp.zeros((buffer_rows, D), jnp.bfloat16).at[slot_place].set(result_grad.reshape(-1, D))
    owner_grad = lax.all_to_all(
        sent.reshape(owned, groups, capacity, D), "expert", split_axis=1, concat_axis=1, tiled=True
    ).reshape(owned, groups * capacity, D)
    hidden_grad = jnp.einsum(
        "erd,efd->erf", owner_grad, second_w, preferred_element_type=jnp.float32
    )
    _, pull_expert = jax.vjp(swiglu, joined)
    joined_grad = pull_expert(hidden_grad)[0].astype(jnp.bfloat16)
    grad_second = jnp.einsum(
        "erf,erd->efd", hidden_b, owner_grad, preferred_element_type=jnp.float32
    )
    grad_first = jnp.einsum(
        "erd,erf->edf", expert_rows, joined_grad, preferred_element_type=jnp.float32
    )
    rows_grad = jnp.einsum("erf,edf->erd", joined_grad, first_w, preferred_element_type=jnp.float32)
    sent_back = lax.all_to_all(
        rows_grad.reshape(owned, groups, capacity, D).astype(jnp.bfloat16),
        "expert",
        split_axis=1,
        concat_axis=1,
        tiled=True,
    ).astype(jnp.float32)
    route_grad = jnp.sum(
        sent_back.reshape(buffer_rows, D)[slot_place].reshape(row_count, topk_count, D), axis=1
    )
    expert_grads = (
        lax.psum_scatter(
            grad_first.astype(jnp.bfloat16), "dp", scatter_dimension=1, tiled=True
        ).astype(jnp.float32),
        lax.psum_scatter(
            grad_second.astype(jnp.bfloat16), "dp", scatter_dimension=2, tiled=True
        ).astype(jnp.float32),
    )
    probs_grad = jnp.sum(jnp.where(one_hot, gate_grad[:, :, None], 0.0), axis=1)
    logit_grad = (
        router_probs * (probs_grad - jnp.sum(router_probs * probs_grad, axis=-1, keepdims=True))
    ).astype(jnp.bfloat16)
    out_grad_b = out_grad.astype(jnp.bfloat16)
    shared_hidden_grad = matmul_nt(out_grad_b, shared_out_back)
    _, pull_shared = jax.vjp(swiglu, shared_join)
    shared_join_grad = pull_shared(shared_hidden_grad)[0].astype(jnp.bfloat16)
    grad_router = matmul_tn(normed_two_b, logit_grad)
    grad_shared_in = matmul_tn(normed_two_b, shared_join_grad)
    grad_shared_out = matmul_tn(shared_hidden_b, out_grad_b)
    normed_two_grad = (
        route_grad
        + matmul_nt(logit_grad, router_back)
        + matmul_nt(shared_join_grad, shared_in_back)
    )
    _, pull_norm_two = jax.vjp(rms_norm, middle, gain_two_back.astype(jnp.float32))
    middle_part, grad_gain_two = pull_norm_two(normed_two_grad)
    ffn_grads = (
        lax.psum_scatter(
            grad_gain_two.astype(jnp.bfloat16), "expert", scatter_dimension=0, tiled=True
        ).astype(jnp.float32),
        lax.psum_scatter(
            grad_router.astype(jnp.bfloat16), "expert", scatter_dimension=0, tiled=True
        ).astype(jnp.float32),
        lax.psum_scatter(
            grad_shared_in.astype(jnp.bfloat16), "expert", scatter_dimension=0, tiled=True
        ).astype(jnp.float32),
        lax.psum_scatter(
            grad_shared_out.astype(jnp.bfloat16), "expert", scatter_dimension=0, tiled=True
        ).astype(jnp.float32),
    )
    middle_grad = out_grad + middle_part
    middle_grad_b = middle_grad.astype(jnp.bfloat16)
    grad_out_w = matmul_tn(mixed_b, middle_grad_b)
    attn_grad_b = matmul_nt(middle_grad_b, out_back).reshape(row_count, H, DV).astype(jnp.bfloat16)
    row_delta = jnp.sum(attn_grad_b.astype(jnp.float32) * attn_full, axis=-1).T
    (query_nope_grad, query_rope_grad), key_terms = attend_grads(
        query_nope,
        query_rope,
        back_blocks,
        query_pos,
        prefix_end,
        score_scale,
        log_total,
        attn_grad_b,
        row_delta,
    )
    key_grad_all, value_grad_all, rope_grad_all = key_terms
    key_sums = (
        lax.psum_scatter(
            key_grad_all.reshape(-1, H * DN).astype(jnp.bfloat16),
            "expert",
            scatter_dimension=0,
            tiled=True,
        ).astype(jnp.float32),
        lax.psum_scatter(
            value_grad_all.reshape(-1, H * DV).astype(jnp.bfloat16),
            "expert",
            scatter_dimension=0,
            tiled=True,
        ).astype(jnp.float32),
        lax.psum_scatter(
            rope_grad_all.reshape(-1, DR).astype(jnp.bfloat16),
            "expert",
            scatter_dimension=0,
            tiled=True,
        ).astype(jnp.float32),
    )
    nope_sum, value_sum, rope_sum = key_sums
    kv_up_grad = (
        jnp.concatenate(
            [nope_sum.reshape(row_count, H, DN), value_sum.reshape(row_count, H, DV)], axis=-1
        )
        .reshape(row_count, H * (DN + DV))
        .astype(jnp.bfloat16)
    )
    grad_kv_up = matmul_tn(latent_b, kv_up_grad)
    latent_upstream = matmul_nt(kv_up_grad, kv_up_back)
    _, pull_latent = jax.vjp(rms_norm, latent, kv_gain_back.astype(jnp.float32))
    latent_grad, grad_kv_gain = pull_latent(latent_upstream)
    _, pull_key_rope = jax.vjp(
        lambda rope_part: rotate(rope_part, cosine, sine_table), kv_down[:, KVR:]
    )
    kv_down_grad = jnp.concatenate([latent_grad, pull_key_rope(rope_sum)[0]], axis=1).astype(
        jnp.bfloat16
    )
    grad_kv_down = matmul_tn(normed_b, kv_down_grad)
    _, pull_query_rope = jax.vjp(
        lambda rope_part: rotate(rope_part, cosine[:, None, :], sine_table[:, None, :]),
        query_raw[..., DN:],
    )
    query_grad = (
        jnp.concatenate([query_nope_grad, pull_query_rope(query_rope_grad)[0]], axis=-1)
        .reshape(row_count, H * (DN + DR))
        .astype(jnp.bfloat16)
    )
    grad_query = matmul_tn(normed_b, query_grad)
    normed_grad = matmul_nt(query_grad, query_back) + matmul_nt(kv_down_grad, kv_down_back)
    _, pull_norm_one = jax.vjp(rms_norm, values, gain_one_back.astype(jnp.float32))
    input_part, grad_gain_one = pull_norm_one(normed_grad)
    grad_tokens = middle_grad + input_part
    attn_grads = (
        lax.psum_scatter(
            grad_gain_one.astype(jnp.bfloat16), "expert", scatter_dimension=0, tiled=True
        ).astype(jnp.float32),
        lax.psum_scatter(
            grad_query.astype(jnp.bfloat16), "expert", scatter_dimension=0, tiled=True
        ).astype(jnp.float32),
        lax.psum_scatter(
            grad_kv_down.astype(jnp.bfloat16), "expert", scatter_dimension=0, tiled=True
        ).astype(jnp.float32),
        lax.psum_scatter(
            grad_kv_gain.astype(jnp.bfloat16), "expert", scatter_dimension=0, tiled=True
        ).astype(jnp.float32),
        lax.psum_scatter(
            grad_kv_up.astype(jnp.bfloat16), "expert", scatter_dimension=0, tiled=True
        ).astype(jnp.float32),
        lax.psum_scatter(
            grad_out_w.astype(jnp.bfloat16), "expert", scatter_dimension=0, tiled=True
        ).astype(jnp.float32),
    )
    summed = (
        lax.psum(attn_grads[0].astype(jnp.bfloat16), "dp").astype(jnp.float32),
        lax.psum(attn_grads[1].astype(jnp.bfloat16), "dp").astype(jnp.float32),
        lax.psum(attn_grads[2].astype(jnp.bfloat16), "dp").astype(jnp.float32),
        lax.psum(attn_grads[3].astype(jnp.bfloat16), "dp").astype(jnp.float32),
        lax.psum(attn_grads[4].astype(jnp.bfloat16), "dp").astype(jnp.float32),
        lax.psum(attn_grads[5].astype(jnp.bfloat16), "dp").astype(jnp.float32),
        lax.psum(ffn_grads[0].astype(jnp.bfloat16), "dp").astype(jnp.float32),
        lax.psum(ffn_grads[1].astype(jnp.bfloat16), "dp").astype(jnp.float32),
        lax.psum(ffn_grads[2].astype(jnp.bfloat16), "dp").astype(jnp.float32),
        lax.psum(ffn_grads[3].astype(jnp.bfloat16), "dp").astype(jnp.float32),
    )
    return (
        out,
        grad_tokens,
        summed[0],
        summed[1],
        summed[2],
        summed[3],
        summed[4],
        summed[5],
        summed[6],
        summed[7],
        summed[8],
        summed[9],
        expert_grads[0],
        expert_grads[1],
    )


def visible_scores(query, key, first_row, prefix_end, scale):
    scores = scale * lax.dot_general(
        query, key, (((1,), (1,)), ((), ())), preferred_element_type=jnp.float32
    )
    row = first_row + lax.broadcasted_iota(jnp.int32, scores.shape, 0)
    column = lax.broadcasted_iota(jnp.int32, scores.shape, 1)
    return jnp.where((column <= row) | (column < prefix_end), scores, MASKED)


def head_operands(heads, head, query, key_rope, kv_up):
    at = head * (DN + DV)
    rope = heads * DN + head * DR
    query_h = jnp.concatenate(
        [query[:, head * DN : (head + 1) * DN], query[:, rope : rope + DR]], axis=1
    )
    key_h = jnp.concatenate([kv_up[:, at : at + DN], key_rope], axis=1)
    return query_h, key_h, kv_up[:, at + DN : at + DN + DV]


def attend_kernel(heads, scale, prefix_ref, query_ref, key_rope_ref, kv_up_ref, mixed_ref):
    tile = query_ref.shape[0]
    first_row = pl.program_id(0) * tile
    query, key_rope, kv_up = query_ref[...], key_rope_ref[...], kv_up_ref[...]
    for head in range(heads):
        query_h, key_h, value_h = head_operands(heads, head, query, key_rope, kv_up)
        scores = visible_scores(query_h, key_h, first_row, prefix_ref[0], scale)
        powers = jnp.exp(scores - jnp.max(scores, axis=1, keepdims=True))
        probs = powers * (1.0 / jnp.sum(powers, axis=1, keepdims=True))
        mixed_ref[:, head * DV : (head + 1) * DV] = jnp.dot(
            probs.astype(jnp.bfloat16), value_h, preferred_element_type=jnp.float32
        ).astype(jnp.bfloat16)


def attend_back_kernel(
    heads, scale, prefix_ref, query_ref, grad_ref, key_rope_ref, kv_up_ref,
    query_nope_ref, query_rope_ref, kv_grad_ref, rope_grad_ref, key_total, value_total,
):
    step = pl.program_id(0)
    tile = query_ref.shape[0]

    @pl.when(step == 0)
    def _():
        key_total[...] = jnp.zeros_like(key_total)
        value_total[...] = jnp.zeros_like(value_total)

    query, key_rope, kv_up = query_ref[...], key_rope_ref[...], kv_up_ref[...]
    tn = (((0,), (0,)), ((), ()))
    for head in range(heads):
        query_h, key_h, value_h = head_operands(heads, head, query, key_rope, kv_up)
        grad_h = grad_ref[:, head * DV : (head + 1) * DV]
        scores = visible_scores(query_h, key_h, step * tile, prefix_ref[0], scale)
        powers = jnp.exp(scores - jnp.max(scores, axis=1, keepdims=True))
        probs = powers * (1.0 / jnp.sum(powers, axis=1, keepdims=True))
        prob_grad = lax.dot_general(
            grad_h, value_h, (((1,), (1,)), ((), ())), preferred_element_type=jnp.float32
        )
        delta = jnp.sum(probs * prob_grad, axis=1, keepdims=True)
        dscore = (probs * (prob_grad - delta)).astype(jnp.bfloat16)
        query_grad = scale * jnp.dot(dscore, key_h, preferred_element_type=jnp.float32)
        query_nope_ref[:, head * DN : (head + 1) * DN] = query_grad[:, :DN].astype(jnp.bfloat16)
        query_rope_ref[:, head * DR : (head + 1) * DR] = query_grad[:, DN:]
        key_total[head] += lax.dot_general(dscore, query_h, tn, preferred_element_type=jnp.float32)
        value_total[head] += lax.dot_general(
            probs.astype(jnp.bfloat16), grad_h, tn, preferred_element_type=jnp.float32
        )

    @pl.when(step == pl.num_programs(0) - 1)
    def _():
        rope = jnp.zeros(rope_grad_ref.shape, jnp.float32)
        for head in range(heads):
            at = head * (DN + DV)
            total = scale * key_total[head]
            kv_grad_ref[:, at : at + DN] = total[:, :DN].astype(jnp.bfloat16)
            kv_grad_ref[:, at + DN : at + DN + DV] = value_total[head].astype(jnp.bfloat16)
            rope += total[:, DN:]
        rope_grad_ref[...] = rope


def attend(prefix, query, key_rope, kv_up, heads, scale):
    length = query.shape[0]
    tile = min(256, length)
    whole = lambda value: pl.BlockSpec(value.shape, lambda i: (0, 0))
    rows = lambda width: pl.BlockSpec((tile, width), lambda i: (i, 0))
    return pl.pallas_call(
        functools.partial(attend_kernel, heads, scale),
        grid=(length // tile,),
        out_shape=jax.ShapeDtypeStruct((length, heads * DV), jnp.bfloat16),
        in_specs=[pl.BlockSpec(memory_space=pltpu.SMEM), rows(query.shape[1]), whole(key_rope), whole(kv_up)],
        out_specs=rows(heads * DV),
        compiler_params=pltpu.CompilerParams(vmem_limit_bytes=48 * 1024 * 1024),
        cost_estimate=pl.CostEstimate(
            flops=2 * heads * length * length * (DN + DR + DV),
            transcendentals=heads * length * length,
            bytes_accessed=2 * length * heads * (DN + DR + DN + DV + DV),
        ),
        name="attend",
    )(prefix, query, key_rope, kv_up)


def attend_back(prefix, query, grad, key_rope, kv_up, heads, scale):
    length = query.shape[0]
    tile = min(256, length)
    whole = lambda shape: pl.BlockSpec(shape, lambda i: (0, 0))
    rows = lambda width: pl.BlockSpec((tile, width), lambda i: (i, 0))
    return pl.pallas_call(
        functools.partial(attend_back_kernel, heads, scale),
        grid=(length // tile,),
        out_shape=[
            jax.ShapeDtypeStruct((length, heads * DN), jnp.bfloat16),
            jax.ShapeDtypeStruct((length, heads * DR), jnp.float32),
            jax.ShapeDtypeStruct(kv_up.shape, jnp.bfloat16),
            jax.ShapeDtypeStruct(key_rope.shape, jnp.float32),
        ],
        in_specs=[
            pl.BlockSpec(memory_space=pltpu.SMEM),
            rows(query.shape[1]),
            rows(grad.shape[1]),
            whole(key_rope.shape),
            whole(kv_up.shape),
        ],
        out_specs=[rows(heads * DN), rows(heads * DR), whole(kv_up.shape), whole(key_rope.shape)],
        scratch_shapes=[
            pltpu.VMEM((heads, length, DN + DR), jnp.float32),
            pltpu.VMEM((heads, length, DV), jnp.float32),
        ],
        compiler_params=pltpu.CompilerParams(vmem_limit_bytes=48 * 1024 * 1024),
        cost_estimate=pl.CostEstimate(
            flops=40 * heads * length * length * 3 * (DN + DR + DV),
            transcendentals=heads * length * length,
            bytes_accessed=2 * length * heads * 3 * (DN + DR + DN + DV + DV),
        ),
        name="attend_back",
    )(prefix, query, grad, key_rope, kv_up)


def expert_kernel(expert_count, spot, *refs):
    x_in, g_in = refs[0:4], refs[4:8]
    first_in, second_in, router = refs[8:10], refs[10:12], refs[12]
    back_out = refs[13:17]
    hidden_out, grads_out, rows_out, grad_rows_out, second_out, logit_out = refs[17:23]
    first_w, second_w, x_buf, g_buf, back_st, hidden_st, grads_st, in_sem, w_sem, out_sem, keep_sem = refs[23:]
    lane, core, expert = spot[0], spot[1], spot[2]
    lanes = len(x_in)
    rows = x_buf.shape[1]
    depth, half = first_w.shape[1], first_w.shape[2]
    slab = depth // lanes
    side = half // 2

    loads = []
    for step in range(lanes):
        loads.append(
            (
                pltpu.make_async_copy(x_in[step], x_buf.at[step], in_sem.at[0, step]),
                pltpu.make_async_copy(g_in[step], g_buf.at[step], in_sem.at[1, step]),
            )
        )
    first_loads, second_loads = [], []
    for part in range(2):
        slot = core if part == 0 else 1 - core
        for step in range(lanes):
            at = pl.multiple_of((lane ^ step) * slab, slab)
            first_loads.append(
                pltpu.make_async_copy(
                    first_in[part].at[pl.ds(step * slab, slab), :], first_w.at[slot, pl.ds(at, slab), :], w_sem.at[0, part, step]
                )
            )
            second_loads.append(
                pltpu.make_async_copy(
                    second_in[part].at[pl.ds(step * side, side), :],
                    second_w.at[pl.ds(pl.multiple_of(slot * side, side), side), pl.ds(at, slab)],
                    w_sem.at[1, part, step],
                )
            )
    loads[0][0].start()
    for copy in first_loads:
        copy.start()
    loads[0][1].start()
    for copy in second_loads:
        copy.start()
    for step in range(1, lanes):
        loads[step][0].start()
        loads[step][1].start()

    def kept(step):
        where = pl.ds(step * rows, rows)
        return [
            pltpu.make_async_copy(x_buf.at[step], rows_out.at[where, :], keep_sem.at[step]),
            pltpu.make_async_copy(g_buf.at[step], grad_rows_out.at[where, :], keep_sem.at[lanes + step]),
        ]

    second_kept = pltpu.make_async_copy(second_w, second_out, keep_sem.at[2 * lanes])

    def stores(step, slot, back):
        where = pl.ds(pl.multiple_of(step * rows, rows), rows)
        return [
            pltpu.make_async_copy(back_st.at[slot], back, out_sem.at[slot, 0]),
            pltpu.make_async_copy(hidden_st.at[slot], hidden_out.at[where, :], out_sem.at[slot, 1]),
            pltpu.make_async_copy(grads_st.at[slot, 0], grads_out.at[0, where, :], out_sem.at[slot, 2]),
            pltpu.make_async_copy(grads_st.at[slot, 1], grads_out.at[1, where, :], out_sem.at[slot, 3]),
        ]

    nt = (((1,), (1,)), ((), ()))

    def compute(step, slot):
        x = x_buf[step]
        a = jnp.dot(x, first_w[0], preferred_element_type=jnp.float32)
        b = jnp.dot(x, first_w[1], preferred_element_type=jnp.float32)
        logits = jnp.dot(x, router[...], preferred_element_type=jnp.float32)
        column = lax.broadcasted_iota(jnp.int32, logits.shape, 1)
        logits = jnp.where(column < expert_count, logits, -1e30)
        top = jnp.max(logits, axis=1, keepdims=True)
        powers = jnp.exp(logits - top)
        probs = powers / jnp.sum(powers, axis=1, keepdims=True)
        hot = (column == expert).astype(jnp.float32)
        gate = jnp.sum(probs * hot, axis=1, keepdims=True)
        g = g_buf[step]
        up = lax.dot_general(g, second_w[...], nt, preferred_element_type=jnp.float32)
        sig = 1.0 / (1.0 + jnp.exp(-a))
        act = a * sig
        hidden = act * b
        hidden_st[slot] = (gate * hidden).astype(jnp.bfloat16)
        gate_grad = jnp.sum(up * hidden, axis=1, keepdims=True)
        up = up * gate
        grad_b = (up * act).astype(jnp.bfloat16)
        grad_a = (up * b * (sig + act * (1.0 - sig))).astype(jnp.bfloat16)
        grads_st[slot, core] = grad_a
        grads_st[slot, 1 - core] = grad_b
        logit = (gate * gate_grad * (hot - probs)).astype(jnp.bfloat16)
        logit_out[pl.ds(pl.multiple_of(step * rows, rows), rows), :] = logit
        back = lax.dot_general(grad_a, first_w[0], nt, preferred_element_type=jnp.float32)
        back += lax.dot_general(grad_b, first_w[1], nt, preferred_element_type=jnp.float32)
        back += lax.dot_general(logit, router[...], nt, preferred_element_type=jnp.float32)
        back_st[slot] = back.astype(jnp.bfloat16)

    for copy in first_loads + second_loads:
        copy.wait()
    second_kept.start()

    def body_step(step, carry):
        slot = lax.rem(step, 2)
        for i in range(lanes):

            @pl.when(step == i)
            def _():
                loads[i][0].wait()
                loads[i][1].wait()
                for copy in kept(i):
                    copy.start()

        for i in range(2, lanes):

            @pl.when(step == i)
            def _():
                for copy in stores(i - 2, i % 2, back_out[i - 2]):
                    copy.wait()

        compute(step, slot)
        for i in range(lanes):

            @pl.when(step == i)
            def _():
                for copy in stores(i, i % 2, back_out[i]):
                    copy.start()

        return carry

    lax.fori_loop(0, lanes, body_step, 0)
    for step in range(lanes - 2, lanes):
        for copy in stores(step, step % 2, back_out[step]):
            copy.wait()
    for step in range(lanes):
        for copy in kept(step):
            copy.wait()
    second_kept.wait()


def expert_step(spot, x_pieces, g_pieces, first_mine, first_other, second_mine, second_other, router_wide, expert_count):
    rows, depth = x_pieces[0].shape
    half = first_mine.shape[1]
    lanes = len(x_pieces)
    total = rows * lanes
    bf = jnp.bfloat16
    any_spec = pl.BlockSpec(memory_space=pl.ANY)
    vmem_spec = pl.BlockSpec(memory_space=pltpu.VMEM)
    return pl.pallas_call(
        functools.partial(expert_kernel, expert_count),
        out_shape=[jax.ShapeDtypeStruct((rows, depth), bf)] * lanes
        + [
            jax.ShapeDtypeStruct((total, half), bf),
            jax.ShapeDtypeStruct((2, total, half), bf),
            jax.ShapeDtypeStruct((total, depth), bf),
            jax.ShapeDtypeStruct((total, depth), bf),
            jax.ShapeDtypeStruct((half, depth), bf),
            jax.ShapeDtypeStruct((total, 128), bf),
        ],
        in_specs=[pl.BlockSpec(memory_space=pltpu.SMEM)] + [any_spec] * (2 * lanes + 4) + [vmem_spec],
        out_specs=[any_spec] * (lanes + 5) + [vmem_spec],
        scratch_shapes=[
            pltpu.VMEM((2, depth, half), bf),
            pltpu.VMEM((half, depth), bf),
            pltpu.VMEM((lanes, rows, depth), bf),
            pltpu.VMEM((lanes, rows, depth), bf),
            pltpu.VMEM((2, rows, depth), bf),
            pltpu.VMEM((2, rows, half), bf),
            pltpu.VMEM((2, 2, rows, half), bf),
            pltpu.SemaphoreType.DMA((2, lanes)),
            pltpu.SemaphoreType.DMA((2, 2, lanes)),
            pltpu.SemaphoreType.DMA((2, 4)),
            pltpu.SemaphoreType.DMA((2 * lanes + 1,)),
        ],
        compiler_params=pltpu.CompilerParams(vmem_limit_bytes=60 * 1024 * 1024),
        cost_estimate=pl.CostEstimate(
            flops=10 * total * depth * half,
            transcendentals=total * half,
            bytes_accessed=2 * (3 * depth * half * 2 + total * (5 * depth + 3 * half)),
        ),
        name="expert_rows",
    )(spot, *x_pieces, *g_pieces, first_mine, first_other, second_mine, second_other, router_wide)


def shared_body(
    tokens,
    cotangent,
    prefix,
    routes,
    norm1_gain,
    w_query,
    w_kv_down,
    kv_gain,
    w_kv_up,
    w_out,
    norm2_gain,
    w_router,
    shared_in,
    shared_out,
    expert_in,
    expert_out,
):
    rows = tokens.shape[0]
    topk = routes.shape[1]
    chips = lax.axis_size("z")
    lanes = lax.axis_size("dp")
    groups = chips * 2
    owned = expert_in.shape[0]
    expert_count = owned * groups
    capacity = 3 * rows * topk // (2 * expert_count)
    heads = H // groups
    length = rows * groups
    scale = float(DN + DR) ** (-0.5)
    my_dp = lax.axis_index("dp")
    my_z = lax.axis_index("z")
    my_core = lax.axis_index("core")
    my_expert = my_z * 2 * owned + my_dp
    group = ("z", "core")
    hidden_n = shared_out.shape[0]
    kv_cols = w_kv_down.shape[1]
    half = expert_in.shape[2] // 2

    def gather(value):
        return lax.all_gather(value, group, axis=0, tiled=True)

    def scatter_sum(value):
        return lax.psum_scatter(value, group, scatter_dimension=0, tiled=True)

    def fence(*values):
        return lax.optimization_barrier(values)

    def swap(value):
        return lax.ppermute(value, "core", [(0, 1), (1, 0)])

    def ordered(mine, other, axis):
        return jnp.where(
            my_core == 0,
            jnp.concatenate([mine, other], axis=axis),
            jnp.concatenate([other, mine], axis=axis),
        )

    def halves(value, axis):
        size = value.shape[axis] // 2
        mine = lax.dynamic_slice_in_dim(value, my_core * size, size, axis)
        other = lax.dynamic_slice_in_dim(value, (1 - my_core) * size, size, axis)
        return mine, other

    def exchange(value):
        return lax.all_to_all(value, group, split_axis=0, concat_axis=0, tiled=True)

    def to_lane(value, step):
        return lax.ppermute(value, "dp", [(lane, lane ^ step) for lane in range(lanes)])

    def by_lane(pieces):
        full = jnp.zeros((lanes,) + pieces[0].shape, pieces[0].dtype)
        for step in range(lanes):
            full = lax.dynamic_update_index_in_dim(full, pieces[step], my_dp ^ step, 0)
        return full

    def to_lanes(pieces):
        return [pieces[0]] + [to_lane(pieces[step], step) for step in range(1, lanes)]

    def lane_exchange(value):
        return to_lanes(
            [lax.dynamic_index_in_dim(value, my_dp ^ step, 0, keepdims=False) for step in range(lanes)]
        )

    def own_part(value):
        part = value.shape[0] // lanes
        return lax.dynamic_slice_in_dim(value, my_dp * part, part, 0).transpose(1, 0, 2)

    share = norm1_gain.shape[0]
    kv_share = kv_gain.shape[0]
    used = kv_cols + expert_count
    extra = 640 - used
    gains = jnp.concatenate([norm1_gain, norm2_gain, kv_gain])
    gain_rows = gains.shape[0] // extra
    small = jnp.concatenate(
        [
            w_kv_down,
            w_router,
            jnp.concatenate(
                [
                    jnp.pad(gains.reshape(gain_rows, extra), ((0, share - rows - gain_rows), (0, 0))),
                    jnp.pad(routes.astype(jnp.bfloat16), ((0, 0), (0, extra - topk))),
                ]
            ),
        ],
        axis=1,
    )
    query_n = heads * (DN + DR)
    kv_width = heads * (DN + DV)
    fold = share // kv_share
    query_parts = w_query.reshape(share, groups, heads, DN + DR)
    attention_parts = jnp.concatenate(
        [
            query_parts[..., :DN].reshape(share, groups, heads * DN),
            query_parts[..., DN:].reshape(share, groups, heads * DR),
            w_kv_up.reshape(kv_share, groups, fold, kv_width // fold)
            .transpose(0, 2, 1, 3)
            .reshape(share, groups, kv_width // fold),
        ],
        axis=2,
    )
    shared_parts = own_part(
        shared_in.reshape(share, 2, groups, hidden_n)
        .transpose(0, 2, 1, 3)
        .reshape(share, groups, 2 * hidden_n)
    )
    tokens_all = gather(tokens)
    small_all = gather(small)
    attention_moved = exchange(own_part(attention_parts))
    attention_pieces = to_lanes([attention_moved] * lanes)
    def lane_pieces(value, axis):
        keep, give = halves(value, axis)
        received = swap(give)
        pieces = []
        for step in range(lanes):
            lane = my_dp ^ step
            pieces.append(
                jnp.where(
                    lane // 2 == my_core,
                    lax.dynamic_index_in_dim(keep, lane % 2, 0, keepdims=False),
                    lax.dynamic_index_in_dim(received, lane % 2, 0, keepdims=False),
                )
            )
        return pieces

    first_pieces = to_lanes(lane_pieces(expert_in, 2))
    second_sources = lane_pieces(expert_out, 1)

    tokens_all, small_all, attention_pieces, first_pieces[:2], second_sources, shared_parts = fence(
        tokens_all, small_all, attention_pieces, first_pieces[:2], second_sources, shared_parts
    )
    shared_moved = exchange(shared_parts)
    grad_all = gather(cotangent)
    second_pieces = to_lanes(second_sources)
    spare = small_all[:, used:].reshape(chips, 2, share, extra)
    routes_mine = lax.dynamic_index_in_dim(
        spare[:, :, share - rows :, :topk], my_core, axis=1, keepdims=False
    ).astype(jnp.int32)

    router_w = small_all[:, kv_cols:used]
    gains_all = (
        spare.reshape(groups, share, extra)[:, :gain_rows].reshape(groups, gain_rows * extra)
    ).astype(jnp.float32)
    gain_one = gains_all[:, :share].reshape(-1)
    gain_two = gains_all[:, share : 2 * share].reshape(-1)
    gain_kv = gains_all[:, 2 * share :].reshape(-1)
    kv_down_w = small_all[:, :kv_cols]
    attention_w = by_lane(attention_pieces).transpose(1, 0, 2, 3)
    query_w = attention_w[..., :query_n].reshape(share * groups, query_n)
    kv_up_w = attention_w[..., query_n:].reshape(kv_share * groups, kv_width)

    plane = my_z * 2 * owned + (my_dp ^ jnp.arange(lanes, dtype=jnp.int32))
    member = jnp.any(routes_mine[:, :, :, None] == plane[None, None, None, :], axis=2)
    earlier = (jnp.arange(rows)[:, None] > jnp.arange(rows)[None, :]).astype(jnp.float32)
    place = jnp.einsum(
        "st,ztq->zqs", earlier, member.astype(jnp.float32), precision=lax.Precision.HIGHEST
    )
    slots = jnp.arange(capacity, dtype=jnp.float32)
    pick = (
        (place[:, :, None, :] == slots[None, None, :, None]) & member.transpose(0, 2, 1)[:, :, None, :]
    ).astype(jnp.bfloat16)

    def picked(blocks):
        return [
            jnp.einsum(
                "zst,ztd->zsd", pick[:, step], blocks, preferred_element_type=jnp.float32
            ).astype(jnp.bfloat16)
            for step in range(lanes)
        ]

    def split_rows(value):
        pieces = value.reshape(lanes, chips, capacity, D)
        return [pieces[step] for step in range(lanes)]

    def placed(pieces):
        return jnp.einsum(
            "zlst,zlsd->ztd", pick, jnp.stack(pieces, axis=1), preferred_element_type=jnp.float32
        )

    def my_blocks(value):
        return lax.dynamic_index_in_dim(
            value.reshape(chips, 2, rows, D), my_core, axis=1, keepdims=False
        )

    def add_mine(total, mine):
        spread = jnp.where((jnp.arange(2) == my_core)[None, :, None, None], mine[:, None], 0.0)
        return total.reshape(chips, 2, rows, D) + spread

    positions = jnp.arange(length, dtype=jnp.int32)
    cosine, sine_table = tables(positions, DR // 2)
    values_all = tokens_all.astype(jnp.float32)
    inverse_one = lax.rsqrt(jnp.mean(values_all * values_all, axis=-1, keepdims=True) + EPSILON)
    normed_b = (values_all * inverse_one * gain_one).astype(jnp.bfloat16)
    query_raw = matmul(normed_b, query_w)
    query_rope = rotate(
        query_raw[:, heads * DN :].reshape(length, heads, DR), cosine[:, None, :], sine_table[:, None, :]
    )
    query = jnp.concatenate(
        [query_raw[:, : heads * DN], query_rope.reshape(length, heads * DR)], axis=1
    ).astype(jnp.bfloat16)
    kv_down = matmul(normed_b, kv_down_w)
    latent = kv_down[:, :KVR]
    inverse_kv = lax.rsqrt(jnp.mean(latent * latent, axis=-1, keepdims=True) + EPSILON)
    latent_n = latent * inverse_kv
    latent_b = (latent_n * gain_kv).astype(jnp.bfloat16)
    key_rope = rotate(kv_down[:, KVR:], cosine, sine_table).astype(jnp.bfloat16)
    kv_up = matmul(latent_b, kv_up_w).astype(jnp.bfloat16)
    query, kv_up, first_pieces = fence(query, kv_up, first_pieces)
    mixed_b = attend(prefix, query, key_rope, kv_up, heads, scale)
    mixed_b, shared_moved, second_pieces = fence(mixed_b, shared_moved, second_pieces)
    grad_picked = picked(my_blocks(grad_all))
    attn_sum = scatter_sum(matmul(mixed_b, w_out).astype(jnp.bfloat16))
    grad_pieces = to_lanes(grad_picked)

    attn_sum, grad_pieces = fence(attn_sum, grad_pieces)
    first_mine = jnp.concatenate(first_pieces)
    first_other = swap(first_mine)
    shared_pieces = to_lanes([shared_moved] * lanes)
    second_mine = jnp.concatenate(second_pieces)
    second_other = swap(second_mine)
    middle = tokens.astype(jnp.float32) + attn_sum.astype(jnp.float32)

    inverse_two = lax.rsqrt(jnp.mean(middle * middle, axis=-1, keepdims=True) + EPSILON)
    normed_two_b = (middle * inverse_two * gain_two).astype(jnp.bfloat16)
    x2 = gather(normed_two_b)
    x2, shared_pieces, first_other, second_other = fence(x2, shared_pieces, first_other, second_other)
    x_pieces = to_lanes(picked(my_blocks(x2)))
    shared_w = by_lane(shared_pieces).transpose(1, 0, 2, 3).reshape(share * groups, 2 * hidden_n)

    shared_a = matmul(x2, shared_w[:, :hidden_n])
    shared_b = matmul(x2, shared_w[:, hidden_n:])
    shared_sig = jax.nn.sigmoid(shared_a)
    shared_hidden = (shared_a * shared_sig * shared_b).astype(jnp.bfloat16)
    shared_up = matmul_nt(grad_all, shared_out)
    shared_ga = (shared_up * shared_b * shared_sig * (1.0 + shared_a * (1.0 - shared_sig))).astype(
        jnp.bfloat16
    )
    shared_gb = (shared_up * shared_a * shared_sig).astype(jnp.bfloat16)
    shared_g = jnp.concatenate([shared_ga, shared_gb], axis=1)
    x_pieces[:3], shared_g, shared_hidden = fence(x_pieces[:3], shared_g, shared_hidden)
    shared_part = matmul(shared_hidden, shared_out).astype(jnp.bfloat16)
    grad_shared_out = matmul_tn(shared_hidden, grad_all).astype(jnp.bfloat16)
    grad_shared_in = matmul_tn(x2, shared_g).astype(jnp.bfloat16)
    shared_back = matmul_nt(shared_g, shared_w).astype(jnp.bfloat16)
    part = share // lanes
    shared_in_lanes = grad_shared_in.reshape(groups, lanes, part, 2 * hidden_n)
    shared_out_lanes = grad_shared_out.reshape(lanes, -1, 2 * hidden_n)
    shared_sources = [
        jnp.concatenate(
            [
                lax.dynamic_index_in_dim(shared_in_lanes, my_dp ^ step, 1, keepdims=False).reshape(
                    groups * part, 2 * hidden_n
                ),
                lax.dynamic_index_in_dim(shared_out_lanes, my_dp ^ step, 0, keepdims=False),
            ]
        )
        for step in range(lanes)
    ]
    x_pieces, shared_part, shared_back, shared_sources = fence(
        x_pieces, shared_part, shared_back, shared_sources
    )

    def lane_parts(value):
        count = value.shape[0] // groups
        return lane_exchange(
            value.reshape(groups, lanes, count // lanes, value.shape[1]).transpose(1, 0, 2, 3)
        )

    def lane_rows(value):
        return lane_exchange(value.reshape(lanes, value.shape[0] // lanes, value.shape[1]))

    def lane_sum(pieces):
        return sum(piece.astype(jnp.float32) for piece in pieces).astype(jnp.bfloat16)

    flat = (chips * capacity, D)
    shared_parts = to_lanes(shared_sources)
    router_lane = kv_cols - KVR
    spot = jnp.stack([my_dp, my_core, my_expert]).astype(jnp.int32)
    step_out = expert_step(
        spot,
        [piece.reshape(flat) for piece in x_pieces],
        [piece.reshape(flat) for piece in grad_pieces],
        first_mine,
        first_other,
        second_mine,
        second_other,
        jnp.pad(router_w, ((0, 0), (0, 128 - expert_count))),
        expert_count,
    )
    step_out, shared_parts = fence(step_out, shared_parts)
    rows_grad = step_out[:lanes]
    row_hidden, grads, x_rows, grad_rows, second_w, logit_grad = step_out[lanes:]
    back_pieces = to_lanes([piece.reshape(chips, capacity, D) for piece in rows_grad])
    grad_second = matmul_tn(row_hidden, grad_rows).astype(jnp.bfloat16)
    result_b = matmul(row_hidden, second_w).astype(jnp.bfloat16)
    logit_wide = jnp.pad(
        logit_grad[:, :expert_count], ((0, 0), (router_lane, 128 - router_lane - expert_count))
    )
    grad_router = matmul_tn(x_rows, logit_wide)
    back_pieces, grad_second, grad_router, result_b = fence(back_pieces, grad_second, grad_router, result_b)
    result_sources, x_rows, grads, shared_parts = fence(split_rows(result_b), x_rows, grads, shared_parts)
    result_pieces = to_lanes(result_sources)
    shared_sum = lane_sum(shared_parts)
    grad_first_other = matmul_tn(x_rows, grads[1]).astype(jnp.bfloat16)
    grad_first_mine = matmul_tn(x_rows, grads[0]).astype(jnp.bfloat16)

    first_sent = swap(grad_first_other)
    second_hold, second_send = halves(grad_second, 0)
    second_sent = swap(second_send)
    back_part = add_mine(shared_back.astype(jnp.float32), placed(back_pieces)).astype(jnp.bfloat16)
    normed_two_grad = scatter_sum(back_part.reshape(length, D))
    normed_two_grad, first_sent, second_sent, grad_first_mine, result_pieces[:3] = fence(
        normed_two_grad, first_sent, second_sent, grad_first_mine, result_pieces[:3]
    )
    normed_two_grad = normed_two_grad.astype(jnp.float32)
    normal_two = middle * inverse_two
    grad_gain_two = jnp.sum(normed_two_grad * normal_two, axis=0)
    scaled = normed_two_grad * gain_two
    middle_grad = cotangent.astype(jnp.float32) + inverse_two * (
        scaled - normal_two * jnp.mean(scaled * normal_two, axis=-1, keepdims=True)
    )
    grad_first = (grad_first_mine.astype(jnp.float32) + first_sent.astype(jnp.float32)).astype(jnp.bfloat16)
    first_lanes = grad_first.reshape(lanes, D // lanes, half)
    first_sources = [
        lax.dynamic_index_in_dim(first_lanes, my_dp ^ step, 0, keepdims=False) for step in range(lanes)
    ]
    grad_second = (second_hold.astype(jnp.float32) + second_sent.astype(jnp.float32)).astype(jnp.bfloat16)

    middle_all = gather(middle_grad.astype(jnp.bfloat16))
    second_lanes = grad_second.reshape(half // 2, lanes, D // lanes)
    second_sources = [
        lax.dynamic_index_in_dim(second_lanes, my_dp ^ step, 1, keepdims=False) for step in range(lanes)
    ]
    first_back = to_lanes(first_sources)
    middle_all, result_pieces, second_sources, first_back[:3], shared_sum = fence(
        middle_all, result_pieces, second_sources, first_back[:3], shared_sum
    )
    shared_in_moved = exchange(shared_sum[: groups * part].reshape(groups, part, 2 * hidden_n))
    shared_out_own = shared_sum[groups * part :].reshape(part, -1)
    out_part = add_mine(shared_part.astype(jnp.float32), placed(result_pieces)).astype(jnp.bfloat16)
    attn_grad = matmul_nt(middle_all, w_out).astype(jnp.bfloat16)
    attn_grad, out_part = fence(attn_grad, out_part)
    ffn = scatter_sum(out_part.reshape(length, D))
    query_nope_grad, query_rope_grad, kv_up_grad, rope_grad = attend_back(
        prefix, query, attn_grad, key_rope, kv_up, heads, scale
    )
    grad_out_w = matmul_tn(mixed_b, middle_all).astype(jnp.bfloat16)
    out_w_parts = lane_rows(grad_out_w)

    def own_slices(pieces, axis):
        def of_core(core):
            near = my_dp // 2 == core
            pair = [jnp.where(near, pieces[i], pieces[2 + i]) for i in range(2)]
            flip = my_dp % 2 == 1
            return jnp.stack(
                [jnp.where(flip, pair[1], pair[0]), jnp.where(flip, pair[0], pair[1])]
            )

        return ordered(of_core(my_core), swap(of_core(1 - my_core)), axis).astype(jnp.float32)

    grad_kv_up = matmul_tn(latent_b, kv_up_grad).astype(jnp.bfloat16)
    latent_up = matmul_nt(kv_up_grad, kv_up_w)
    grad_kv_gain = jnp.sum(latent_up * latent_n, axis=0)
    latent_scaled = latent_up * gain_kv
    latent_grad = inverse_kv * (
        latent_scaled - latent_n * jnp.mean(latent_scaled * latent_n, axis=-1, keepdims=True)
    )
    rope_grad = rotate(rope_grad, cosine, -sine_table)
    kv_down_grad = jnp.concatenate([latent_grad, rope_grad], axis=1).astype(jnp.bfloat16)
    query_rope_grad = rotate(
        query_rope_grad.reshape(length, heads, DR), cosine[:, None, :], -sine_table[:, None, :]
    )
    query_grad = jnp.concatenate(
        [query_nope_grad, query_rope_grad.reshape(length, heads * DR).astype(jnp.bfloat16)], axis=1
    )
    normed_part = matmul_nt(query_grad, query_w) + matmul_nt(kv_down_grad, kv_down_w)
    grad_gain_one = jnp.sum(normed_part * (values_all * inverse_one), axis=0)
    early = jnp.concatenate(
        [
            shared_in_moved.reshape(groups, part, 2, hidden_n)
            .transpose(1, 2, 0, 3)
            .reshape(part, 2 * groups * hidden_n),
            shared_out_own,
        ],
        axis=1,
    )
    normed_part, ffn = fence(normed_part.astype(jnp.bfloat16), ffn)
    grad_query = matmul_tn(normed_b, query_grad).astype(jnp.bfloat16)
    attention_grad = jnp.concatenate(
        [
            grad_query.reshape(groups, share, query_n),
            grad_kv_up.reshape(groups, share, kv_width // fold),
        ],
        axis=2,
    ).reshape(groups * share, query_n + kv_width // fold)
    attention_parts_sum = lane_parts(attention_grad)

    kv_wide = jnp.pad(kv_down_grad, ((0, 0), (0, 640 - kv_cols)))
    gains_grad = jnp.concatenate(
        [
            grad_gain_one.reshape(groups, share),
            grad_gain_two.reshape(groups, share),
            grad_kv_gain.reshape(groups, kv_share),
        ],
        axis=1,
    ).reshape(groups, gain_rows, extra)
    gains_wide = jnp.pad(
        gains_grad, ((0, 0), (0, share - gain_rows), (128 - extra, 0))
    ).reshape(groups * share, 128)
    small_grad = (
        matmul_tn(normed_b, kv_wide) + jnp.pad(grad_router + gains_wide, ((0, 0), (KVR, 0)))
    ).astype(jnp.bfloat16)
    small_sum = scatter_sum(small_grad)
    normed_grad = scatter_sum(normed_part)
    normed_grad, first_back, attention_parts_sum, out_w_parts, early, second_sources = fence(
        normed_grad, first_back, attention_parts_sum, out_w_parts, early, second_sources
    )
    attention_moved = exchange(lane_sum(attention_parts_sum))
    early = lax.all_gather(early, "dp", axis=0, tiled=True)
    second_back = to_lanes(second_sources)
    small_part = lane_sum(lane_rows(small_sum))

    grad_first = own_slices(first_back, 2)
    grad_second = own_slices(second_back, 1)
    def lane_gather(value):
        return lax.all_gather(value, "dp", axis=0, tiled=True)

    query_cols = attention_moved[..., :query_n].transpose(1, 0, 2)
    query_cols = jnp.concatenate(
        [
            query_cols[..., : heads * DN].reshape(part, groups, heads, DN),
            query_cols[..., heads * DN :].reshape(part, groups, heads, DR),
        ],
        axis=-1,
    ).reshape(part, H * (DN + DR))
    kv_cols_grad = (
        attention_moved[..., query_n:]
        .reshape(groups, part // fold, fold, kv_width // fold)
        .transpose(1, 2, 0, 3)
        .reshape(part, groups * kv_width // fold)
    )
    late = jnp.concatenate([query_cols, kv_cols_grad, lane_sum(out_w_parts), small_part], axis=1)
    late, normed_grad, early = fence(late, normed_grad, early)
    late = lane_gather(late)
    cut = 2 * groups * hidden_n
    shared_in_grad = early[:, :cut].astype(jnp.float32)
    shared_out_grad = early[:, cut:].reshape(hidden_n, D).astype(jnp.float32)
    cut = H * (DN + DR)
    query_grad_out = late[:, :cut].astype(jnp.float32)
    kv_up_grad_out = (
        late[:, cut : cut + groups * kv_width // fold]
        .reshape(kv_share, fold, groups, kv_width // fold)
        .transpose(0, 2, 1, 3)
        .reshape(kv_share, H * (DN + DV))
        .astype(jnp.float32)
    )
    cut += groups * kv_width // fold
    out_w_grad = late[:, cut : cut + D].astype(jnp.float32)
    small_sum = late[:, cut + D :].astype(jnp.float32)
    gains_sum = small_sum[:gain_rows, used:].reshape(-1)

    out = (middle + ffn.astype(jnp.float32)).astype(jnp.bfloat16)
    normed_grad = normed_grad.astype(jnp.float32)
    values = tokens.astype(jnp.float32)
    inverse_own = lax.rsqrt(jnp.mean(values * values, axis=-1, keepdims=True) + EPSILON)
    normal_one = values * inverse_own
    scaled_one = normed_grad * gain_one
    grad_tokens = middle_grad + inverse_own * (
        scaled_one - normal_one * jnp.mean(scaled_one * normal_one, axis=-1, keepdims=True)
    )
    return (
        out,
        grad_tokens,
        gains_sum[:share],
        query_grad_out,
        small_sum[:, :kv_cols],
        gains_sum[2 * share :],
        kv_up_grad_out,
        out_w_grad,
        gains_sum[share : 2 * share],
        small_sum[:, kv_cols:used],
        shared_in_grad,
        shared_out_grad,
        grad_first,
        grad_second,
    )


def solution(mesh):
    groups = mesh.shape["expert"]
    lanes = mesh.shape["dp"]
    if H % groups == 0 and groups % 2 == 0 and lanes == 4:
        inner = Mesh(mesh.devices.reshape(lanes, groups // 2, 2), ("dp", "z", "core"))
        return sharded(shared_body, inner, "dp", ("z", "core"))
    return sharded(body, mesh, "dp", "expert")


def sharded(function, mesh, dp, expert):
    every = (dp, expert) if isinstance(expert, str) else (dp,) + expert
    row = P(every, None)
    vector = P(expert)
    matrix = P(expert, None)
    first = P(expert, dp, None)
    second = P(expert, None, dp)
    weights = (vector, matrix, matrix, vector, matrix, matrix, vector, matrix, matrix, matrix, first, second)
    return jax.shard_map(
        function,
        mesh=mesh,
        in_specs=(row, row, P(dp), row) + weights,
        out_specs=(row, row) + weights,
        check_vma=False,
    )
```
